32 devices in a mesh: dp: 8 (over z, x), mp: 4 (over y, core).
Axes of the slice: x: 2, y: 2, z: 4, core: 2. Of those that a mesh axis runs over, the one named last changes fastest.
Arguments:
- images: bfloat16 [128, 52, 768], P('dp'), may hold values from -6 to 6
- ln1_gain: bfloat16 [768], replicated, may hold values from 0.5 to 1.5
- ln1_bias: bfloat16 [768], replicated, may hold values from -1 to 1
- w_qkv: bfloat16 [768, 3, 768], P(None, None, 'mp'), may hold values from -0.21875 to 0.21875
- qv_bias: bfloat16 [2, 768], P(None, 'mp'), may hold values from -1 to 1
- w_out: bfloat16 [768, 768], P('mp'), may hold values from -0.625 to 0.625
- out_bias: bfloat16 [768], replicated, may hold values from -1 to 1
- ln2_gain: bfloat16 [768], replicated, may hold values from 0.5 to 1.5
- ln2_bias: bfloat16 [768], replicated, may hold values from -1 to 1
- w_fc1: bfloat16 [768, 3072], P(None, 'mp'), may hold values from -0.21875 to 0.21875
- fc1_bias: bfloat16 [3072], P('mp'), may hold values from -1.5 to 1.5
- w_fc2: bfloat16 [3072, 768], P('mp'), may hold values from -0.15625 to 0.15625
- fc2_bias: bfloat16 [768], replicated, may hold values from -1 to 1
- post_gain: float32 [768], replicated, may hold values from 0.5 to 1.5
- post_bias: float32 [768], replicated, may hold values from -1 to 1
- w_proj: float32 [768, 512], replicated, may hold values from -0.21875 to 0.21875
- captions: float32 [384, 512], P('dp'), may hold values from 0.01 to 0.1
- logit_scale: float32 [1], replicated, may hold values from 3 to 3.7
- caption_counts: int32 [128], P('dp'), may hold values from 1 to 5, as said below
- positives: int32 [128, 5], P('dp'), may hold values from -1 to 383, as said below
Outputs:
- loss: float32 [1], replicated
- block_out: bfloat16 [128, 52, 768], P('dp')
- images_grad: float32 [128, 52, 768], P('dp')
- ln1_gain_grad: float32 [768], replicated
- ln1_bias_grad: float32 [768], replicated
- w_qkv_grad: float32 [768, 3, 768], P(None, None, 'mp')
- qv_bias_grad: float32 [2, 768], P(None, 'mp')
- w_out_grad: float32 [768, 768], P('mp')
- out_bias_grad: float32 [768], replicated
- ln2_gain_grad: float32 [768], replicated
- ln2_bias_grad: float32 [768], replicated
- w_fc1_grad: float32 [768, 3072], P(None, 'mp')
- fc1_bias_grad: float32 [3072], P('mp')
- w_fc2_grad: float32 [3072, 768], P('mp')
- fc2_bias_grad: float32 [768], replicated
- post_gain_grad: float32 [768], replicated
- post_bias_grad: float32 [768], replicated
- w_proj_grad: float32 [768, 512], replicated
- captions_grad: float32 [384, 512], P('dp')
- logit_scale_grad: float32 [1], replicated
The draws below stay inside these ranges and needn't reach their ends.
Inputs may be any that keep to these rules, and one draw needn't show every extreme that they name: `caption_counts`: the counts of all images sum to 384. `positives`: row i names the distinct captions of image i in its first caption_counts[i] places and holds -1 in the rest; every caption belongs to exactly one image.
All inputs are finite; a program needn't handle non-finite values.
Results may differ from the reference program's by a relative error of at most 0.03.
Values may be sent and summed in bfloat16 or wider, within the bound.
A program may use at most 128 MiB of HBM per device.

```python
import math
import jax
import jax.numpy as jnp
from jax import lax

D = 768
HEADS = 12
HEAD_DIM = 64
FF = 3072
EMB = 512
SEQ = 52
MAXPOS = 5
IMAGES = 128
CAPTIONS = 384


def caption_plan(key):
    base = jax.random.fold_in(key, 11)
    first_key, second_key, third_key = jax.random.split(base, 3)
    half_count = IMAGES // 2
    firsts = jax.random.randint(first_key, (half_count,), 1, 6)
    firsts = jnp.where(jnp.arange(half_count) == 0, 5, firsts)
    counts = jnp.concatenate([firsts, 6 - firsts])
    counts = counts[jax.random.permutation(second_key, IMAGES)]
    offsets = jnp.cumsum(counts) - counts
    order = jax.random.permutation(third_key, CAPTIONS)
    places = jnp.arange(MAXPOS)
    where_at = jnp.minimum(offsets[:, None] + places[None, :], CAPTIONS - 1)
    listed = jnp.where(places[None, :] < counts[:, None], order[where_at], -1)
    return (counts.astype(jnp.int32), listed.astype(jnp.int32))


def draw_caption_counts(key, part):
    return caption_plan(key)[0]


def draw_positives(key, part):
    return caption_plan(key)[1]


def shard_levels(stream_key, dims, pieces, smallest, high):
    level, own = 1.0, jax.random.fold_in(stream_key, 6)
    for position, parts in pieces:
        draws = jnp.exp(jax.random.uniform(jax.random.fold_in(own, position), (parts,), jnp.float32, smallest / len(pieces), high / len(pieces)))
        level = level * jnp.repeat(draws, dims[position] // parts).reshape([-1 if axis == position else 1 for axis in range(len(dims))])
    return level


def normal_values(key, shape, deviation, reach, shards=(), kind=jnp.bfloat16):
    values = deviation * jax.random.normal(key, shape, jnp.float32)
    if shards:
        values = values * shard_levels(key, shape, shards, -0.22, 0.18)
    return jnp.clip(values, -reach, reach).astype(kind)


def setup_inputs(seed: int = 0) -> dict:
    key_of = jax.random.split(jax.random.key(seed), 21)
    images = normal_values(key_of[0], (IMAGES, SEQ, D), 1.0, 6.0, ((0, 8),))
    ln1_gain = jnp.clip(1.0 + 0.1 * jax.random.normal(key_of[1], (D,), jnp.float32), 0.5, 1.5).astype(jnp.bfloat16)
    ln1_bias = normal_values(key_of[2], (D,), 0.2, 1.0)
    w_qkv = normal_values(key_of[3], (D, 3, D), D ** -0.5, 0.21875, ((2, 4),))
    qv_bias = normal_values(key_of[4], (2, D), 0.2, 1.0, ((1, 4),))
    w_out = normal_values(key_of[5], (D, D), (D // 8) ** -0.5, 0.625, ((0, 4),))
    out_bias = normal_values(key_of[6], (D,), 0.2, 1.0)
    ln2_gain = jnp.clip(1.0 + 0.1 * jax.random.normal(key_of[7], (D,), jnp.float32), 0.5, 1.5).astype(jnp.bfloat16)
    ln2_bias = normal_values(key_of[8], (D,), 0.2, 1.0)
    w_fc1 = normal_values(key_of[9], (D, FF), D ** -0.5, 0.21875, ((1, 4),))
    fc1_bias = normal_values(key_of[10], (FF,), 0.3, 1.5, ((0, 4),))
    w_fc2 = normal_values(key_of[11], (FF, D), (FF // 2) ** -0.5, 0.15625, ((0, 4),))
    fc2_bias = normal_values(key_of[12], (D,), 0.2, 1.0)
    post_gain = jnp.clip(1.0 + 0.1 * jax.random.normal(key_of[13], (D,), jnp.float32), 0.5, 1.5)
    post_bias = normal_values(key_of[14], (D,), 0.2, 1.0, (), jnp.float32)
    w_proj = normal_values(key_of[15], (D, EMB), D ** -0.5, 0.21875, (), jnp.float32)
    captions = jnp.clip(0.01 + 0.09 * jax.random.uniform(key_of[16], (CAPTIONS, EMB), jnp.float32) ** shard_levels(key_of[16], (CAPTIONS, EMB), ((0, 8),), -0.2, 0.2), 0.01, 0.1)
    logit_scale = jnp.clip(jax.random.uniform(key_of[17], (1,), jnp.float32, 3.0, 3.7), 3.0, 3.7)
    caption_counts = draw_caption_counts(jax.random.fold_in(key_of[20], 71), 0)
    positives = draw_positives(jax.random.fold_in(key_of[20], 71), 0)
    return {"images": images, "ln1_gain": ln1_gain, "ln1_bias": ln1_bias, "w_qkv": w_qkv, "qv_bias": qv_bias, "w_out": w_out, "out_bias": out_bias, "ln2_gain": ln2_gain, "ln2_bias": ln2_bias, "w_fc1": w_fc1, "fc1_bias": fc1_bias, "w_fc2": w_fc2, "fc2_bias": fc2_bias, "post_gain": post_gain, "post_bias": post_bias, "w_proj": w_proj, "captions": captions, "logit_scale": logit_scale, "caption_counts": caption_counts, "positives": positives}


HIGH = lax.Precision.HIGHEST

@jax.custom_vjp
def low(v):
    return lax.optimization_barrier(v.astype(jnp.bfloat16)).astype(jnp.float32)

@jax.custom_vjp
def low_back(v):
    return v

def low_keep(v):
    return (low(v), None)

def low_pass(kept, grad):
    return (grad,)

def back_keep(v):
    return (v, None)

def back_low(kept, grad):
    return (low(grad),)
low.defvjp(low_keep, low_pass)
low_back.defvjp(back_keep, back_low)

def layer_norm(values, gain, shift):
    centre = values - lax.optimization_barrier(jnp.mean(values, -1, keepdims=True))
    spread = lax.rsqrt(lax.optimization_barrier(jnp.mean(centre * centre, -1, keepdims=True)) + 1e-05)
    return centre * spread * gain + shift

def block_layer(block, weights):
    gain_one, shift_one, w_qkv, qv_bias, w_out, out_bias, gain_two, shift_two, w_fc1, fc1_bias, w_fc2, fc2_bias = weights
    group = block.shape[0]
    attn_in = low(layer_norm(block, gain_one, shift_one))
    projected = jnp.einsum('gsd,dke->gske', attn_in, w_qkv, precision=HIGH)
    queries = low(low_back(projected[:, :, 0] + qv_bias[0])).reshape(group, SEQ, HEADS, HEAD_DIM)
    keys_all = low(low_back(projected[:, :, 1])).reshape(group, SEQ, HEADS, HEAD_DIM)
    values_all = low(low_back(projected[:, :, 2] + qv_bias[1])).reshape(group, SEQ, HEADS, HEAD_DIM)
    scores = low_back(jnp.einsum('gqhe,gkhe->ghqk', queries, keys_all, precision=HIGH) * 0.125)
    probs = low(jax.nn.softmax(scores, -1))
    context = jnp.einsum('ghqk,gkhe->gqhe', probs, values_all, precision=HIGH).reshape(group, SEQ, D)
    context = low(low_back(context))
    middle = block + low_back(jnp.einsum('gsd,de->gse', context, w_out, precision=HIGH)) + out_bias
    mlp_in = low(layer_norm(middle, gain_two, shift_two))
    pre_act = low_back(jnp.einsum('gsd,df->gsf', mlp_in, w_fc1, precision=HIGH) + fc1_bias)
    activated = low(pre_act * jax.nn.sigmoid(1.702 * pre_act))
    return middle + low_back(jnp.einsum('gsf,fd->gsd', activated, w_fc2, precision=HIGH)) + fc2_bias

def contrast_loss(cls_rows, post_gain, post_bias, w_proj, captions, logit_scale, caption_counts, positives):
    post = layer_norm(cls_rows, post_gain, post_bias)
    embedded = jnp.dot(post, w_proj, precision=HIGH)
    image_unit = embedded * lax.rsqrt(lax.optimization_barrier(jnp.sum(embedded * embedded, -1, keepdims=True)) + 1e-06)
    text_unit = captions * lax.rsqrt(lax.optimization_barrier(jnp.sum(captions * captions, -1, keepdims=True)) + 1e-06)
    image_low = low(image_unit)
    text_low = low(text_unit)
    scale = jnp.exp(logit_scale[0])
    logits = low_back(scale * jnp.dot(image_low, text_low.T, precision=HIGH))
    caption_ids = jnp.arange(CAPTIONS, dtype=jnp.int32)
    matches = jnp.any(positives[:, :, None] == caption_ids[None, None, :], axis=1).astype(logits.dtype)
    row_lse = jax.nn.logsumexp(logits, axis=1)
    col_lse = jax.nn.logsumexp(logits, axis=0)
    image_terms = row_lse - lax.optimization_barrier(jnp.sum(matches * logits, 1)) / caption_counts.astype(logits.dtype)
    text_terms = col_lse - lax.optimization_barrier(jnp.sum(matches * logits, 0))
    return 0.5 * (jnp.mean(image_terms) + jnp.mean(text_terms))

def reference(images, ln1_gain, ln1_bias, w_qkv, qv_bias, w_out, out_bias, ln2_gain, ln2_bias, w_fc1, fc1_bias, w_fc2, fc2_bias, post_gain, post_bias, w_proj, captions, logit_scale, caption_counts, positives):
    params = tuple((t.astype(jnp.float32) for t in (images, ln1_gain, ln1_bias, w_qkv, qv_bias, w_out, out_bias, ln2_gain, ln2_bias, w_fc1, fc1_bias, w_fc2, fc2_bias, post_gain, post_bias, w_proj, captions, logit_scale)))

    def forward(inputs, *rest):
        weights = rest[:12]
        group = math.gcd(IMAGES, 64)

        def one_group(block):
            return block_layer(block, weights)
        blocks = inputs.reshape(IMAGES // group, group, SEQ, D)
        result = lax.map(jax.checkpoint(one_group), blocks).reshape(IMAGES, SEQ, D)
        loss = contrast_loss(result[:, 0], rest[12], rest[13], rest[14], rest[15], rest[16], caption_counts, positives)
        return (loss, result)
    loss, pullback, result = jax.vjp(forward, *params, has_aux=True)
    grads = pullback(jnp.ones((), loss.dtype))
    return (loss.reshape(1), result.astype(jnp.bfloat16), grads[0], grads[1], grads[2], grads[3], grads[4], grads[5], grads[6], grads[7], grads[8], grads[9], grads[10], grads[11], grads[12], grads[13], grads[14], grads[15], grads[16], grads[17])
```

```python
import jax
import jax.numpy as jnp
from jax import lax
from jax.sharding import PartitionSpec as P

HEAD_DIM = 64
HIGH = lax.Precision.HIGHEST
F32 = jnp.float32
BF16 = jnp.bfloat16


def norm_rows(values, gain, shift):
    centre = values - jnp.mean(values, -1, keepdims=True)
    spread = lax.rsqrt(jnp.mean(centre * centre, -1, keepdims=True) + 1e-05)
    scaled = centre * spread
    return (scaled * gain + shift, scaled, spread)


def norm_back(upper, gain, scaled, spread):
    inner = upper * gain
    return spread * (
        inner
        - jnp.mean(inner, -1, keepdims=True)
        - scaled * jnp.mean(inner * scaled, -1, keepdims=True)
    )


def dot(a, b, ca=1, cb=0, precision=None):
    return lax.dot_general(
        a, b, (((ca,), (cb,)), ((), ())), precision=precision, preferred_element_type=F32
    )


def gather_dp(x):
    return lax.all_gather(x, "dp", axis=0, tiled=True)


def gather_mp(x):
    return lax.all_gather(x, "mp", axis=0, tiled=True)


def sum_mp(x):
    return lax.psum(x, "mp")


def body(
    images,
    ln1_gain,
    ln1_bias,
    w_qkv,
    qv_bias,
    w_out,
    out_bias,
    ln2_gain,
    ln2_bias,
    w_fc1,
    fc1_bias,
    w_fc2,
    fc2_bias,
    post_gain,
    post_bias,
    w_proj,
    captions,
    logit_scale,
    caption_counts,
    positives,
):
    group, seq, width = images.shape
    rows = group * seq
    local = w_qkv.shape[2]
    heads = local // HEAD_DIM
    dp = lax.axis_index("dp")
    image_total = group * lax.axis_size("dp")
    cap_own = captions.shape[0]
    caption_total = cap_own * lax.axis_size("dp")

    x = jnp.transpose(images, (1, 0, 2)).reshape(rows, width).astype(F32)
    wt = jnp.transpose(w_qkv, (1, 2, 0)).reshape(3 * local, width)
    g1, b1, g2, b2 = (v.astype(F32) for v in (ln1_gain, ln1_bias, ln2_gain, ln2_bias))
    attn_f, xhat, spread1 = norm_rows(x, g1, b1)
    attn_in = attn_f.astype(BF16)
    bias = qv_bias.astype(F32)
    q = (dot(attn_in, wt[:local], 1, 1) + bias[0]).astype(BF16)
    k = dot(attn_in, wt[local : 2 * local], 1, 1).astype(BF16)
    v = (dot(attn_in, wt[2 * local :], 1, 1) + bias[1]).astype(BF16)

    lane_head = lax.broadcasted_iota(jnp.int32, (heads, group, local), 2) // HEAD_DIM
    own_head = lane_head == lax.broadcasted_iota(jnp.int32, (heads, group, local), 0)
    own_head = own_head.reshape(heads * group, local)

    def spread_heads(t):
        return jnp.where(own_head, jnp.tile(t, (heads, 1)), 0)

    def join_heads(t):
        return jnp.sum(jnp.where(own_head, t, 0).reshape(heads, group, local), 0)

    hg = heads * group
    same = (
        lax.broadcasted_iota(jnp.int32, (hg, rows), 0) % group
        == lax.broadcasted_iota(jnp.int32, (hg, rows), 1) % group
    )
    q_cls = q[:group]
    qx = spread_heads(q_cls)
    scores = jnp.where(same, dot(qx, k, 1, 1) * 0.125, -jnp.inf)
    probs = jax.nn.softmax(scores, -1)
    probs_low = probs.astype(BF16)
    ctx_cls = join_heads(dot(probs_low, v)).astype(BF16)
    b_rows = dot(probs_low, attn_in).astype(BF16)
    prob_sum = jnp.sum(probs_low.astype(F32), -1, keepdims=True)

    def grouped(t):
        return jnp.transpose(t.reshape(seq, group, heads, HEAD_DIM), (1, 2, 0, 3))

    sc = jnp.einsum("ghqe,ghke->ghqk", grouped(q), grouped(k), preferred_element_type=F32) * 0.125
    pr = jax.nn.softmax(sc, -1).astype(BF16)
    ctx = jnp.einsum("ghqk,ghke->ghqe", pr, grouped(v), preferred_element_type=F32)
    ctx = jnp.transpose(ctx, (2, 0, 1, 3)).reshape(rows, local).astype(BF16)

    x_cls = gather_dp(images[:, 0])
    text_unit_own_factor = lax.rsqrt(jnp.sum(captions * captions, -1, keepdims=True) + 1e-06)
    text_unit = captions * text_unit_own_factor
    text_low = gather_dp(text_unit.astype(BF16))
    plan = gather_dp(jnp.concatenate([positives, caption_counts[:, None]], 1))
    w_out_all = gather_mp(w_out)
    ctx_mine = gather_dp(ctx_cls)
    ctx_all = lax.all_gather(ctx_mine, "mp", axis=1, tiled=True)
    middle = x_cls.astype(F32) + dot(ctx_all, w_out_all) + out_bias.astype(F32)
    norm2, xhat2, spread2 = norm_rows(middle, g2, b2)
    mlp_in = norm2.astype(BF16)
    pre = dot(mlp_in, w_fc1) + fc1_bias.astype(F32)
    sigma = jax.nn.sigmoid(1.702 * pre)
    act = (pre * sigma).astype(BF16)
    y = middle + sum_mp(dot(act, w_fc2).astype(BF16)).astype(F32) + fc2_bias.astype(F32)

    ctx_full = lax.all_gather(ctx, "mp", axis=1, tiled=True)
    mid_bulk = x + dot(ctx_full, w_out_all) + out_bias.astype(F32)
    in_bulk = norm_rows(mid_bulk, g2, b2)[0].astype(BF16)
    pre_bulk = dot(in_bulk, w_fc1) + fc1_bias.astype(F32)
    act_bulk = (pre_bulk * jax.nn.sigmoid(1.702 * pre_bulk)).astype(BF16)
    out_bulk = sum_mp(dot(act_bulk, w_fc2).astype(BF16)).astype(F32)
    block_out = (mid_bulk + out_bulk + fc2_bias.astype(F32)).astype(BF16)

    post, post_hat, post_spread = norm_rows(y, post_gain, post_bias)
    emb = dot(post, w_proj, precision=HIGH)
    factor = lax.rsqrt(jnp.sum(emb * emb, -1, keepdims=True) + 1e-06)
    unit = emb * factor
    image_low = unit.astype(BF16)
    scale = jnp.exp(logit_scale[0])
    cosine = dot(image_low, text_low, 1, 1)
    logits = scale * cosine
    ids = lax.broadcasted_iota(jnp.int32, (image_total, caption_total), 1)
    match = jnp.zeros((image_total, caption_total), jnp.bool_)
    for place in range(positives.shape[1]):
        match |= plan[:, place : place + 1] == ids
    match = match.astype(F32)
    counts = plan[:, positives.shape[1] :].astype(F32)
    row_lse = jax.nn.logsumexp(logits, 1, keepdims=True)
    col_lse = jax.nn.logsumexp(logits, 0, keepdims=True)
    matched = match * logits
    loss = 0.5 / image_total * jnp.sum(
        row_lse - jnp.sum(matched, 1, keepdims=True) / counts
    ) + 0.5 / caption_total * jnp.sum(col_lse - jnp.sum(matched, 0, keepdims=True))
    dlog = 0.5 / image_total * (jnp.exp(logits - row_lse) - match / counts)
    dlog += 0.5 / caption_total * (jnp.exp(logits - col_lse) - match)
    dlog = dlog.astype(BF16)
    scale_grad = scale * jnp.sum(dlog.astype(F32) * cosine)
    dimage = scale * dot(dlog, text_low)
    dtext = scale * dot(dlog, image_low, 0, 0)
    dtext = lax.dynamic_slice_in_dim(dtext, dp * cap_own, cap_own)
    captions_grad = text_unit_own_factor * (
        dtext - text_unit * jnp.sum(text_unit * dtext, -1, keepdims=True)
    )
    demb = factor * (dimage - unit * jnp.sum(unit * dimage, -1, keepdims=True))
    proj_grad = dot(post, demb, 0, 0, HIGH)
    dpost = dot(demb, w_proj, 1, 1, HIGH)
    dcls = norm_back(dpost, post_gain, post_hat, post_spread)
    dy = dcls.astype(BF16)
    fc2_grad = dot(act, dy, 0, 0)
    dpre = dot(dy, w_fc2, 1, 1) * (sigma + 1.702 * pre * sigma * (1.0 - sigma))
    dpre = dpre.astype(BF16)
    fc1_grad = dot(mlp_in, dpre, 0, 0)
    dmlp = sum_mp(dot(dpre, w_fc1, 1, 1).astype(BF16)).astype(F32)
    dmid = dcls + norm_back(dmlp, g2, xhat2, spread2)
    dmid_low = dmid.astype(BF16)
    out_grad = dot(ctx_mine, dmid_low, 0, 0)
    dctx = dot(dmid_low, w_out, 1, 1).astype(BF16)

    dctx_own = lax.dynamic_slice_in_dim(dctx, dp * group, group)
    dmid_own = lax.dynamic_slice_in_dim(dmid, dp * group, group)
    dx = spread_heads(dctx_own)
    dprobs = dot(dx, v, 1, 1)
    dscores = probs * (dprobs - jnp.sum(probs * dprobs, -1, keepdims=True))
    dscores = (dscores * 0.125).astype(BF16)
    dq = join_heads(dot(dscores, k)).astype(BF16)
    a_rows = dot(dscores, attn_in).astype(BF16)
    u_k = dot(qx, wt[local : 2 * local]).astype(BF16)
    u_v = dot(dx, wt[2 * local :]).astype(BF16)
    u_q = dot(dq, wt[:local]).astype(BF16)
    fold = (
        lax.broadcasted_iota(jnp.int32, (rows, seq), 0) // group
        == lax.broadcasted_iota(jnp.int32, (rows, seq), 1)
    ).astype(BF16)
    coef = dot(jnp.concatenate([dscores, probs_low], 0), fold).astype(BF16)
    u_all = gather_mp(jnp.concatenate([u_k, u_v], 0))
    c_all = gather_mp(coef)
    q_all = jnp.sum(gather_mp(u_q).reshape(-1, group, width).astype(F32), 0)
    ct = dot(fold, c_all, 1, 1)
    ct = jnp.where(
        lax.broadcasted_iota(jnp.int32, ct.shape, 0) % group
        == lax.broadcasted_iota(jnp.int32, ct.shape, 1) % group,
        ct,
        0,
    ).astype(BF16)
    dattn = dot(ct, u_all)
    dattn = jnp.concatenate([dattn[:group] + q_all, dattn[group:]], 0)
    back1 = norm_back(dattn, g1, xhat, spread1)
    images_grad = jnp.concatenate([back1[:group] + dmid_own, back1[group:]], 0)

    a_all = gather_dp(a_rows)
    b_all = gather_dp(b_rows)
    dq_all = gather_dp(dq)
    qx_all = gather_dp(qx)
    dx_all = gather_dp(dx)
    attn_cls = norm_rows(x_cls.astype(F32), g1, b1)[0].astype(BF16)
    wq_grad = dot(dq_all, attn_cls, 0, 0)
    wk_grad = dot(qx_all, a_all, 0, 0)
    wv_grad = dot(dx_all, b_all, 0, 0)
    qkv_grad = jnp.concatenate([wq_grad, wk_grad, wv_grad], 0)
    qkv_grad = jnp.transpose(qkv_grad.reshape(3, local, width), (2, 0, 1))
    small = lax.psum(
        (
            jnp.sum(dattn * xhat, 0),
            jnp.sum(dattn, 0),
            jnp.stack(
                [jnp.sum(dq.astype(F32), 0), jnp.sum(dx.astype(F32) * prob_sum, 0)]
            ),
        ),
        "dp",
    )

    def as_images(t):
        return jnp.transpose(t.reshape(seq, group, width), (1, 0, 2))

    return (
        loss.reshape(1),
        as_images(block_out),
        as_images(images_grad),
        small[0],
        small[1],
        qkv_grad,
        small[2],
        out_grad,
        jnp.sum(dmid, 0),
        jnp.sum(dmlp * xhat2, 0),
        jnp.sum(dmlp, 0),
        fc1_grad,
        jnp.sum(dpre.astype(F32), 0),
        fc2_grad,
        jnp.sum(dcls, 0),
        jnp.sum(dpost * post_hat, 0),
        jnp.sum(dpost, 0),
        proj_grad,
        captions_grad,
        scale_grad.reshape(1),
    )


def solution(mesh):
    full, per_dp = P(), P("dp")
    return jax.shard_map(
        body,
        mesh=mesh,
        in_specs=(
            P("dp", None, None),
            full,
            full,
            P(None, None, "mp"),
            P(None, "mp"),
            P("mp", None),
            full,
            full,
            full,
            P(None, "mp"),
            P("mp"),
            P("mp", None),
            full,
            full,
            full,
            full,
            P("dp", None),
            full,
            per_dp,
            P("dp", None),
        ),
        out_specs=(
            full,
            P("dp", None, None),
            P("dp", None, None),
            full,
            full,
            P(None, None, "mp"),
            P(None, "mp"),
            P("mp", None),
            full,
            full,
            full,
            P(None, "mp"),
            P("mp"),
            P("mp", None),
            full,
            full,
            full,
            full,
            P("dp", None),
            full,
        ),
        check_vma=False,
    )
```

```python
import functools

import jax
import jax.numpy as jnp
from jax import lax
from jax.experimental import pallas as pl
from jax.experimental.pallas import tpu as pltpu
from jax.sharding import PartitionSpec as P

HEAD_DIM = 64
HIGH = lax.Precision.HIGHEST
F32 = jnp.float32
BF16 = jnp.bfloat16
MESH = pl.DeviceIdType.MESH
LOW = -1e30

G1, B1, G2, B2, OUTB, FC2B, PG, PB, FC1B, QB, VB, SCALE = range(12)
(LOSS, DG1, DB1, DQB, DVB, DOUTB, DG2, DB2, DFC1B, DFC2B, DPG, DPB) = range(12)


def norm_rows(values, gain, shift):
    centre = values - jnp.mean(values, -1, keepdims=True)
    spread = lax.rsqrt(jnp.mean(centre * centre, -1, keepdims=True) + 1e-05)
    scaled = centre * spread
    return (scaled * gain + shift, scaled, spread)


def norm_back(upper, gain, scaled, spread):
    inner = upper * gain
    return spread * (
        inner
        - jnp.mean(inner, -1, keepdims=True)
        - scaled * jnp.mean(inner * scaled, -1, keepdims=True)
    )


def dot(a, b, ca=1, cb=0, precision=None):
    return lax.dot_general(
        a, b, (((ca,), (cb,)), ((), ())), precision=precision, preferred_element_type=F32
    )


def iota(shape, dim):
    return lax.broadcasted_iota(jnp.int32, shape, dim)


def loop(count, step):
    if count == 1:
        step(0)
    else:
        lax.fori_loop(0, count, lambda i, c: (step(i), c)[1], 0)


def rows_at(index, size):
    if isinstance(index, int):
        return pl.ds(index * size, size)
    return pl.ds(pl.multiple_of(index * size, size), size)


class Plan:
    def __init__(self, mesh_sizes, images, w_qkv, w_fc1, w_proj, captions, positives):
        self.dps, self.mps = mesh_sizes
        self.group, self.seq, self.width = images.shape
        self.rows = self.group * self.seq
        self.local = w_qkv.shape[2]
        self.heads = self.local // HEAD_DIM
        self.hg = self.heads * self.group
        self.hidden = w_fc1.shape[1]
        self.emb = w_proj.shape[1]
        self.images = self.group * self.dps
        self.own = captions.shape[0]
        self.captions = self.own * self.dps
        self.places = positives.shape[1]
        self.block = min(128, self.images)
        self.blocks = self.images // self.block
        self.part = self.images // self.mps
        self.quarter = self.rows // self.mps

    def operands(self):
        r, d, loc, hid = self.rows, self.width, self.local, self.hidden
        return dict(
            x_in=((r, d), BF16),
            vec_in=((16, d), F32),
            plan_in=((self.group, 128), F32),
            wt_in=((3 * loc, d), BF16),
            wo_in=((loc, d), BF16),
            w1_in=((d, hid), BF16),
            w2_in=((hid, d), BF16),
            wp_in=((d, self.emb), F32),
            cap_in=((self.own, self.emb), F32),
        )

    def results(self):
        n, d, loc, hid = self.images, self.width, self.local, self.hidden
        return dict(
            block_out=((self.rows, d), BF16),
            images_out=((self.rows, d), F32),
            small_out=((16, d), F32),
            cap_out=((self.own, self.emb), F32),
            post_out=((n, d), F32),
            demb_out=((n, self.emb), F32),
            act_out=((n, hid), BF16),
            dy_out=((n, d), BF16),
            mlp_out=((n, d), BF16),
            dpre_out=((n, hid), BF16),
            ctx_out=((n, loc), BF16),
            dmid_out=((n, d), BF16),
            a_out=((self.dps * self.hg, d), BF16),
            b_out=((self.dps * self.hg, d), BF16),
            dq_out=((n, loc), BF16),
            dctx_out=((n, loc), BF16),
            xc_out=((n, d), BF16),
        )

    def scratch(self):
        r, d, loc, hid = self.rows, self.width, self.local, self.hidden
        n, m, hg, b = self.images, self.mps, self.hg, self.block
        return dict(
            x=((r, d), BF16),
            vec=((16, d), F32),
            wt=((3 * loc, d), BF16),
            w1=((d, hid), BF16),
            w2=((hid, d), BF16),
            wp=((d, self.emb), F32),
            cap=((self.own, self.emb), F32),
            wo=((m * loc, d), BF16),
            wod=((m * 128, d), BF16),
            attn=((r, d), BF16),
            q=((r, loc), BF16),
            k=((r, loc), BF16),
            v=((r, loc), BF16),
            q0=((r, 128), F32),
            q1=((r, 128), F32),
            k0=((r, 128), F32),
            k1=((r, 128), F32),
            v0=((r, 128), F32),
            v1=((r, 128), F32),
            c0=((r, 128), F32),
            c1=((r, 128), F32),
            qp=((128, 256), F32),
            kp=((128, 256), F32),
            vp=((128, 256), F32),
            probs=((hg, r), F32),
            plow=((hg, r), BF16),
            ca=((m, r, 128), BF16),
            cb=((m, r // 2, 128), BF16),
            mid=((r, d), F32),
            part=((r, d), BF16),
            half=((r // 2, d), BF16),
            send=((r // m, d), BF16),
            quart=((r // m, d), BF16),
            blk=((r, d), BF16),
            xc=((n, d), BF16),
            plan=((n, 128), F32),
            text=((self.captions, self.emb), BF16),
            cg=((m, n, loc), BF16),
            midc=((n, d), F32),
            mlp=((b, d), BF16),
            pre=((n, hid), F32),
            act=((b, hid), BF16),
            part1=((n, d), BF16),
            sum1=((m, n // m, d), BF16),
            all1=((n, d), BF16),
            part2=((n, d), BF16),
            sum2=((m, n // m, d), BF16),
            all2=((n, d), BF16),
            post=((b, d), F32),
            unit=((n, self.emb), F32),
            stat=((n, 2), F32),
            low=((n, self.emb), BF16),
            lg=((b, self.captions), F32),
            dtext=((self.own, self.emb), F32),
            arow=((hg, d), BF16),
            brow=((hg, d), BF16),
            crow=((8, self.captions), F32),
            demb=((b, self.emb), F32),
            dy=((b, d), BF16),
            dpre=((b, hid), BF16),
            dmid=((n, d), F32),
            dmidl=((b, d), BF16),
            dctx=((n, loc), BF16),
            capg=((self.own, self.emb), F32),
            small=((16, d), F32),
            dq=((n, loc), BF16),
            u=((m * 2 * hg, d), BF16),
            uq=((m * self.group, d), BF16),
            coef=((m * 2 * hg, 128), BF16),
            dattn=((r, d), F32),
            tot=((self.dps * 24, 128), F32),
        )


def kernel(plan, *refs):
    names = [*plan.operands(), *plan.results(), *plan.scratch()]
    sems = refs[len(names)]
    used = iter(range(256))

    def sem():
        return sems.at[next(used)]

    R = dict(zip(names, refs))
    rows, width, local, heads = plan.rows, plan.width, plan.local, plan.heads
    group, hg, dps, mps = plan.group, plan.hg, plan.dps, plan.mps
    dp, mp = lax.axis_index("dp"), lax.axis_index("mp")
    low_bit, high_bit = lax.rem(mp, 2), lax.div(mp, 2)
    near = mp + 1 - 2 * low_bit
    far = lax.rem(mp + 2, 4)
    ends = []
    put_sem = {n: sem() for n in ("mlp", "act", "post", "demb", "dy", "dpre", "dmidl")}

    def load(src, dst):
        copy = pltpu.make_async_copy(src, dst, sem())
        copy.start()
        return copy

    def store(name, dst=None):
        copy = pltpu.make_async_copy(R[name], R[dst or name + "_out"], sem())
        copy.start()
        ends.append(copy.wait)

    def put(name, i, value):
        R[name][...] = value
        copy = pltpu.make_async_copy(
            R[name], R[name.removesuffix("l") + "_out"].at[rows_at(i, plan.block)], put_sem[name]
        )
        copy.start()
        if plan.blocks == 1:
            ends.append(copy.wait)
        else:
            copy.wait()

    def send(src, dst, dp_to, mp_to, out, into):
        return pltpu.make_async_remote_copy(
            src_ref=src,
            dst_ref=dst,
            send_sem=out,
            recv_sem=into,
            device_id=(dp_to, mp_to),
            device_id_type=MESH,
        )

    class GatherDp:
        def __init__(self, buf, size, source=None):
            self.buf, self.size, self.source = buf, size, source
            self.out, self.into = sem(), sem()

        def start(self):
            mine = self.buf.at[rows_at(dp, self.size)]
            source = mine if self.source is None else self.source

            def one(i):
                to = lax.rem(dp + 1 + i, dps)
                send(source, mine, to, mp, self.out, self.into).start()

            loop(dps - 1, one)
            rest = self.buf.at[pl.ds(0, (dps - 1) * self.size)]
            self.all = send(rest, rest, dp, near, self.out, self.into)
            ends.append(self.all.wait_send)

        def wait(self):
            self.all.wait_recv()

    class GatherMp:
        def __init__(self, slot):
            self.slot = slot
            self.to_near = send(slot(mp), slot(mp), dp, near, sem(), sem())
            self.to_far = send(slot(mp), slot(mp), dp, far, sem(), sem())
            self.pass_on = send(slot(far), slot(far), dp, near, sem(), sem())

        def start(self):
            self.to_far.start()
            self.to_near.start()
            ends.extend([self.to_near.wait_send, self.to_far.wait_send])

        def forward(self):
            self.to_far.wait_recv()
            self.pass_on.start()
            ends.append(self.pass_on.wait_send)

        def wait(self):
            self.to_near.wait_recv()
            self.pass_on.wait_recv()

    class SumMp:
        def __init__(self, part, slots, total):
            self.part, self.slots, self.total = part, slots, total
            self.peers = [lax.rem(mp + i, mps) for i in (2, 3, 1)]
            self.out, self.into, self.back, self.done = sem(), sem(), sem(), sem()

        def start(self):
            for to in self.peers:
                send(
                    self.part.at[rows_at(to, plan.part)],
                    self.slots.at[mp],
                    dp,
                    to,
                    self.out,
                    self.into,
                ).start()
            self.slots[mp] = self.part[rows_at(mp, plan.part), :]
            three = self.slots.at[pl.ds(0, mps - 1)]
            self.first = send(three, three, dp, near, self.out, self.into)
            ends.append(self.first.wait_send)

        def turn(self):
            self.first.wait_recv()
            total = self.slots[0].astype(F32)
            for i in range(1, mps):
                total += self.slots[i].astype(F32)
            mine = rows_at(mp, plan.part)
            self.total[mine, :] = total.astype(BF16)
            for to in self.peers:
                send(
                    self.total.at[mine], self.total.at[mine], dp, to, self.back, self.done
                ).start()
            three = self.total.at[pl.ds(0, (mps - 1) * plan.part)]
            self.second = send(three, three, dp, near, self.back, self.done)
            ends.append(self.second.wait_send)

        def wait(self):
            self.second.wait_recv()

    barrier = pltpu.get_barrier_semaphore()

    def greet(i):
        pl.semaphore_signal(
            barrier, inc=1, device_id=(lax.rem(dp + 1 + i, dps), mp), device_id_type=MESH
        )

    loop(dps - 1, greet)
    for i in range(1, mps):
        pl.semaphore_signal(
            barrier, inc=1, device_id=(dp, lax.rem(mp + i, mps)), device_id_type=MESH
        )
    vec = R["vec"]
    got_vec = load(R["vec_in"], vec)
    got_x = load(R["x_in"], R["x"])
    got_wt = load(R["wt_in"], R["wt"])
    got_cls = load(
        R["x_in"].at[pl.ds(0, group)], R["xc"].at[rows_at(dp, group)]
    )
    got_plan = load(R["plan_in"], R["plan"].at[rows_at(dp, group)])
    got_wo = load(R["wo_in"], R["wo"].at[rows_at(mp, local)])
    got_cap = load(R["cap_in"], R["cap"])
    got_w1 = load(R["w1_in"], R["w1"])
    got_w2 = load(R["w2_in"], R["w2"])
    got_wp = load(R["wp_in"], R["wp"])
    R["small"][...] = jnp.zeros_like(R["small"])
    R["crow"][...] = jnp.zeros_like(R["crow"])
    R["dtext"][...] = jnp.zeros_like(R["dtext"])
    R["qp"][...] = jnp.zeros_like(R["qp"])
    R["kp"][...] = jnp.zeros_like(R["kp"])
    R["vp"][...] = jnp.zeros_like(R["vp"])
    for name in ("q1", "k1", "v1"):
        R[name][...] = jnp.zeros_like(R[name])
    got_vec.wait()
    got_x.wait()

    def row(i, size=width):
        return vec[i : i + 1, 0:size]

    def first_norm(i):
        at = rows_at(i, 64)
        normed = norm_rows(R["x"][at, :].astype(F32), row(G1), row(B1))[0]
        R["attn"][at, :] = normed.astype(BF16)

    loop(rows // 64, first_norm)
    pl.semaphore_wait(barrier, dps - 1 + mps - 1)
    got_wo.wait()
    gather_wo = GatherMp(lambda i: R["wo"].at[rows_at(i, local)])
    gather_wo.start()
    got_cls.wait()
    gather_xc = GatherDp(R["xc"], group)
    gather_xc.start()
    got_plan.wait()
    gather_plan = GatherDp(R["plan"], group)
    gather_plan.start()
    got_wt.wait()

    def project(i):
        at = rows_at(i, plan.quarter)
        a = R["attn"][at, :]
        for j, (name, shift) in enumerate((("q", QB), ("k", None), ("v", VB))):
            t = dot(a, R["wt"][j * local : (j + 1) * local, :], 1, 1)
            if shift is not None:
                t = t + row(shift, local)
            t = t.astype(BF16)
            R[name][at, :] = t
            t = t.astype(F32)
            R[name + "0"][at, :] = t[:, 0:128]
            R[name + "1"][at, 0 : local - 128] = t[:, 128:local]

    loop(mps, project)

    lane_head = iota((hg, local), 1) // HEAD_DIM
    own_head = lane_head == iota((hg, local), 0) // group

    def spread_heads(t):
        wide = jnp.concatenate([t.astype(F32)] * heads, 0)
        return jnp.where(own_head, wide, 0.0).astype(BF16)

    def join_heads(t):
        t = jnp.where(own_head, t, 0.0)
        total = t[0:group]
        for h in range(1, heads):
            total = total + t[h * group : (h + 1) * group]
        return total

    same = lax.rem(iota((hg, rows), 0), group) == lax.rem(iota((hg, rows), 1), group)
    qx = spread_heads(R["q"][0:group, :])
    scores = jnp.where(same, dot(qx, R["k"][...], 1, 1) * 0.125, LOW)
    weights = jnp.exp(scores - jnp.max(scores, -1, keepdims=True))
    probs = weights / jnp.sum(weights, -1, keepdims=True)
    R["probs"][...] = probs
    R["plow"][...] = probs.astype(BF16)
    mine = rows_at(dp, group)
    ctx = join_heads(dot(R["plow"][...], R["v"][...])).astype(BF16)
    cg = R["cg"].at[mp]
    cg[mine, :] = ctx
    gather_ctx = GatherDp(cg, group)
    gather_ctx.start()
    got_cap.wait()
    cap = R["cap"][...]
    cap_factor = lax.rsqrt(jnp.sum(cap * cap, -1, keepdims=True) + 1e-06)
    R["text"][rows_at(dp, plan.own), :] = (cap * cap_factor).astype(BF16)
    gather_text = GatherDp(R["text"], plan.own)
    gather_text.start()
    gather_wo.forward()

    def attend(t):
        for j in range(2):
            at = pl.ds(2 * t + j, plan.seq, stride=group)
            for name in "qkv":
                for i in range(2):
                    into = R[name + "p"].at[j * 64 : j * 64 + plan.seq, i * 128 : i * 128 + 128]
                    into[...] = R[name + str(i)][at, :]
        qb = R["qp"][...].astype(BF16)
        kb, vb = R["kp"][...], R["vp"][...]
        head_of = iota((128, 256), 1) // HEAD_DIM
        r, c = iota((128, 128), 0), iota((128, 128), 1)
        seen = (r // 64 == c // 64) & (lax.rem(c, 64) < plan.seq)
        total = jnp.zeros((128, 256), F32)
        for h in range(heads):
            kh = jnp.where(head_of == h, kb, 0.0).astype(BF16)
            vh = jnp.where(head_of == h, vb, 0.0).astype(BF16)
            s = jnp.where(seen, dot(qb, kh, 1, 1) * 0.125, LOW)
            e = jnp.exp(s - jnp.max(s, -1, keepdims=True))
            p = (e / jnp.sum(e, -1, keepdims=True)).astype(BF16)
            total += dot(p, vh)
        for j in range(2):
            at = pl.ds(2 * t + j, plan.seq, stride=group)
            for i in range(2):
                R["c" + str(i)][at, :] = total[
                    j * 64 : j * 64 + plan.seq, i * 128 : i * 128 + 128
                ]

    loop(group // 2, attend)
    R["ca"][mp] = R["c0"][...].astype(BF16)
    R["cb"][mp] = jnp.concatenate(
        [R["c1"][0 : rows // 2, 0:64], R["c1"][rows // 2 : rows, 0:64]], 1
    ).astype(BF16)

    gather_ctx.wait()
    gather_cg = GatherMp(lambda i: R["cg"].at[i])
    gather_cg.start()
    gather_ca = GatherMp(lambda i: R["ca"].at[i])
    gather_cb = GatherMp(lambda i: R["cb"].at[i])
    gather_ca.start()
    gather_cb.start()

    R["brow"][...] = dot(R["plow"][...], R["attn"][...]).astype(BF16)
    gather_b = GatherDp(R["b_out"], hg, R["brow"])
    gather_b.start()
    ends.append(load(R["brow"], R["b_out"].at[rows_at(dp, hg)]).wait)

    gather_cg.forward()
    gather_wo.wait()
    for m in range(mps):
        tail = R["wo"][m * local + 128 : (m + 1) * local, :]
        R["wod"][m * 128 : (m + 1) * 128, :] = jnp.concatenate([tail, tail], 0)
    gather_xc.wait()
    got_w1.wait()
    got_w2.wait()
    gather_cg.wait()

    def class_forward(i):
        at = rows_at(i, plan.block)
        total = R["xc"][at, :].astype(F32) + row(OUTB)
        for m in range(mps):
            total += dot(R["cg"][m, at, :], R["wo"][m * local : (m + 1) * local, :])
        R["midc"][at, :] = total
        mlp = norm_rows(total, row(G2), row(B2))[0].astype(BF16)
        put("mlp", i, mlp)
        pre = dot(mlp, R["w1"][...]) + row(FC1B, plan.hidden)
        R["pre"][at, :] = pre
        act = (pre * jax.nn.sigmoid(1.702 * pre)).astype(BF16)
        put("act", i, act)
        R["part1"][at, :] = dot(act, R["w2"][...]).astype(BF16)

    loop(plan.blocks, class_forward)
    sum1 = SumMp(R["part1"], R["sum1"], R["all1"])
    sum1.start()
    store("xc")

    size = plan.quarter

    def bulk(index):
        at = rows_at(index, size)
        side = lax.div(index, 2)
        at_half = rows_at(lax.rem(index, 2), size)
        total = R["x"][at, :].astype(F32) + row(OUTB)
        keep = iota((size, 128), 1) // HEAD_DIM == side
        for m in range(mps):
            total += dot(R["ca"][m, at, :], R["wo"][m * local : m * local + 128, :])
            tail = jnp.where(keep, R["cb"][m, at_half, :].astype(F32), 0.0).astype(BF16)
            total += dot(tail, R["wod"][m * 128 : (m + 1) * 128, :])
        R["mid"][at, :] = total
        mlp = norm_rows(total, row(G2), row(B2))[0].astype(BF16)
        pre = dot(mlp, R["w1"][...]) + row(FC1B, plan.hidden)
        act = (pre * jax.nn.sigmoid(1.702 * pre)).astype(BF16)
        R["part"][at, :] = dot(act, R["w2"][...]).astype(BF16)

    q_near_far = 2 * (1 - low_bit) + 1 - high_bit
    q_near = 2 * (1 - low_bit) + high_bit
    q_far = 2 * low_bit + 1 - high_bit
    q_own = 2 * low_bit + high_bit

    def to_near(index, slot):
        move = send(
            R["part"].at[rows_at(index, size)],
            R["half"].at[pl.ds(slot * size, size)],
            dp,
            near,
            sem(),
            sem(),
        )
        move.start()
        ends.append(move.wait_send)
        return move

    gather_ca.forward()
    gather_cb.forward()
    gather_ca.wait()
    gather_cb.wait()
    bulk(q_near_far)
    half0 = to_near(q_near_far, 0)
    sum1.turn()
    bulk(q_near)
    half1 = to_near(q_near, 1)
    gather_text.wait()
    gather_plan.wait()
    got_wp.wait()
    sum1.wait()

    scale = jnp.exp(row(SCALE, 1))
    crow = R["crow"]
    crow[0:1, :] = jnp.full((1, plan.captions), LOW, F32)

    def class_out(at):
        return R["midc"][at, :] + R["all1"][at, :].astype(F32) + row(FC2B)

    def logits_at(at):
        if plan.blocks == 1:
            return R["lg"][...]
        return scale * dot(R["low"][at, :], R["text"][...], 1, 1)

    def head(i):
        at = rows_at(i, plan.block)
        post = norm_rows(class_out(at), row(PG), row(PB))[0]
        put("post", i, post)
        emb = dot(post, R["wp"][...], precision=HIGH)
        factor = lax.rsqrt(jnp.sum(emb * emb, -1, keepdims=True) + 1e-06)
        R["stat"][at, 0:1] = factor
        unit = emb * factor
        R["unit"][at, :] = unit
        image_low = unit.astype(BF16)
        R["low"][at, :] = image_low
        logits = scale * dot(image_low, R["text"][...], 1, 1)
        R["lg"][...] = logits
        crow[0:1, :] = jnp.maximum(crow[0:1, :], jnp.max(logits, 0, keepdims=True))

    loop(plan.blocks, head)

    def matches(at):
        ids = iota((plan.block, plan.captions), 1).astype(F32)
        found = R["plan"][at, 0:1] == ids
        for place in range(1, plan.places):
            found |= R["plan"][at, place : place + 1] == ids
        return jnp.where(found, 1.0, 0.0)

    def put_small(i, value):
        R["small"][i : i + 1, 0 : value.shape[1]] += value

    half_i, half_c = 0.5 / plan.images, 0.5 / plan.captions

    def stats(i):
        at = rows_at(i, plan.block)
        logits = logits_at(at)
        matched = matches(at) * logits
        crow[1:2, :] += jnp.sum(jnp.exp(logits - crow[0:1, :]), 0, keepdims=True)
        crow[2:3, :] += jnp.sum(matched, 0, keepdims=True)
        top = jnp.max(logits, 1, keepdims=True)
        lse = top + jnp.log(jnp.sum(jnp.exp(logits - top), 1, keepdims=True))
        R["stat"][at, 1:2] = lse
        counts = R["plan"][at, plan.places : plan.places + 1]
        terms = lse - jnp.sum(matched, 1, keepdims=True) / counts
        put_small(LOSS, half_i * jnp.sum(terms, 0, keepdims=True))

    loop(plan.blocks, stats)
    crow[3:4, :] = crow[0:1, :] + jnp.log(crow[1:2, :])
    put_small(LOSS, half_c * jnp.sum(crow[3:4, :] - crow[2:3, :], 1, keepdims=True))

    shape = (plan.captions, plan.own)
    own_captions = iota(shape, 0) == iota(shape, 1) + dp * plan.own
    own_captions = jnp.where(own_captions, 1.0, 0.0).astype(BF16)

    def head_back(i):
        at = rows_at(i, plan.block)
        logits = logits_at(at)
        match = matches(at)
        counts = R["plan"][at, plan.places : plan.places + 1]
        dlog = half_i * (jnp.exp(logits - R["stat"][at, 1:2]) - match / counts)
        dlog += half_c * (jnp.exp(logits - crow[3:4, :]) - match)
        dlow = dlog.astype(BF16)
        both = jnp.sum(dlow.astype(F32) * logits, 1, keepdims=True)
        R["small"][LOSS : LOSS + 1, 128:129] += jnp.sum(both, 0, keepdims=True)
        dimage = scale * dot(dlow, R["text"][...])
        own = dot(dlow, own_captions).astype(BF16)
        R["dtext"][...] += dot(own, R["low"][at, :], 0, 0)
        unit = R["unit"][at, :]
        demb = R["stat"][at, 0:1] * (dimage - unit * jnp.sum(unit * dimage, -1, keepdims=True))
        put("demb", i, demb)
        dpost = dot(demb, R["wp"][...], 1, 1, HIGH)
        _, hat, spread = norm_rows(class_out(at), row(PG), row(PB))
        dcls = norm_back(dpost, row(PG), hat, spread)
        put_small(DPG, jnp.sum(dpost * hat, 0, keepdims=True))
        put_small(DPB, jnp.sum(dpost, 0, keepdims=True))
        put_small(DFC2B, jnp.sum(dcls, 0, keepdims=True))
        R["dmid"][at, :] = dcls
        dy = dcls.astype(BF16)
        put("dy", i, dy)
        pre = R["pre"][at, :]
        sigma = jax.nn.sigmoid(1.702 * pre)
        slope = sigma + 1.702 * pre * sigma * (1.0 - sigma)
        dpre = (dot(dy, R["w2"][...], 1, 1) * slope).astype(BF16)
        put("dpre", i, dpre)
        put_small(DFC1B, jnp.sum(dpre.astype(F32), 0, keepdims=True))
        R["part2"][at, :] = dot(dpre, R["w1"][...], 1, 1).astype(BF16)

    loop(plan.blocks, head_back)
    sum2 = SumMp(R["part2"], R["sum2"], R["all2"])
    sum2.start()
    dtext = scale * R["dtext"][...]
    text_unit = cap * cap_factor
    R["capg"][...] = cap_factor * (
        dtext - text_unit * jnp.sum(text_unit * dtext, -1, keepdims=True)
    )
    store("capg", "cap_out")

    bulk(q_far)
    half0.wait_recv()
    R["send"][...] = (
        R["part"][rows_at(q_far, size), :].astype(F32) + R["half"][0:size, :].astype(F32)
    ).astype(BF16)
    to_far = send(R["send"], R["quart"], dp, far, sem(), sem())
    to_far.start()
    ends.append(to_far.wait_send)
    sum2.turn()
    bulk(q_own)
    half1.wait_recv()
    sum2.wait()

    def class_back(i):
        at = rows_at(i, plan.block)
        dmlp = R["all2"][at, :].astype(F32)
        _, hat, spread = norm_rows(R["midc"][at, :], row(G2), row(B2))
        dmid = R["dmid"][at, :] + norm_back(dmlp, row(G2), hat, spread)
        put_small(DG2, jnp.sum(dmlp * hat, 0, keepdims=True))
        put_small(DB2, jnp.sum(dmlp, 0, keepdims=True))
        put_small(DOUTB, jnp.sum(dmid, 0, keepdims=True))
        R["dmid"][at, :] = dmid
        dlow = dmid.astype(BF16)
        put("dmidl", i, dlow)
        R["dctx"][at, :] = dot(dlow, R["wo"][rows_at(mp, local), :], 1, 1).astype(BF16)

    loop(plan.blocks, class_back)
    store("dctx")

    dx = spread_heads(R["dctx"][mine, :])
    qx = spread_heads(R["q"][0:group, :])
    probs = R["probs"][...]
    dprobs = dot(dx, R["v"][...], 1, 1)
    dscores = probs * (dprobs - jnp.sum(probs * dprobs, -1, keepdims=True))
    dscores = (dscores * 0.125).astype(BF16)
    dq = join_heads(dot(dscores, R["k"][...])).astype(BF16)
    R["dq"][mine, :] = dq
    R["arow"][...] = dot(dscores, R["attn"][...]).astype(BF16)
    gather_a = GatherDp(R["a_out"], hg, R["arow"])
    R["uq"][rows_at(mp, group), :] = dot(dq, R["wt"][0:local, :]).astype(BF16)
    uk = dot(qx, R["wt"][local : 2 * local, :])
    uv = dot(dx, R["wt"][2 * local : 3 * local, :])
    u_at = rows_at(mp, 2 * hg)
    R["u"][u_at, :] = jnp.concatenate([uk, uv], 0).astype(BF16)
    fold = jnp.where(
        iota((rows, 128), 0) // group == iota((rows, 128), 1), 1.0, 0.0
    ).astype(BF16)
    coef = jnp.concatenate([dot(dscores, fold), dot(R["plow"][...], fold)], 0)
    R["coef"][u_at, :] = coef.astype(BF16)
    gather_coef = GatherMp(lambda i: R["coef"].at[rows_at(i, 2 * hg)])
    gather_uq = GatherMp(lambda i: R["uq"].at[rows_at(i, group)])
    gather_u = GatherMp(lambda i: R["u"].at[rows_at(i, 2 * hg)])
    for g in (gather_coef, gather_uq, gather_u):
        g.start()
    gather_a.start()
    ends.append(load(R["arow"], R["a_out"].at[rows_at(dp, hg)]).wait)
    gather_dq = GatherDp(R["dq"], group)
    gather_dq.start()

    to_far.wait_recv()
    at = rows_at(q_own, size)
    quarter = R["part"][at, :].astype(F32) + R["half"][size : 2 * size, :].astype(F32)
    quarter += R["quart"][...].astype(F32)
    R["blk"][at, :] = (R["mid"][at, :] + quarter + row(FC2B)).astype(BF16)
    for g in (gather_coef, gather_uq, gather_u):
        g.forward()
    blk = R["blk"]
    blk_far = send(blk.at[at], blk.at[at], dp, far, sem(), sem())
    blk_far.start()
    for g in (gather_coef, gather_uq, gather_u):
        g.wait()

    def spread_coef(i):
        at = rows_at(i, size)
        pick = jnp.where(
            (iota((size, 128), 0) + i * size) // group == iota((size, 128), 1), 1.0, 0.0
        ).astype(BF16)
        wide = dot(pick, R["coef"][...], 1, 1)
        shape = wide.shape
        fits = lax.rem(iota(shape, 0), group) == lax.rem(iota(shape, 1), group)
        R["dattn"][at, :] = dot(jnp.where(fits, wide, 0.0).astype(BF16), R["u"][...])

    loop(mps, spread_coef)
    total = R["uq"][0:group, :].astype(F32)
    for m in range(1, mps):
        total += R["uq"][m * group : (m + 1) * group, :].astype(F32)
    R["dattn"][0:group, :] += total

    def first_back(i):
        at = rows_at(i, 64)
        upper = R["dattn"][at, :]
        _, hat, spread = norm_rows(R["x"][at, :].astype(F32), row(G1), row(B1))
        R["dattn"][at, :] = norm_back(upper, row(G1), hat, spread)
        put_small(DG1, jnp.sum(upper * hat, 0, keepdims=True))
        put_small(DB1, jnp.sum(upper, 0, keepdims=True))

    loop(rows // 64, first_back)
    R["dattn"][0:group, :] += R["dmid"][mine, :]
    store("dattn", "images_out")

    put_small(DQB, jnp.sum(dq.astype(F32), 0, keepdims=True))
    prob_sum = jnp.sum(R["plow"][...].astype(F32), -1, keepdims=True)
    put_small(DVB, jnp.sum(dx.astype(F32) * prob_sum, 0, keepdims=True))
    spans = []
    for i, count in ((DG1, width), (DB1, width), (DQB, local), (DVB, local)):
        spans += [(i, c, min(128, count - c)) for c in range(0, count, 128)]
    mine24 = pl.multiple_of(dp * 24, 8)
    R["tot"][pl.ds(mine24, 24), :] = jnp.zeros((24, 128), F32)
    for n, (i, c, size_c) in enumerate(spans):
        R["tot"][pl.ds(mine24 + n, 1), 0:size_c] = R["small"][i : i + 1, c : c + size_c]
    gather_tot = GatherDp(R["tot"], 24)
    gather_tot.start()
    blk_far.wait()
    both = blk.at[rows_at(low_bit, 2 * size)]
    blk_near = send(both, both, dp, near, sem(), sem())
    blk_near.start()
    gather_tot.wait()

    def add_up(i):
        for n, (j, c, size_c) in enumerate(spans):
            value = R["tot"][pl.ds(i * 24 + n, 1), 0:size_c]
            R["small"][j : j + 1, c : c + size_c] += value

    for i in (DG1, DB1, DQB, DVB):
        R["small"][i : i + 1, :] = jnp.zeros((1, width), F32)
    loop(dps, add_up)
    store("small")
    gather_dq.wait()
    store("dq")
    store_ctx = pltpu.make_async_copy(cg, R["ctx_out"], sem())
    store_ctx.start()
    ends.append(store_ctx.wait)
    gather_b.wait()
    blk_near.wait()
    store("blk", "block_out")
    gather_a.wait()
    for end in ends:
        end()


def run_kernel(plan, *operands):
    anywhere = pl.BlockSpec(memory_space=pl.ANY)
    return pl.pallas_call(
        functools.partial(kernel, plan),
        out_shape=[jax.ShapeDtypeStruct(s, t) for s, t in plan.results().values()],
        in_specs=[anywhere] * len(plan.operands()),
        out_specs=[anywhere] * len(plan.results()),
        scratch_shapes=[pltpu.VMEM(s, t) for s, t in plan.scratch().values()]
        + [pltpu.SemaphoreType.DMA((160,))],
        compiler_params=pltpu.CompilerParams(
            collective_id=0, has_side_effects=True, vmem_limit_bytes=61 << 20
        ),
    )(*operands)


def body(
    images,
    ln1_gain,
    ln1_bias,
    w_qkv,
    qv_bias,
    w_out,
    out_bias,
    ln2_gain,
    ln2_bias,
    w_fc1,
    fc1_bias,
    w_fc2,
    fc2_bias,
    post_gain,
    post_bias,
    w_proj,
    captions,
    logit_scale,
    caption_counts,
    positives,
):
    sizes = (lax.axis_size("dp"), lax.axis_size("mp"))
    plan = Plan(sizes, images, w_qkv, w_fc1, w_proj, captions, positives)
    width, local, group, heads = plan.width, plan.local, plan.group, plan.heads

    x = jnp.transpose(images, (1, 0, 2)).reshape(plan.rows, width)
    wt = jnp.transpose(w_qkv, (1, 2, 0)).reshape(3 * local, width)

    def fit(t):
        t = t.astype(F32)
        return jnp.pad(t, (0, width - t.shape[0]))

    vectors = (
        *(ln1_gain, ln1_bias, ln2_gain, ln2_bias, out_bias, fc2_bias, post_gain, post_bias),
        *(fc1_bias, qv_bias[0], qv_bias[1], logit_scale),
    )
    vec = jnp.stack([fit(t) for t in vectors] + [jnp.zeros((width,), F32)] * 4)
    table = jnp.concatenate([positives, caption_counts[:, None]], 1).astype(F32)
    table = jnp.pad(table, ((0, 0), (0, 128 - table.shape[1])))
    got = run_kernel(plan, x, vec, table, wt, w_out, w_fc1, w_fc2, w_proj, captions)
    R = dict(zip(plan.results(), got))

    hg = plan.hg
    lane_head = iota((heads, group, local), 2) // HEAD_DIM
    own_head = lane_head == iota((heads, group, local), 0)

    def spread_heads(t):
        t = t.reshape(plan.dps, 1, group, local)
        return jnp.where(own_head[None], t, 0).reshape(plan.dps * hg, local)

    attn_cls = norm_rows(R["xc_out"].astype(F32), ln1_gain.astype(F32), ln1_bias.astype(F32))[0]
    attn_cls = attn_cls.astype(BF16)
    q_all = (dot(attn_cls, wt[:local], 1, 1) + qv_bias[0].astype(F32)).astype(BF16)
    wq_grad = dot(R["dq_out"], attn_cls, 0, 0)
    wk_grad = dot(spread_heads(q_all), R["a_out"], 0, 0)
    wv_grad = dot(spread_heads(R["dctx_out"]), R["b_out"], 0, 0)
    qkv_grad = jnp.concatenate([wq_grad, wk_grad, wv_grad], 0)
    small = R["small_out"]

    def as_images(t):
        return jnp.transpose(t.reshape(plan.seq, group, width), (1, 0, 2))

    return (
        small[LOSS, 0:1],
        as_images(R["block_out"]),
        as_images(R["images_out"]),
        small[DG1],
        small[DB1],
        jnp.transpose(qkv_grad.reshape(3, local, width), (2, 0, 1)),
        small[DQB : DVB + 1, :local],
        dot(R["ctx_out"], R["dmid_out"], 0, 0),
        small[DOUTB],
        small[DG2],
        small[DB2],
        dot(R["mlp_out"], R["dpre_out"], 0, 0),
        small[DFC1B],
        dot(R["act_out"], R["dy_out"], 0, 0),
        small[DFC2B],
        small[DPG],
        small[DPB],
        dot(R["post_out"], R["demb_out"], 0, 0, HIGH),
        R["cap_out"],
        small[LOSS, 128:129],
    )


def solution(mesh):
    full, per_dp = P(), P("dp")
    return jax.shard_map(
        body,
        mesh=mesh,
        in_specs=(
            P("dp", None, None),
            full,
            full,
            P(None, None, "mp"),
            P(None, "mp"),
            P("mp", None),
            full,
            full,
            full,
            P(None, "mp"),
            P("mp"),
            P("mp", None),
            full,
            full,
            full,
            full,
            P("dp", None),
            full,
            per_dp,
            P("dp", None),
        ),
        out_specs=(
            full,
            P("dp", None, None),
            P("dp", None, None),
            full,
            full,
            P(None, None, "mp"),
            P(None, "mp"),
            P("mp", None),
            full,
            full,
            full,
            P(None, "mp"),
            P("mp"),
            P("mp", None),
            full,
            full,
            full,
            full,
            P("dp", None),
            full,
        ),
        check_vma=False,
    )
```

```python
import functools

import jax
import jax.numpy as jnp
from jax import lax
from jax.experimental import pallas as pl
from jax.experimental.pallas import tpu as pltpu
from jax.sharding import PartitionSpec as P

HEAD_DIM = 64
HIGH = lax.Precision.HIGHEST
F32 = jnp.float32
BF16 = jnp.bfloat16
MESH = pl.DeviceIdType.MESH
LOW = -1e30

G1, B1, G2, B2, OUTB, FC2B, PG, PB, FC1B, QB, VB, SCALE = range(12)
(LOSS, DG1, DB1, DQB, DVB, DOUTB, DG2, DB2, DFC1B, DFC2B, DPG, DPB) = range(12)


def norm_rows(values, gain, shift):
    centre = values - jnp.mean(values, -1, keepdims=True)
    spread = lax.rsqrt(jnp.mean(centre * centre, -1, keepdims=True) + 1e-05)
    scaled = centre * spread
    return (scaled * gain + shift, scaled, spread)


def norm_back(upper, gain, scaled, spread):
    inner = upper * gain
    return spread * (
        inner
        - jnp.mean(inner, -1, keepdims=True)
        - scaled * jnp.mean(inner * scaled, -1, keepdims=True)
    )


def dot(a, b, ca=1, cb=0, precision=None):
    return lax.dot_general(
        a, b, (((ca,), (cb,)), ((), ())), precision=precision, preferred_element_type=F32
    )


def iota(shape, dim):
    return lax.broadcasted_iota(jnp.int32, shape, dim)


def loop(count, step):
    if count == 1:
        step(0)
    else:
        lax.fori_loop(0, count, lambda i, c: (step(i), c)[1], 0)


def rows_at(index, size):
    if isinstance(index, int):
        return pl.ds(index * size, size)
    return pl.ds(pl.multiple_of(index * size, size), size)


class Named(dict):
    __getattr__ = dict.__getitem__


SEMS = 119


class Plan:
    def __init__(self, mesh_sizes, images, w_qkv, w_fc1, w_proj, captions, positives):
        self.dps, self.mps = mesh_sizes
        self.group, self.seq, self.width = images.shape
        self.rows = self.group * self.seq
        self.local = w_qkv.shape[2]
        self.heads = self.local // HEAD_DIM
        self.hg = self.heads * self.group
        self.hidden = w_fc1.shape[1]
        self.emb = w_proj.shape[1]
        self.images = self.group * self.dps
        self.own = captions.shape[0]
        self.captions = self.own * self.dps
        self.places = positives.shape[1]
        self.block = min(128, self.images)
        self.blocks = self.images // self.block
        self.part = self.images // self.mps
        self.quarter = self.rows // self.mps

    def semaphores(self):
        return SEMS + self.dps // 2 + (0 if self.blocks == 1 else 4)

    def operands(self):
        r, d, loc, hid = self.rows, self.width, self.local, self.hidden
        return dict(
            x_in=((r, d), BF16),
            wt_in=((3 * loc, d), BF16),
            wo_in=((loc, d), BF16),
            w1_in=((d, hid), BF16),
            w2_in=((hid, d), BF16),
            wp_in=((d, self.emb), F32),
            cap_in=((self.own, self.emb), F32),
            pos_in=((self.places, self.group), jnp.int32),
            count_in=((self.group,), jnp.int32),
            **{name + "_in": (s, t) for name, (s, t) in self.vectors().items()},
        )

    def vectors(self):
        d = self.width
        low = {name: ((d,), BF16) for name in ("g1", "b1", "g2", "b2", "ob", "f2b")}
        return dict(
            **low,
            pg=((d,), F32),
            pb=((d,), F32),
            f1b=((self.hidden,), BF16),
            qvb=((2, self.local), BF16),
            ls=((1,), F32),
        )

    def results(self):
        n, d, loc, hid = self.images, self.width, self.local, self.hidden
        return dict(
            block_out=((self.rows, d), BF16),
            images_out=((self.rows, d), BF16),
            small_out=((16, d), F32),
            cap_out=((self.own, self.emb), F32),
            post_out=((n, d), BF16),
            demb_out=((n, self.emb), BF16),
            act_out=((n, hid), BF16),
            dy_out=((n, d), BF16),
            mlp_out=((n, d), BF16),
            dpre_out=((n, hid), BF16),
            ctx_out=((n, loc), BF16),
            dmid_out=((n, d), BF16),
            a_out=((self.dps * self.hg, d), BF16),
            b_out=((self.dps * self.hg, d), BF16),
            dctx_out=((n, loc), BF16),
            ac_out=((n, d), BF16),
            qa_out=((n, loc), BF16),
        )

    def scratch(self):
        r, d, loc, hid = self.rows, self.width, self.local, self.hidden
        n, m, hg, b = self.images, self.mps, self.hg, self.block
        return dict(
            x=((r, d), BF16),
            vec=((16, d), F32),
            pos=((self.places, self.group), jnp.int32),
            count=((self.group,), jnp.int32),
            **self.vectors(),
            wt=((3 * loc, d), BF16),
            w1=((d, hid), BF16),
            w2=((hid, d), BF16),
            wpb=((d, self.emb), BF16),
            cap=((self.own, self.emb), F32),
            wo=((m * loc, d), BF16),
            attn=((r, d), BF16),
            hat=((r, d), BF16),
            spread=((r, 1), F32),
            q=((r, loc), BF16),
            k=((r, loc), BF16),
            v=((r, loc), BF16),
            q0=((64 * self.group, 128), F32),
            q1=((64 * self.group, 128), F32),
            k0=((64 * self.group, 128), F32),
            k1=((64 * self.group, 128), F32),
            v0=((64 * self.group, 128), F32),
            v1=((64 * self.group, 128), F32),
            probs=((hg, r), F32),
            plow=((hg, r), BF16),
            ca=((m, r, 128), BF16),
            cb=((m, r // 2, 128), BF16),
            mid=((r, d), F32),
            midq=((2, r // m, d), F32),
            part=((r, d), BF16),
            half=((r // 2, d), BF16),
            chip=((2, r // m, d), BF16),
            got=((2, r // m, d), BF16),
            blk=((r, d), BF16),
            xc=((n, d), BF16),
            plan=((n, 128), F32),
            text=((self.captions, self.emb), BF16),
            own=((self.own, self.emb), BF16),
            cg=((m, n, loc), BF16),
            midc=((n, d), F32),
            mlp=((b, d), BF16),
            pre=((n, hid), F32),
            act=((b, hid), BF16),
            part1=((n, d), BF16),
            sums=((4, n // 2, d), BF16),
            all1=((n, d), BF16),
            all2=((n, d), BF16),
            post=((b, d), BF16),
            unit=((n, self.emb), F32),
            stat=((n, 2), F32),
            low=((n, self.emb), BF16),
            lg=((b, self.captions), F32),
            dtext=((self.own, self.emb), F32),
            arow=((hg, d), BF16),
            brow=((hg, d), BF16),
            crow=((8, self.captions), F32),
            demb=((b, self.emb), BF16),
            dy=((b, d), BF16),
            dpre=((b, hid), BF16),
            dmid=((n, d), F32),
            dmidl=((b, d), BF16),
            dctx=((n, loc), BF16),
            capg=((self.own, self.emb), F32),
            small=((16, d), F32),
            ac=((b, d), BF16),
            qa=((b, loc), BF16),
            u=((m * 2 * hg, d), BF16),
            uq=((m * self.group, d), BF16),
            coef=((m * 2 * hg, 128), BF16),
            tot=((self.dps * 16, 128), BF16),
            sums_left=((16, 128), F32),
        )


def kernel(plan, *refs):
    names = [*plan.operands(), *plan.results(), *plan.scratch()]
    sems = refs[len(names)]
    used = iter(range(plan.semaphores()))

    places, free, ends = {}, [], []

    def sem():
        return sems.at[next(used)]

    def own():
        place = free.pop() if free else next(used)
        ref = sems.at[place]
        places[id(ref)] = (place, ref)
        return ref

    def done(copy):
        if copy.is_remote:
            copy.wait_send()
        else:
            copy.wait()
        free.append(places[id(copy.src_sem if copy.is_remote else copy.dst_sem)][0])

    def settle(count):
        for copy in ends[:count]:
            done(copy)
        del ends[:count]

    R = Named(zip(names, refs))
    rows, width, local, heads = plan.rows, plan.width, plan.local, plan.heads
    group, hg, dps, mps = plan.group, plan.hg, plan.dps, plan.mps
    dp, mp = lax.axis_index("dp"), lax.axis_index("mp")
    low_bit, high_bit = lax.rem(mp, 2), lax.div(mp, 2)
    near = mp + 1 - 2 * low_bit
    far = lax.rem(mp + 2, 4)
    put_sem = {n: own() for n in ("mlp", "act", "post", "demb", "dy", "dpre", "dmidl", "ac", "qa")}

    def dp_peer(i):
        return lax.rem(dp + dps + (i + 2) // 2 * (1 - 2 * (i % 2)), dps)

    def load(src, dst):
        copy = pltpu.make_async_copy(src, dst, own())
        copy.start()
        return copy

    def store(name, dst=None):
        ends.append(load(R[name], R[dst or name + "_out"]))

    def put(name, i, value):
        R[name][...] = value
        copy = pltpu.make_async_copy(
            R[name], R[name.removesuffix("l") + "_out"].at[rows_at(i, plan.block)], put_sem[name]
        )
        copy.start()
        if plan.blocks == 1:
            ends.append(copy)
        else:
            copy.wait()

    def send(src, dst, dp_to, mp_to, out, into):
        return pltpu.make_async_remote_copy(
            src_ref=src,
            dst_ref=dst,
            send_sem=out,
            recv_sem=into,
            device_id=(dp_to, mp_to),
            device_id_type=MESH,
        )

    class GatherDp:
        def __init__(self, buf, size, source=None):
            self.buf, self.size, self.source = buf, size, source
            self.out, self.into = own(), sem()

        def start(self):
            mine = self.buf.at[rows_at(dp, self.size)]
            source = mine if self.source is None else self.source

            def one(i):
                send(source, mine, dp_peer(i), mp, self.out, self.into).start()

            loop(dps - 1, one)
            rest = self.buf.at[pl.ds(0, (dps - 1) * self.size)]
            self.all = send(rest, rest, dp, near, self.out, self.into)
            ends.append(self.all)

        def wait(self):
            self.all.wait_recv()

    class GatherDpHalf:
        def __init__(self, buf, size, source):
            self.size, self.source = size, source
            self.out, self.into = own(), sem()
            half = buf.shape[1] // 2
            self.cols = pl.ds(pl.multiple_of(low_bit * half, 128), half)
            self.buf = buf.at[:, self.cols]
            self.near = send(self.buf, self.buf, dp, near, own(), sem())

        def start(self):
            source = self.source.at[:, self.cols]
            mine = self.buf.at[rows_at(dp, self.size)]
            self.own = load(source, mine)

            def one(i):
                send(source, mine, dp_peer(i), mp, self.out, self.into).start()

            loop(dps - 1, one)
            rest = self.buf.at[pl.ds(0, (dps - 1) * self.size)]
            self.all = send(rest, rest, dp, near, self.out, self.into)
            ends.append(self.all)

        def relay(self):
            done(self.own)
            self.all.wait_recv()
            self.near.start()
            ends.append(self.near)

        def wait(self):
            self.near.wait_recv()

    class GatherDpTwice:
        def __init__(self, buf, size, source):
            self.buf, self.size, self.source = buf, size, source
            self.out, self.into = own(), sem()
            self.beside = dp + 1 - 2 * lax.rem(dp, 2)
            self.arrive = [sem() for _ in range(dps // 2 - 1)]
            self.left = list(range(dps // 2 - 1))

        def at(self, i):
            return self.buf.at[rows_at(i, self.size)]

        def start(self):
            send(self.source, self.at(dp), self.beside, mp, self.out, self.into).start()
            for i, into in enumerate(self.arrive):
                send(self.source, self.at(dp), self.pair(i), mp, self.out, into).start()

        def pair(self, i):
            other, bit = lax.rem(dp, 2), 1
            while bit < dps // 2:
                other += 2 * bit * lax.rem(lax.div(dp, 2 * bit) + (i + 1) // bit, 2)
                bit *= 2
            return other

        def forward(self, part):
            count = len(self.arrive)
            for i in range(count * (part - 1) // 3, count * part // 3):
                block = self.at(self.pair(i))
                send(block, block, self.beside, mp, self.out, self.arrive[i]).wait_recv()
                send(block, block, self.beside, mp, self.out, self.into).start()

        def wait(self):
            half = self.buf.at[pl.ds(0, dps // 2 * self.size)]
            rest = self.buf.at[pl.ds(0, (dps - 1) * self.size)]
            send(half, half, self.beside, mp, self.out, self.into).wait_recv()
            ends.append(send(rest, rest, self.beside, mp, self.out, self.into))

    class GatherMp:
        def __init__(self, slot):
            self.slot = slot
            self.to_near = send(slot(mp), slot(mp), dp, near, own(), sem())
            self.to_far = send(slot(mp), slot(mp), dp, far, own(), sem())
            self.pass_on = send(slot(far), slot(far), dp, near, own(), sem())

        def start(self):
            self.to_far.start()
            self.to_near.start()
            ends.extend([self.to_near, self.to_far])

        def forward(self):
            self.to_far.wait_recv()
            self.pass_on.start()
            ends.append(self.pass_on)

        def wait(self):
            self.to_near.wait_recv()
            self.pass_on.wait_recv()

    class SumMp:
        def __init__(self, part, slots, got, total):
            self.part, self.slots, self.got, self.total = part, slots, got, total
            count = part.shape[0] // 2
            self.mine, other = rows_at(low_bit, count), rows_at(1 - low_bit, count)
            half = self.total.at[self.mine]
            self.first = send(part.at[other], slots.at[0], dp, near, own(), sem())
            self.second = send(slots.at[1], slots.at[got], dp, far, own(), sem())
            self.third = send(half, half, dp, near, own(), sem())

        def start(self):
            self.first.start()

        def middle(self):
            self.first.wait_recv()
            mine = self.part[self.mine, :].astype(F32)
            self.slots[1] = (mine + self.slots[0].astype(F32)).astype(BF16)
            self.second.start()

        def turn(self):
            self.second.wait_recv()
            done(self.second)
            total = self.slots[1].astype(F32) + self.slots[self.got].astype(F32)
            self.total[self.mine, :] = total.astype(BF16)
            self.third.start()
            ends.append(self.third)

        def wait(self):
            self.third.wait_recv()

    barrier = pltpu.get_barrier_semaphore()

    def greet(i):
        pl.semaphore_signal(
            barrier, inc=1, device_id=(lax.rem(dp + 1 + i, dps), mp), device_id_type=MESH
        )

    loop(dps - 1, greet)
    for i in range(1, mps):
        pl.semaphore_signal(
            barrier, inc=1, device_id=(dp, lax.rem(mp + i, mps)), device_id_type=MESH
        )
    vec = R.vec
    vectors = ("g1", "b1", "g2", "b2", "ob", "f2b", "pg", "pb", "f1b")
    got_first = [load(R[n + "_in"], R[n]) for n in ("x", "g1", "b1")]
    got_wo = load(R.wo_in, R.wo.at[rows_at(mp, local)])
    got_wt = load(R.wt_in, R.wt)
    got_small = [
        load(R[n + "_in"], R[n]) for n in (*vectors[2:], "qvb", "ls", "pos", "count", "cap")
    ]
    got_w1 = load(R.w1_in, R.w1)
    got_w2 = load(R.w2_in, R.w2)
    wp = R.mid.at[pl.ds(0, width), pl.ds(0, plan.emb)]
    got_wp = load(R.wp_in, wp)
    for name in ("small", "crow", "dtext", "q1"):
        R[name][...] = jnp.zeros_like(R[name])
    for name in ("v0", "v1"):
        R[name][rows : 64 * group, :] = jnp.zeros((64 * group - rows, 128), F32)

    def place(i):
        name = vectors[i]
        vec[i : i + 1, 0 : R[name].shape[0]] = R[name][...].astype(F32).reshape(1, -1)

    for got in got_first:
        done(got)
    place(0)
    place(1)

    def row(i, size=width):
        return vec[i : i + 1, 0:size]

    step = rows // 4

    def first_norm(i):
        at = rows_at(i, rows // 2)
        normed, hat, spread = norm_rows(R.x[at, :].astype(F32), row(G1), row(B1))
        R.spread[at, :] = spread
        R.attn[at, :] = normed.astype(BF16)
        R.hat[at, :] = hat.astype(BF16)

    loop(2, first_norm)
    for got in got_small:
        done(got)
    for i in range(2, len(vectors)):
        place(i)
    vec[QB : VB + 1, 0:local] = R.qvb[...].astype(F32)
    vec[SCALE : SCALE + 1, 0:1] = R.ls[...].reshape(1, 1)
    pl.semaphore_wait(barrier, dps - 1 + mps - 1)
    done(got_wo)
    gather_wo = GatherMp(lambda i: R.wo.at[rows_at(i, local)])
    gather_wo.start()
    done(got_wt)

    def project(i):
        at = rows_at(i, rows // 2)
        a = R.attn[at, :]
        for j, (name, shift) in enumerate((("q", QB), ("k", None), ("v", VB))):
            t = dot(a, R.wt[j * local : (j + 1) * local, :], 1, 1)
            if shift is not None:
                t = t + row(shift, local)
            t = t.astype(BF16)
            R[name][at, :] = t
            t = t.astype(F32)
            R[name + "0"][at, :] = t[:, 0:128]
            R[name + "1"][at, 0 : local - 128] = t[:, 128:local]

    loop(2, project)

    lane_head = iota((hg, local), 1) // HEAD_DIM
    own_head = lane_head == iota((hg, local), 0) // group

    def spread_heads(t):
        wide = jnp.concatenate([t.astype(F32)] * heads, 0)
        return jnp.where(own_head, wide, 0.0).astype(BF16)

    def join_heads(t):
        t = jnp.where(own_head, t, 0.0)
        total = t[0:group]
        for h in range(1, heads):
            total = total + t[h * group : (h + 1) * group]
        return total

    same = lax.rem(iota((hg, rows), 0), group) == lax.rem(iota((hg, rows), 1), group)
    qx = spread_heads(R.q[0:group, :])
    scores = jnp.where(same, dot(qx, R.k[...], 1, 1) * 0.125, LOW)
    weights = jnp.exp(scores - jnp.max(scores, -1, keepdims=True))
    probs = weights * (1.0 / jnp.sum(weights, -1, keepdims=True))
    R.probs[...] = probs
    R.plow[...] = probs.astype(BF16)
    mine = rows_at(dp, group)
    ctx = join_heads(dot(R.plow[...], R.v[...])).astype(BF16)
    cg = R.cg.at[mp]
    cg[mine, :] = ctx
    gather_ctx = GatherDp(cg, group)
    gather_ctx.start()
    gather_xc = GatherDpHalf(R.xc, group, R.x.at[pl.ds(0, group)])
    gather_xc.start()
    head_of = iota((128, 256), 1) // HEAD_DIM
    seen = iota((128, 128), 0) // 64 == iota((128, 128), 1) // 64
    seen &= lax.rem(iota((128, 128), 1), 64) < plan.seq

    def pair(t):
        both = [pl.ds(2 * t + j, 64, stride=group) for j in range(2)]

        def taken(name):
            parts = [R[name + i] for i in "01"]
            return jnp.concatenate(
                [jnp.concatenate([ref[at, :] for at in both], 0) for ref in parts], 1
            )

        qb = (taken("q") * 0.125).astype(BF16)
        kb, vb = taken("k"), taken("v")
        of_head = [head_of == h for h in range(heads)]
        k_wide = jnp.concatenate([jnp.where(m, kb, 0.0) for m in of_head], 0).astype(BF16)
        v_wide = jnp.concatenate([jnp.where(m, vb, 0.0) for m in of_head], 0).astype(BF16)
        scores = dot(qb, k_wide, 1, 1)
        scale = jnp.zeros((128, 256), F32)
        parts = []
        for h in range(heads):
            s = jnp.where(seen, scores[:, h * 128 : (h + 1) * 128], LOW)
            e = jnp.exp(s - jnp.max(s, -1, keepdims=True))
            scale = jnp.where(of_head[h], 1.0 / jnp.sum(e, -1, keepdims=True), scale)
            parts.append(e.astype(BF16))
        total = dot(jnp.concatenate(parts, 1), v_wide) * scale
        for j, at in enumerate(both):
            R.q0[at, :] = total[j * 64 : j * 64 + 64, 0:128]
            R.q1[at, :] = total[j * 64 : j * 64 + 64, 128:256]

    def attend(t):
        pair(2 * t)
        pair(2 * t + 1)

    first_part = 3 * group // 16
    loop(first_part, attend)
    table = [R.pos[...].astype(F32), R.count[...].astype(F32).reshape(1, group)]
    table = jnp.concatenate(table, 0)
    table = jnp.pad(table, ((0, 128 - table.shape[0]), (0, 128 - group)))
    R.plan[rows_at(dp, group), :] = table.T[0:group]
    gather_plan = GatherDp(R.plan, group)
    gather_plan.start()
    cap = R.cap[...]
    cap_factor = lax.rsqrt(jnp.sum(cap * cap, -1, keepdims=True) + 1e-06)
    R.own[...] = (cap * cap_factor).astype(BF16)
    gather_text = GatherDpHalf(R.text, plan.own, R.own)
    gather_text.start()
    gather_ctx.wait()
    gather_cg = GatherMp(lambda i: R.cg.at[i])
    gather_cg.start()
    loop(group // 4 - first_part, lambda t: attend(t + first_part))
    quarter = plan.quarter
    for i, index in enumerate((0, 2, 1, 3)):
        taken_rows = R.q0[index * quarter : (index + 1) * quarter, :]
        R.ca[mp, i * quarter : (i + 1) * quarter, :] = taken_rows.astype(BF16)
    R.cb[mp] = jnp.concatenate(
        [R.q1[0 : rows // 2, 0:64], R.q1[rows // 2 : rows, 0:64]], 1
    ).astype(BF16)

    class GatherSet:
        def __init__(self, i):
            wide, packed = pl.ds(2 * i * quarter, 2 * quarter), pl.ds(i * quarter, quarter)
            self.parts = (
                GatherMp(lambda m: R.ca.at[m, wide]),
                GatherMp(lambda m: R.cb.at[m, packed]),
            )

        def start(self):
            for part in self.parts:
                part.start()

        def forward(self):
            for part in self.parts:
                part.forward()

        def wait(self):
            for part in self.parts:
                part.wait()

    gather_sets = [GatherSet(i) for i in range(2)]
    gather_uk = GatherMp(lambda i: R.u.at[rows_at(i, hg)])
    gather_pc = GatherMp(lambda i: R.coef.at[rows_at(mps + i, hg)])
    gather_xc.relay()
    R.brow[...] = dot(R.plow[...], R.attn[...]).astype(BF16)
    uk = dot(qx, R.wt[local : 2 * local, :])
    R.u[rows_at(mp, hg), :] = uk.astype(BF16)
    fold = jnp.where(
        iota((rows, 128), 0) // group == iota((rows, 128), 1), 1.0, 0.0
    ).astype(BF16)
    late = rows_at(mps + mp, hg)
    R.coef[late, :] = dot(R.plow[...], fold).astype(BF16)
    gather_wo.forward()
    gather_cg.forward()
    for g in (gather_sets[0], gather_uk, gather_pc):
        g.start()
    gather_wo.wait()
    done(got_w1)
    done(got_w2)
    gather_xc.wait()
    gather_cg.wait()

    def class_forward(i):
        at = rows_at(i, plan.block)
        total = R.xc[at, :].astype(F32) + row(OUTB)
        joined = jnp.concatenate([R.cg[m, at, :].astype(F32) for m in range(mps)], 1)
        total += dot(joined.astype(BF16), R.wo[...])
        R.midc[at, :] = total
        mlp = norm_rows(total, row(G2), row(B2))[0].astype(BF16)
        put("mlp", i, mlp)
        pre = dot(mlp, R.w1[...]) + row(FC1B, plan.hidden)
        R.pre[at, :] = pre
        act = (pre * jax.nn.sigmoid(1.702 * pre)).astype(BF16)
        put("act", i, act)
        R.part1[at, :] = dot(act, R.w2[...]).astype(BF16)

    loop(plan.blocks, class_forward)
    sum1 = SumMp(R.part1, R.sums, 2, R.all1)
    sum1.start()

    size = plan.quarter

    def joined_context(index):
        side, which = lax.div(index, 2), lax.rem(index, 2)
        joined = []
        for m in range(mps):
            tail = R.cb[m, rows_at(which, size), :].astype(F32)
            tail = jnp.where(side == 0, tail[:, 0:64], tail[:, 64:128])
            joined += [R.ca[m, rows_at(2 * which + side, size), :].astype(F32), tail]
        return jnp.concatenate(joined, 1).astype(BF16)

    def bulk(i):
        at = [rows_at(index, size) for index in (others[i], owned[i])]
        total = jnp.concatenate([R.x[a, :].astype(F32) for a in at], 0) + row(OUTB)
        joined = [joined_context(index) for index in (others[i], owned[i])]
        total += dot(jnp.concatenate(joined, 0), R.wo[...])
        R.midq[i] = total[size : 2 * size]
        mlp = norm_rows(total, row(G2), row(B2))[0].astype(BF16)
        pre = dot(mlp, R.w1[...]) + row(FC1B, plan.hidden)
        act = (pre * jax.nn.sigmoid(1.702 * pre)).astype(BF16)
        part = dot(act, R.w2[...]).astype(BF16)
        R.part[at[0], :] = part[0:size]
        R.part[at[1], :] = part[size : 2 * size]

    others = [2 * (1 - low_bit) + i for i in range(2)]
    owned = [2 * low_bit + i for i in range(2)]
    def cut_rows(*counts):
        starts = [sum(counts[:n]) for n in range(len(counts))]
        return [pl.ds(a, c) for a, c in zip(starts, counts)]

    pieces = [cut_rows(96, size - 96), cut_rows(64, 96, size - 160)]

    def near_move(i):
        rows_other = R.part.at[rows_at(others[i], size)]
        return send(rows_other, R.half.at[pl.ds(i * size, size)], dp, near, own(), sem())

    def far_move(i, p):
        return send(R.chip.at[i, p], R.got.at[i, p], dp, far, own(), sem())

    to_near = [near_move(i) for i in range(2)]
    to_far = [[far_move(i, p) for p in pieces[i]] for i in range(2)]

    def chip_sum(i):
        to_near[i].wait_recv()
        mine = R.part[rows_at(owned[i], size), :].astype(F32)
        R.chip[i] = (mine + R.half[i * size : (i + 1) * size, :].astype(F32)).astype(BF16)

    def block_rows(index, p):
        return pl.ds(pl.multiple_of(index * size + p.start, 16), p.size)

    def near_block(i, p):
        at = R.blk.at[block_rows(owned[i], p)]
        return send(at, at, dp, near, own(), sem())

    blk_near = [[near_block(i, p) for p in pieces[i]] for i in range(2)]

    def store_rows(index, p):
        at = block_rows(index, p)
        ends.append(load(R.blk.at[at], R.block_out.at[at]))

    def finish(i):
        for n, p in enumerate(pieces[i]):
            to_far[i][n].wait_recv()
            total = R.chip[i, p, :].astype(F32) + R.got[i, p, :].astype(F32)
            total += R.midq[i, p, :] + row(FC2B)
            R.blk[block_rows(owned[i], p), :] = total.astype(BF16)
            blk_near[i][n].start()
            store_rows(owned[i], p)

    def class_queries(i):
        normed = norm_rows(R.xc[rows_at(i, plan.block), :].astype(F32), row(G1), row(B1))[0]
        normed = normed.astype(BF16)
        put("ac", i, normed)
        queries = dot(normed, R.wt[0:local, :], 1, 1) + row(QB, local)
        put("qa", i, queries.astype(BF16))

    loop(plan.blocks, class_queries)
    sum1.middle()
    done(got_wp)
    R.wpb[...] = wp[...].astype(BF16)
    gather_sets[0].forward()
    gather_text.relay()
    gather_sets[0].wait()
    started = len(ends)
    gather_sets[1].start()
    gather_b = GatherDp(R.b_out, hg, R.brow)
    gather_b.start()
    ends.append(load(R.brow, R.b_out.at[rows_at(dp, hg)]))
    bulk(0)
    sum1.turn()
    to_near[0].start()
    gather_plan.wait()
    gather_text.wait()
    sum1.wait()
    settle(started)

    done(sum1.first)
    scale = jnp.exp(row(SCALE, 1))
    crow = R.crow
    crow[0:1, :] = jnp.full((1, plan.captions), LOW, F32)

    def class_out(at):
        return R.midc[at, :] + R.all1[at, :].astype(F32) + row(FC2B)

    def logits_at(at):
        if plan.blocks == 1:
            return R.lg[...]
        return scale * dot(R.low[at, :], R.text[...], 1, 1)

    def head(i):
        at = rows_at(i, plan.block)
        post = norm_rows(class_out(at), row(PG), row(PB))[0]
        put("post", i, post.astype(BF16))
        emb = dot(post.astype(BF16), R.wpb[...])
        factor = lax.rsqrt(jnp.sum(emb * emb, -1, keepdims=True) + 1e-06)
        R.stat[at, 0:1] = factor
        unit = emb * factor
        R.unit[at, :] = unit
        image_low = unit.astype(BF16)
        R.low[at, :] = image_low
        logits = scale * dot(image_low, R.text[...], 1, 1)
        R.lg[...] = logits
        crow[0:1, :] = jnp.maximum(crow[0:1, :], jnp.max(logits, 0, keepdims=True))

    loop(plan.blocks, head)
    chip_sum(0)
    to_far[0][0].start()

    def matches(at):
        ids = iota((plan.block, plan.captions), 1).astype(F32)
        found = R.plan[at, 0:1] == ids
        for place in range(1, plan.places):
            found |= R.plan[at, place : place + 1] == ids
        return jnp.where(found, 1.0, 0.0)

    def put_small(i, value):
        R.small[i : i + 1, 0 : value.shape[1]] += value

    half_i, half_c = 0.5 / plan.images, 0.5 / plan.captions

    def stats(i):
        at = rows_at(i, plan.block)
        logits = logits_at(at)
        matched = matches(at) * logits
        crow[1:2, :] += jnp.sum(jnp.exp(logits - crow[0:1, :]), 0, keepdims=True)
        crow[2:3, :] += jnp.sum(matched, 0, keepdims=True)
        top = jnp.max(logits, 1, keepdims=True)
        lse = top + jnp.log(jnp.sum(jnp.exp(logits - top), 1, keepdims=True))
        R.stat[at, 1:2] = lse
        counts = R.plan[at, plan.places : plan.places + 1]
        terms = lse - jnp.sum(matched, 1, keepdims=True) / counts
        put_small(LOSS, half_i * jnp.sum(terms, 0, keepdims=True))

    loop(plan.blocks, stats)
    crow[3:4, :] = crow[0:1, :] + jnp.log(crow[1:2, :])
    put_small(LOSS, half_c * jnp.sum(crow[3:4, :] - crow[2:3, :], 1, keepdims=True))

    shape = (plan.captions, plan.own)
    own_captions = iota(shape, 0) == iota(shape, 1) + dp * plan.own
    own_captions = jnp.where(own_captions, 1.0, 0.0).astype(BF16)

    def head_back(i):
        at = rows_at(i, plan.block)
        logits = logits_at(at)
        match = matches(at)
        counts = R.plan[at, plan.places : plan.places + 1]
        dlog = half_i * (jnp.exp(logits - R.stat[at, 1:2]) - match / counts)
        dlog += half_c * (jnp.exp(logits - crow[3:4, :]) - match)
        dlow = dlog.astype(BF16)
        both = jnp.sum(dlow.astype(F32) * logits, 1, keepdims=True)
        R.small[LOSS : LOSS + 1, 128:129] += jnp.sum(both, 0, keepdims=True)
        dimage = scale * dot(dlow, R.text[...])
        own = dot(dlow, own_captions).astype(BF16)
        R.dtext[...] += dot(own, R.low[at, :], 0, 0)
        unit = R.unit[at, :]
        demb = R.stat[at, 0:1] * (dimage - unit * jnp.sum(unit * dimage, -1, keepdims=True))
        put("demb", i, demb.astype(BF16))
        dpost = dot(demb.astype(BF16), R.wpb[...], 1, 1)
        _, hat, spread = norm_rows(class_out(at), row(PG), row(PB))
        dcls = norm_back(dpost, row(PG), hat, spread)
        put_small(DPG, jnp.sum(dpost * hat, 0, keepdims=True))
        put_small(DPB, jnp.sum(dpost, 0, keepdims=True))
        put_small(DFC2B, jnp.sum(dcls, 0, keepdims=True))
        R.dmid[at, :] = dcls
        dy = dcls.astype(BF16)
        put("dy", i, dy)
        pre = R.pre[at, :]
        sigma = jax.nn.sigmoid(1.702 * pre)
        slope = sigma + 1.702 * pre * sigma * (1.0 - sigma)
        dpre = (dot(dy, R.w2[...], 1, 1) * slope).astype(BF16)
        put("dpre", i, dpre)
        put_small(DFC1B, jnp.sum(dpre.astype(F32), 0, keepdims=True))
        R.part1[at, :] = dot(dpre, R.w1[...], 1, 1).astype(BF16)

    loop(plan.blocks, head_back)
    sum2 = SumMp(R.part1, R.sums, 3, R.all2)
    sum2.start()
    gather_sets[1].forward()
    ends.append(sum2.first)
    dtext = scale * R.dtext[...]
    text_unit = cap * cap_factor
    R.capg[...] = cap_factor * (
        dtext - text_unit * jnp.sum(text_unit * dtext, -1, keepdims=True)
    )
    store("capg", "cap_out")

    sum2.middle()
    gather_uk.forward()
    gather_pc.forward()
    gather_sets[1].wait()
    bulk(1)
    to_far[0][1].start()
    sum2.turn()
    to_near[1].start()
    sum2.wait()

    def class_back(i):
        at = rows_at(i, plan.block)
        dmlp = R.all2[at, :].astype(F32)
        _, hat, spread = norm_rows(R.midc[at, :], row(G2), row(B2))
        dmid = R.dmid[at, :] + norm_back(dmlp, row(G2), hat, spread)
        put_small(DG2, jnp.sum(dmlp * hat, 0, keepdims=True))
        put_small(DB2, jnp.sum(dmlp, 0, keepdims=True))
        put_small(DOUTB, jnp.sum(dmid, 0, keepdims=True))
        R.dmid[at, :] = dmid
        dlow = dmid.astype(BF16)
        put("dmidl", i, dlow)
        R.dctx[at, :] = dot(dlow, R.wo[rows_at(mp, local), :], 1, 1).astype(BF16)

    loop(plan.blocks, class_back)
    store("dctx")

    dx = spread_heads(R.dctx[mine, :])
    probs = R.probs[...]
    dprobs = dot(dx, R.v[...], 1, 1)
    dscores = probs * (dprobs - jnp.sum(probs * dprobs, -1, keepdims=True))
    dscores = (dscores * 0.125).astype(BF16)
    R.arow[...] = dot(dscores, R.attn[...]).astype(BF16)
    gather_a = GatherDpTwice(R.a_out, hg, R.arow)
    gather_a.start()
    ends.append(load(R.arow, R.a_out.at[rows_at(dp, hg)]))
    dq = join_heads(dot(dscores, R.k[...])).astype(BF16)
    R.u[late, :] = dot(dx, R.wt[2 * local : 3 * local, :]).astype(BF16)
    gather_uv = GatherMp(lambda i: R.u.at[rows_at(mps + i, hg)])
    gather_uv.start()
    R.coef[rows_at(mp, hg), :] = dot(dscores, fold).astype(BF16)
    R.uq[rows_at(mp, group), :] = dot(dq, R.wt[0:local, :]).astype(BF16)
    gather_dc = GatherMp(lambda i: R.coef.at[rows_at(i, hg)])
    gather_uq = GatherMp(lambda i: R.uq.at[rows_at(i, group)])
    gather_dc.start()
    gather_uq.start()
    put_small(DQB, jnp.sum(dq.astype(F32), 0, keepdims=True))
    prob_sum = jnp.sum(R.plow[...].astype(F32), -1, keepdims=True)
    put_small(DVB, jnp.sum(dx.astype(F32) * prob_sum, 0, keepdims=True))
    gather_pc.wait()
    shape = (mps * hg, rows)
    fits = lax.rem(iota(shape, 0), group) == lax.rem(iota(shape, 1), group)

    def by_rows(first):
        coef = R.coef[first : first + mps * hg, :]
        wide = jnp.where(fits, dot(coef, fold, 1, 1), 0.0).astype(BF16)
        return dot(wide, R.hat[...])

    by_probs = by_rows(mps * hg)
    chip_sum(1)
    for move in to_far[1]:
        move.start()
    gather_uv.forward()
    gather_dc.forward()
    gather_uq.forward()
    for g in (gather_uk, gather_uv, gather_dc, gather_uq):
        g.wait()
    gather_a.forward(1)

    query = R.uq[0:group, :].astype(F32)
    for m in range(1, mps):
        query += R.uq[m * group : (m + 1) * group, :].astype(F32)
    factors = R.u[...].astype(F32)
    weight = jnp.sum(R.coef[...].astype(F32), -1, keepdims=True)
    summed = jnp.concatenate([by_rows(0), by_probs], 0)
    scaled = jnp.sum(factors * summed, 0, keepdims=True)
    scaled += jnp.sum(query * R.hat[0:group, :].astype(F32), 0, keepdims=True)
    shift = jnp.sum(factors * weight, 0, keepdims=True) + jnp.sum(query, 0, keepdims=True)
    put_small(DG1, scaled)
    put_small(DB1, shift)
    spans = []
    for i, count in ((DG1, width), (DB1, width), (DQB, local), (DVB, local)):
        spans += [(i, c, min(128, count - c)) for c in range(0, count, 128)]
    tile = []
    for i, c, size_c in spans:
        piece = R.small[i : i + 1, c : c + size_c]
        tile.append(jnp.pad(piece, ((0, 0), (0, 128 - size_c))))
    R.tot[rows_at(dp, 16), :] = jnp.concatenate(tile, 0).astype(BF16)
    gather_tot = GatherDp(R.tot, 16)
    gather_tot.start()

    def spread_coef(i):
        at = rows_at(i, 2 * size)
        pick = jnp.where(
            iota((2 * size, 128), 0) // group + i * (2 * size // group)
            == iota((2 * size, 128), 1),
            1.0,
            0.0,
        ).astype(BF16)
        wide = dot(pick, R.coef[...], 1, 1)
        shape = wide.shape
        fits = lax.rem(iota(shape, 0), group) == lax.rem(iota(shape, 1), group)
        R.mid[at, :] = dot(jnp.where(fits, wide, 0.0).astype(BF16), R.u[...])

    gather_a.forward(2)
    loop(2, spread_coef)
    R.mid[0:group, :] += query
    gather_a.forward(3)
    def first_back(i):
        at = rows_at(i, step)
        hat = R.hat[at, :].astype(F32)
        R.attn[at, :] = norm_back(R.mid[at, :], row(G1), hat, R.spread[at, :]).astype(BF16)

    for i in range(mps):
        loop(size // step, lambda t, i=i: first_back(t + i * (size // step)))
        at = pl.ds(i * size, size)
        if i == 0:
            top = R.attn[0:group, :].astype(F32) + R.dmid[mine, :]
            R.attn[0:group, :] = top.astype(BF16)
        ends.append(load(R.attn.at[at], R.images_out.at[at]))

    finish(0)
    finish(1)
    gather_tot.wait()

    R.sums_left[...] = jnp.zeros((16, 128), F32)

    def add_up(i):
        R.sums_left[...] += R.tot[rows_at(i, 16), :].astype(F32)

    loop(dps, add_up)
    for n, (i, c, size_c) in enumerate(spans):
        R.small[i : i + 1, c : c + size_c] = R.sums_left[n : n + 1, 0:size_c]
    store("small")
    ends.append(load(cg, R.ctx_out))
    gather_b.wait()
    for i in range(2):
        for n, p in enumerate(pieces[i]):
            blk_near[i][n].wait_recv()
            store_rows(others[i], p)
    gather_a.wait()
    ends.extend([*to_near, *to_far[0], *to_far[1], *blk_near[0], *blk_near[1]])
    settle(len(ends))


def run_kernel(plan, *operands):
    anywhere = pl.BlockSpec(memory_space=pl.ANY)
    return pl.pallas_call(
        functools.partial(kernel, plan),
        out_shape=[jax.ShapeDtypeStruct(s, t) for s, t in plan.results().values()],
        in_specs=[anywhere] * len(plan.operands()),
        out_specs=[anywhere] * len(plan.results()),
        scratch_shapes=[pltpu.VMEM(s, t) for s, t in plan.scratch().values()]
        + [pltpu.SemaphoreType.DMA((plan.semaphores(),))],
        compiler_params=pltpu.CompilerParams(
            collective_id=0, has_side_effects=True, vmem_limit_bytes=62 << 20
        ),
    )(*operands)


def final_operands(plan):
    names = ("images", "block", "cap", "small", "post", "demb", "act", "dy", "mlp", "dpre")
    names += ("ctx", "dmid", "a", "b", "dctx", "ac", "qa")
    return {n: plan.results()[n + "_out"] for n in names}


def final_results(plan):
    d, loc, hid = plan.width, plan.local, plan.hidden
    return dict(
        loss=((1,), F32),
        block=((plan.rows, d), BF16),
        images=((plan.rows, d), F32),
        g1=((d,), F32),
        b1=((d,), F32),
        wt=((3 * loc, d), F32),
        qvb=((2, loc), F32),
        wo=((loc, d), F32),
        ob=((d,), F32),
        g2=((d,), F32),
        b2=((d,), F32),
        w1=((d, hid), F32),
        f1b=((hid,), F32),
        w2=((hid, d), F32),
        f2b=((d,), F32),
        pg=((d,), F32),
        pb=((d,), F32),
        wp=((d, plan.emb), F32),
        cap=((plan.own, plan.emb), F32),
        ls=((1,), F32),
    )


STRAIGHT = ("block", "cap")


def final_kernel(plan, *refs):
    taken, given = final_operands(plan), final_results(plan)
    given_scratch = [n for n in given if n not in STRAIGHT]
    sems = refs[-1]
    I = Named(zip((*taken, "wt"), refs))
    refs = refs[len(taken) + 1 :]
    O = Named(zip(given, refs))
    rest = refs[len(given) :]
    L = Named(zip((*taken, "wk", "dq"), rest))
    S = Named(zip(given_scratch, rest[len(taken) + 2 :]))
    used, ends, free = iter(range(40)), [], []

    def copy(src, dst):
        place = free.pop() if free else next(used)
        move = pltpu.make_async_copy(src, dst, sems.at[place])
        move.start()

        def wait():
            move.wait()
            free.append(place)

        return wait

    late = ("images", "block", "cap", "small")
    order = ("act", "dy", "mlp", "dpre", *(n for n in taken if n not in late), *late)
    local = plan.local
    loads = {"wk": copy(I.wt.at[pl.ds(local, local)], L.wk)}
    loads |= {n: copy(I[n], L[n]) for n in dict.fromkeys(order)}

    def product(name, left, right, at=0, fix=None):
        for n in (left, right):
            if n in loads:
                loads.pop(n)()
        size = L[left].shape[1]
        step = 128 if size % 128 == 0 else size
        for c in range(0, size, step):
            a, b = L[left][:, c : c + step], L[right][...]
            rows = pl.ds(at + c, step)
            S[name][rows, :] = dot(fix(a) if fix else a, b, 0, 0)
            ends.append(copy(S[name].at[rows], O[name].at[rows]))

    group, heads = plan.group, plan.heads

    def spread_heads(t):
        pieces = []
        lane = iota((group, local), 1) // HEAD_DIM
        t = t.astype(F32)
        for i in range(plan.dps):
            for h in range(heads):
                pieces.append(jnp.where(lane == h, t[i * group : (i + 1) * group], 0.0))
        return jnp.concatenate(pieces, 0).astype(BF16)

    product("w2", "act", "dy")
    product("w1", "mlp", "dpre")
    product("wp", "post", "demb")
    loads.pop("images")()
    for i in range(plan.mps):
        rows = pl.ds(i * plan.quarter, plan.quarter)
        S.images[rows, :] = L.images[rows, :].astype(F32)
        ends.append(copy(S.images.at[rows], O.images.at[rows]))
    product("wo", "ctx", "dmid")
    loads.pop("block")()
    ends.append(copy(L.block, O.block))
    product("wt", "dctx", "b", 2 * local, spread_heads)
    product("wt", "qa", "a", local, spread_heads)
    loads.pop("wk")()
    wide = dot(L.a[...], L.wk[...], 1, 1)
    lane = iota((group, local), 1) // HEAD_DIM
    for i in range(plan.dps):
        total = jnp.zeros((group, local), F32)
        for h in range(heads):
            first = (i * heads + h) * group
            total += jnp.where(lane == h, wide[first : first + group], 0.0)
        L.dq[i * group : (i + 1) * group, :] = total.astype(BF16)
    product("wt", "dq", "ac")
    loads.pop("cap")()
    ends.append(copy(L.cap, O.cap))
    loads.pop("small")()
    small = L.small
    S.loss[...] = small[LOSS, 0:1]
    S.ls[...] = small[LOSS, 128:129]
    S.qvb[...] = small[DQB : DVB + 1, 0:local]
    vectors = dict(g1=DG1, b1=DB1, ob=DOUTB, g2=DG2, b2=DB2, f1b=DFC1B, f2b=DFC2B, pg=DPG, pb=DPB)
    for n, i in vectors.items():
        S[n][...] = small[i, 0 : S[n].shape[0]]
    for n in ("loss", "ls", "qvb", *vectors):
        ends.append(copy(S[n], O[n]))
    for end in ends:
        end()


def run_final(plan, got, wt):
    taken, given = final_operands(plan), final_results(plan)
    anywhere = pl.BlockSpec(memory_space=pl.ANY)
    scratch = [*taken.values(), ((plan.local, plan.width), BF16), ((plan.images, plan.local), BF16)]
    scratch += [st for n, st in given.items() if n not in STRAIGHT]
    out = pl.pallas_call(
        functools.partial(final_kernel, plan),
        out_shape=[jax.ShapeDtypeStruct(s, t) for s, t in given.values()],
        in_specs=[anywhere] * (len(taken) + 1),
        out_specs=[anywhere] * len(given),
        scratch_shapes=[pltpu.VMEM(s, t) for s, t in scratch]
        + [pltpu.SemaphoreType.DMA((40,))],
        compiler_params=pltpu.CompilerParams(vmem_limit_bytes=60 << 20),
    )(*(got[n + "_out"] for n in taken), wt)
    return dict(zip(given, out))


def body(
    images,
    ln1_gain,
    ln1_bias,
    w_qkv,
    qv_bias,
    w_out,
    out_bias,
    ln2_gain,
    ln2_bias,
    w_fc1,
    fc1_bias,
    w_fc2,
    fc2_bias,
    post_gain,
    post_bias,
    w_proj,
    captions,
    logit_scale,
    caption_counts,
    positives,
):
    sizes = (lax.axis_size("dp"), lax.axis_size("mp"))
    plan = Plan(sizes, images, w_qkv, w_fc1, w_proj, captions, positives)

    x = jnp.transpose(images, (1, 0, 2)).reshape(plan.rows, plan.width)
    wt = jnp.transpose(w_qkv, (1, 2, 0)).reshape(3 * plan.local, plan.width)

    got = run_kernel(
        plan,
        *(x, wt, w_out, w_fc1, w_fc2, w_proj, captions),
        jnp.transpose(positives),
        caption_counts,
        *(ln1_gain, ln1_bias, ln2_gain, ln2_bias, out_bias, fc2_bias),
        *(post_gain, post_bias, fc1_bias, qv_bias, logit_scale),
    )
    out = run_final(plan, dict(zip(plan.results(), got)), wt)

    def as_images(t):
        return jnp.transpose(t.reshape(plan.seq, plan.group, plan.width), (1, 0, 2))

    out["block"], out["images"] = as_images(out["block"]), as_images(out["images"])
    out["wt"] = jnp.transpose(out["wt"].reshape(3, plan.local, plan.width), (2, 0, 1))
    return tuple(out.values())


def solution(mesh):
    full, per_dp = P(), P("dp")
    return jax.shard_map(
        body,
        mesh=mesh,
        in_specs=(
            P("dp", None, None),
            full,
            full,
            P(None, None, "mp"),
            P(None, "mp"),
            P("mp", None),
            full,
            full,
            full,
            P(None, "mp"),
            P("mp"),
            P("mp", None),
            full,
            full,
            full,
            full,
            P("dp", None),
            full,
            per_dp,
            P("dp", None),
        ),
        out_specs=(
            full,
            P("dp", None, None),
            P("dp", None, None),
            full,
            full,
            P(None, None, "mp"),
            P(None, "mp"),
            P("mp", None),
            full,
            full,
            full,
            P(None, "mp"),
            P("mp"),
            P("mp", None),
            full,
            full,
            full,
            full,
            P("dp", None),
            full,
        ),
        check_vma=False,
    )
```

```python
import functools

import jax
import jax.numpy as jnp
from jax import lax
from jax.experimental import pallas as pl
from jax.experimental.pallas import tpu as pltpu
from jax.sharding import PartitionSpec as P

HEAD_DIM = 64
HIGH = lax.Precision.HIGHEST
F32 = jnp.float32
BF16 = jnp.bfloat16
MESH = pl.DeviceIdType.MESH
LOW = -1e30

G1, B1, G2, B2, OUTB, FC2B, PG, PB, FC1B, QB, VB, SCALE = range(12)
(LOSS, DG1, DB1, DQB, DVB, DOUTB, DG2, DB2, DFC1B, DFC2B, DPG, DPB) = range(12)


def norm_rows(values, gain, shift):
    centre = values - jnp.mean(values, -1, keepdims=True)
    spread = lax.rsqrt(jnp.mean(centre * centre, -1, keepdims=True) + 1e-05)
    scaled = centre * spread
    return (scaled * gain + shift, scaled, spread)


def norm_back(upper, gain, scaled, spread):
    inner = upper * gain
    return spread * (
        inner
        - jnp.mean(inner, -1, keepdims=True)
        - scaled * jnp.mean(inner * scaled, -1, keepdims=True)
    )


def dot(a, b, ca=1, cb=0, precision=None):
    return lax.dot_general(
        a, b, (((ca,), (cb,)), ((), ())), precision=precision, preferred_element_type=F32
    )


def iota(shape, dim):
    return lax.broadcasted_iota(jnp.int32, shape, dim)


def loop(count, step):
    if count == 1:
        step(0)
    else:
        lax.fori_loop(0, count, lambda i, c: (step(i), c)[1], 0)


def rows_at(index, size):
    if isinstance(index, int):
        return pl.ds(index * size, size)
    return pl.ds(pl.multiple_of(index * size, size), size)


class Named(dict):
    __getattr__ = dict.__getitem__


SEMS = 110


class Plan:
    def __init__(self, mesh_sizes, images, w_qkv, w_fc1, w_proj, captions, positives):
        self.dps, self.mps = mesh_sizes
        self.group, self.seq, self.width = images.shape
        self.rows = self.group * self.seq
        self.local = w_qkv.shape[2]
        self.heads = self.local // HEAD_DIM
        self.hg = self.heads * self.group
        self.hidden = w_fc1.shape[1]
        self.emb = w_proj.shape[1]
        self.images = self.group * self.dps
        self.own = captions.shape[0]
        self.captions = self.own * self.dps
        self.places = positives.shape[1]
        self.block = min(128, self.images)
        self.blocks = self.images // self.block
        self.part = self.images // self.mps
        self.quarter = self.rows // self.mps

    def semaphores(self):
        return SEMS + self.dps // 2 + (0 if self.blocks == 1 else 4)

    def operands(self):
        r, d, loc, hid = self.rows, self.width, self.local, self.hidden
        return dict(
            x_in=((r, d), BF16),
            wt_in=((3 * loc, d), BF16),
            wo_in=((loc, d), BF16),
            w1_in=((d, hid), BF16),
            w2_in=((hid, d), BF16),
            wp_in=((d, self.emb), F32),
            cap_in=((self.own, self.emb), F32),
            pos_in=((self.places, self.group), jnp.int32),
            count_in=((self.group,), jnp.int32),
            **{name + "_in": (s, t) for name, (s, t) in self.vectors().items()},
        )

    def vectors(self):
        d = self.width
        low = {name: ((d,), BF16) for name in ("g1", "b1", "g2", "b2", "ob", "f2b")}
        return dict(
            **low,
            pg=((d,), F32),
            pb=((d,), F32),
            f1b=((self.hidden,), BF16),
            qvb=((2, self.local), BF16),
            ls=((1,), F32),
        )

    def results(self):
        n, d, loc, hid = self.images, self.width, self.local, self.hidden
        return dict(
            block_out=((self.rows, d), BF16),
            images_out=((self.rows, d), BF16),
            small_out=((16, d), F32),
            cap_out=((self.own, self.emb), F32),
            post_out=((n, d), BF16),
            demb_out=((n, self.emb), BF16),
            act_out=((n, hid), BF16),
            dy_out=((n, d), BF16),
            mlp_out=((n, d), BF16),
            dpre_out=((n, hid), BF16),
            ctx_out=((n, loc), BF16),
            dmid_out=((n, d), BF16),
            a_out=((self.dps * self.hg, d), BF16),
            b_out=((self.dps * self.hg, d), BF16),
            dctx_out=((n, loc), BF16),
            ac_out=((n, d), BF16),
            qa_out=((n, loc), BF16),
        )

    def scratch(self):
        r, d, loc, hid = self.rows, self.width, self.local, self.hidden
        n, m, hg, b = self.images, self.mps, self.hg, self.block
        return dict(
            x=((r, d), BF16),
            vec=((16, d), F32),
            pos=((self.places, self.group), jnp.int32),
            count=((self.group,), jnp.int32),
            **self.vectors(),
            wt=((3 * loc, d), BF16),
            w1=((d, hid), BF16),
            w2=((hid, d), BF16),
            wpb=((d, self.emb), BF16),
            cap=((self.own, self.emb), F32),
            wo=((m * loc, d), BF16),
            attn=((r, d), BF16),
            hat=((r, d), BF16),
            spread=((r, 1), F32),
            q=((r, loc), BF16),
            k=((r, loc), BF16),
            v=((r, loc), BF16),
            q0=((64 * self.group, 128), F32),
            q1=((64 * self.group, 128), F32),
            k0=((64 * self.group, 128), F32),
            k1=((64 * self.group, 128), F32),
            v0=((64 * self.group, 128), F32),
            v1=((64 * self.group, 128), F32),
            probs=((hg, r), F32),
            plow=((hg, r), BF16),
            cx=((m, 2, 3 * self.quarter, 128), BF16),
            mid=((r, d), F32),
            midq=((2, r // m, d), F32),
            part=((r, d), BF16),
            half=((r // 2, d), BF16),
            chip=((2, r // m, d), BF16),
            got=((2, r // m, d), BF16),
            blk=((r, d), BF16),
            xc=((n, d), BF16),
            plan=((n, 128), F32),
            text=((self.captions, self.emb), BF16),
            own=((self.own, self.emb), BF16),
            cg=((m, n, loc), BF16),
            midc=((n, d), F32),
            mlp=((b, d), BF16),
            pre=((n, hid), F32),
            act=((b, hid), BF16),
            part1=((n, d), BF16),
            sums=((4, n // 2, d), BF16),
            all1=((n, d), BF16),
            all2=((n, d), BF16),
            post=((b, d), BF16),
            unit=((n, self.emb), F32),
            stat=((n, 2), F32),
            low=((n, self.emb), BF16),
            lg=((b, self.captions), F32),
            dtext=((self.own, self.emb), F32),
            arow=((hg, d), BF16),
            brow=((hg, d), BF16),
            crow=((8, self.captions), F32),
            demb=((b, self.emb), BF16),
            dy=((b, d), BF16),
            dpre=((b, hid), BF16),
            dmid=((n, d), F32),
            dmidl=((b, d), BF16),
            dctx=((n, loc), BF16),
            capg=((self.own, self.emb), F32),
            small=((16, d), F32),
            ac=((b, d), BF16),
            qa=((b, loc), BF16),
            u=((m * 2 * hg, d), BF16),
            uq=((m * self.group, d), BF16),
            coef=((m * 2 * hg, 128), BF16),
            tot=((self.dps * 16, 128), BF16),
            sums_left=((16, 128), F32),
        )


def kernel(plan, *refs):
    names = [*plan.operands(), *plan.results(), *plan.scratch()]
    sems = refs[len(names)]
    used = iter(range(plan.semaphores()))

    places, free, ends = {}, [], []

    def sem():
        return sems.at[next(used)]

    def own():
        place = free.pop() if free else next(used)
        ref = sems.at[place]
        places[id(ref)] = (place, ref)
        return ref

    def done(copy):
        if copy.is_remote:
            copy.wait_send()
        else:
            copy.wait()
        free.append(places[id(copy.src_sem if copy.is_remote else copy.dst_sem)][0])

    def settle(count):
        for copy in ends[:count]:
            done(copy)
        del ends[:count]

    R = Named(zip(names, refs))
    rows, width, local, heads = plan.rows, plan.width, plan.local, plan.heads
    group, hg, dps, mps = plan.group, plan.hg, plan.dps, plan.mps
    dp, mp = lax.axis_index("dp"), lax.axis_index("mp")
    low_bit, high_bit = lax.rem(mp, 2), lax.div(mp, 2)
    near = mp + 1 - 2 * low_bit
    far = lax.rem(mp + 2, 4)
    put_sem = {n: own() for n in ("mlp", "act", "post", "demb", "dy", "dpre", "dmidl", "ac", "qa")}

    def dp_peer(i):
        return lax.rem(dp + dps + (i + 2) // 2 * (1 - 2 * (i % 2)), dps)

    def load(src, dst):
        copy = pltpu.make_async_copy(src, dst, own())
        copy.start()
        return copy

    def store(name, dst=None):
        ends.append(load(R[name], R[dst or name + "_out"]))

    def put(name, i, value):
        R[name][...] = value
        copy = pltpu.make_async_copy(
            R[name], R[name.removesuffix("l") + "_out"].at[rows_at(i, plan.block)], put_sem[name]
        )
        copy.start()
        if plan.blocks == 1:
            ends.append(copy)
        else:
            copy.wait()

    def send(src, dst, dp_to, mp_to, out, into):
        return pltpu.make_async_remote_copy(
            src_ref=src,
            dst_ref=dst,
            send_sem=out,
            recv_sem=into,
            device_id=(dp_to, mp_to),
            device_id_type=MESH,
        )

    class GatherDp:
        def __init__(self, buf, size, source=None):
            self.buf, self.size, self.source = buf, size, source
            self.out, self.into = own(), sem()

        def start(self):
            mine = self.buf.at[rows_at(dp, self.size)]
            source = mine if self.source is None else self.source

            def one(i):
                send(source, mine, dp_peer(i), mp, self.out, self.into).start()

            loop(dps - 1, one)
            rest = self.buf.at[pl.ds(0, (dps - 1) * self.size)]
            self.all = send(rest, rest, dp, near, self.out, self.into)
            ends.append(self.all)

        def wait(self):
            self.all.wait_recv()

    class GatherDpHalf:
        def __init__(self, buf, size, source):
            self.size, self.source = size, source
            self.out, self.into = own(), sem()
            half = buf.shape[1] // 2
            self.cols = pl.ds(pl.multiple_of(low_bit * half, 128), half)
            self.buf = buf.at[:, self.cols]
            self.near = send(self.buf, self.buf, dp, near, own(), sem())

        def start(self):
            source = self.source.at[:, self.cols]
            mine = self.buf.at[rows_at(dp, self.size)]
            self.own = load(source, mine)

            def one(i):
                send(source, mine, dp_peer(i), mp, self.out, self.into).start()

            loop(dps - 1, one)
            rest = self.buf.at[pl.ds(0, (dps - 1) * self.size)]
            self.all = send(rest, rest, dp, near, self.out, self.into)
            ends.append(self.all)

        def relay(self):
            done(self.own)
            self.all.wait_recv()
            self.near.start()
            ends.append(self.near)

        def wait(self):
            self.near.wait_recv()

    class GatherDpTwice:
        def __init__(self, buf, size, source):
            self.buf, self.size, self.source = buf, size, source
            self.out, self.into = own(), sem()
            self.beside = dp + 1 - 2 * lax.rem(dp, 2)
            self.arrive = [sem() for _ in range(dps // 2 - 1)]
            self.left = list(range(dps // 2 - 1))

        def at(self, i):
            return self.buf.at[rows_at(i, self.size)]

        def start(self):
            send(self.source, self.at(dp), self.beside, mp, self.out, self.into).start()
            for i, into in enumerate(self.arrive):
                send(self.source, self.at(dp), self.pair(i), mp, self.out, into).start()

        def pair(self, i):
            other, bit = lax.rem(dp, 2), 1
            while bit < dps // 2:
                other += 2 * bit * lax.rem(lax.div(dp, 2 * bit) + (i + 1) // bit, 2)
                bit *= 2
            return other

        def forward(self, part):
            count = len(self.arrive)
            for i in range(count * (part - 1) // 3, count * part // 3):
                block = self.at(self.pair(i))
                send(block, block, self.beside, mp, self.out, self.arrive[i]).wait_recv()
                send(block, block, self.beside, mp, self.out, self.into).start()

        def wait(self):
            half = self.buf.at[pl.ds(0, dps // 2 * self.size)]
            rest = self.buf.at[pl.ds(0, (dps - 1) * self.size)]
            send(half, half, self.beside, mp, self.out, self.into).wait_recv()
            ends.append(send(rest, rest, self.beside, mp, self.out, self.into))

    class GatherMp:
        def __init__(self, slot):
            self.slot = slot
            self.to_near = send(slot(mp), slot(mp), dp, near, own(), sem())
            self.to_far = send(slot(mp), slot(mp), dp, far, own(), sem())
            self.pass_on = send(slot(far), slot(far), dp, near, own(), sem())

        def start(self):
            self.to_far.start()
            self.to_near.start()
            ends.extend([self.to_near, self.to_far])

        def forward(self):
            self.to_far.wait_recv()
            self.pass_on.start()
            ends.append(self.pass_on)

        def wait(self):
            self.to_near.wait_recv()
            self.pass_on.wait_recv()

    class SumMp:
        def __init__(self, part, slots, got, total):
            self.part, self.slots, self.got, self.total = part, slots, got, total
            count = part.shape[0] // 2
            self.mine, other = rows_at(low_bit, count), rows_at(1 - low_bit, count)
            half = self.total.at[self.mine]
            self.first = send(part.at[other], slots.at[0], dp, near, own(), sem())
            self.second = send(slots.at[1], slots.at[got], dp, far, own(), sem())
            self.third = send(half, half, dp, near, own(), sem())

        def start(self):
            self.first.start()

        def middle(self):
            self.first.wait_recv()
            mine = self.part[self.mine, :].astype(F32)
            self.slots[1] = (mine + self.slots[0].astype(F32)).astype(BF16)
            self.second.start()

        def turn(self):
            self.second.wait_recv()
            done(self.second)
            total = self.slots[1].astype(F32) + self.slots[self.got].astype(F32)
            self.total[self.mine, :] = total.astype(BF16)
            self.third.start()
            ends.append(self.third)

        def wait(self):
            self.third.wait_recv()

    barrier = pltpu.get_barrier_semaphore()

    def greet(i):
        pl.semaphore_signal(
            barrier, inc=1, device_id=(lax.rem(dp + 1 + i, dps), mp), device_id_type=MESH
        )

    loop(dps - 1, greet)
    for i in range(1, mps):
        pl.semaphore_signal(
            barrier, inc=1, device_id=(dp, lax.rem(mp + i, mps)), device_id_type=MESH
        )
    vec = R.vec
    vectors = ("g1", "b1", "g2", "b2", "ob", "f2b", "pg", "pb", "f1b")
    got_first = [load(R[n + "_in"], R[n]) for n in ("x", "g1", "b1")]
    got_wo = load(R.wo_in, R.wo.at[rows_at(mp, local)])
    got_wt = load(R.wt_in, R.wt)
    got_small = [
        load(R[n + "_in"], R[n]) for n in (*vectors[2:], "qvb", "ls", "pos", "count", "cap")
    ]
    got_w1 = load(R.w1_in, R.w1)
    got_w2 = load(R.w2_in, R.w2)
    wp = R.mid.at[pl.ds(0, width), pl.ds(0, plan.emb)]
    got_wp = load(R.wp_in, wp)
    for name in ("small", "crow", "dtext", "q1"):
        R[name][...] = jnp.zeros_like(R[name])
    for name in ("v0", "v1"):
        R[name][rows : 64 * group, :] = jnp.zeros((64 * group - rows, 128), F32)

    def place(i):
        name = vectors[i]
        vec[i : i + 1, 0 : R[name].shape[0]] = R[name][...].astype(F32).reshape(1, -1)

    for got in got_first:
        done(got)
    place(0)
    place(1)

    def row(i, size=width):
        return vec[i : i + 1, 0:size]

    step = rows // 4

    def first_norm(i):
        at = rows_at(i, rows // 2)
        normed, hat, spread = norm_rows(R.x[at, :].astype(F32), row(G1), row(B1))
        R.spread[at, :] = spread
        R.attn[at, :] = normed.astype(BF16)
        R.hat[at, :] = hat.astype(BF16)

    loop(2, first_norm)
    for got in got_small:
        done(got)
    for i in range(2, len(vectors)):
        place(i)
    vec[QB : VB + 1, 0:local] = R.qvb[...].astype(F32)
    vec[SCALE : SCALE + 1, 0:1] = R.ls[...].reshape(1, 1)
    pl.semaphore_wait(barrier, dps - 1 + mps - 1)
    done(got_wo)
    gather_wo = GatherMp(lambda i: R.wo.at[rows_at(i, local)])
    gather_wo.start()
    done(got_wt)

    def project(i):
        at = rows_at(i, rows // 2)
        a = R.attn[at, :]
        for j, (name, shift) in enumerate((("q", QB), ("k", None), ("v", VB))):
            t = dot(a, R.wt[j * local : (j + 1) * local, :], 1, 1)
            if shift is not None:
                t = t + row(shift, local)
            t = t.astype(BF16)
            R[name][at, :] = t
            t = t.astype(F32)
            R[name + "0"][at, :] = t[:, 0:128]
            R[name + "1"][at, 0 : local - 128] = t[:, 128:local]

    loop(2, project)

    lane_head = iota((hg, local), 1) // HEAD_DIM
    own_head = lane_head == iota((hg, local), 0) // group

    def spread_heads(t):
        wide = jnp.concatenate([t.astype(F32)] * heads, 0)
        return jnp.where(own_head, wide, 0.0).astype(BF16)

    def join_heads(t):
        t = jnp.where(own_head, t, 0.0)
        total = t[0:group]
        for h in range(1, heads):
            total = total + t[h * group : (h + 1) * group]
        return total

    same = lax.rem(iota((hg, rows), 0), group) == lax.rem(iota((hg, rows), 1), group)
    qx = spread_heads(R.q[0:group, :])
    scores = jnp.where(same, dot(qx, R.k[...], 1, 1) * 0.125, LOW)
    weights = jnp.exp(scores - jnp.max(scores, -1, keepdims=True))
    probs = weights * (1.0 / jnp.sum(weights, -1, keepdims=True))
    R.probs[...] = probs
    R.plow[...] = probs.astype(BF16)
    mine = rows_at(dp, group)
    ctx = join_heads(dot(R.plow[...], R.v[...])).astype(BF16)
    cg = R.cg.at[mp]
    cg[mine, :] = ctx
    gather_ctx = GatherDp(cg, group)
    gather_ctx.start()
    gather_xc = GatherDpHalf(R.xc, group, R.x.at[pl.ds(0, group)])
    gather_xc.start()
    head_of = iota((128, 256), 1) // HEAD_DIM
    seen = iota((128, 128), 0) // 64 == iota((128, 128), 1) // 64
    seen &= lax.rem(iota((128, 128), 1), 64) < plan.seq

    def pair(t):
        both = [pl.ds(2 * t + j, 64, stride=group) for j in range(2)]

        def taken(name):
            parts = [R[name + i] for i in "01"]
            return jnp.concatenate(
                [jnp.concatenate([ref[at, :] for at in both], 0) for ref in parts], 1
            )

        qb = (taken("q") * 0.125).astype(BF16)
        kb, vb = taken("k"), taken("v")
        of_head = [head_of == h for h in range(heads)]
        k_wide = jnp.concatenate([jnp.where(m, kb, 0.0) for m in of_head], 0).astype(BF16)
        v_wide = jnp.concatenate([jnp.where(m, vb, 0.0) for m in of_head], 0).astype(BF16)
        scores = dot(qb, k_wide, 1, 1)
        scale = jnp.zeros((128, 256), F32)
        parts = []
        for h in range(heads):
            s = jnp.where(seen, scores[:, h * 128 : (h + 1) * 128], LOW)
            e = jnp.exp(s - jnp.max(s, -1, keepdims=True))
            scale = jnp.where(of_head[h], 1.0 / jnp.sum(e, -1, keepdims=True), scale)
            parts.append(e.astype(BF16))
        total = dot(jnp.concatenate(parts, 1), v_wide) * scale
        for j, at in enumerate(both):
            R.q0[at, :] = total[j * 64 : j * 64 + 64, 0:128]
            R.q1[at, :] = total[j * 64 : j * 64 + 64, 128:256]

    def attend(t):
        pair(2 * t)
        pair(2 * t + 1)

    first_part = 3 * group // 16
    loop(first_part, attend)
    table = [R.pos[...].astype(F32), R.count[...].astype(F32).reshape(1, group)]
    table = jnp.concatenate(table, 0)
    table = jnp.pad(table, ((0, 128 - table.shape[0]), (0, 128 - group)))
    R.plan[rows_at(dp, group), :] = table.T[0:group]
    gather_plan = GatherDp(R.plan, group)
    gather_plan.start()
    cap = R.cap[...]
    cap_factor = lax.rsqrt(jnp.sum(cap * cap, -1, keepdims=True) + 1e-06)
    R.own[...] = (cap * cap_factor).astype(BF16)
    gather_text = GatherDpHalf(R.text, plan.own, R.own)
    gather_text.start()
    gather_ctx.wait()
    gather_cg = GatherMp(lambda i: R.cg.at[i])
    gather_cg.start()
    loop(group // 4 - first_part, lambda t: attend(t + first_part))
    quarter = plan.quarter
    for i in range(2):
        both = [slice((i + 2 * n) * quarter, (i + 2 * n + 1) * quarter) for n in range(2)]
        for n, at in enumerate(both):
            R.cx[mp, i, n * quarter : (n + 1) * quarter, :] = R.q0[at, :].astype(BF16)
        last = jnp.concatenate([R.q1[at, 0:64] for at in both], 1)
        R.cx[mp, i, 2 * quarter : 3 * quarter, :] = last.astype(BF16)
    gather_sets = [GatherMp(lambda m, i=i: R.cx.at[m, i]) for i in range(2)]
    gather_uk = GatherMp(lambda i: R.u.at[rows_at(i, hg)])
    gather_pc = GatherMp(lambda i: R.coef.at[rows_at(mps + i, hg)])
    gather_xc.relay()
    R.brow[...] = dot(R.plow[...], R.attn[...]).astype(BF16)
    uk = dot(qx, R.wt[local : 2 * local, :])
    R.u[rows_at(mp, hg), :] = uk.astype(BF16)
    fold = jnp.where(
        iota((rows, 128), 0) // group == iota((rows, 128), 1), 1.0, 0.0
    ).astype(BF16)
    late = rows_at(mps + mp, hg)
    R.coef[late, :] = dot(R.plow[...], fold).astype(BF16)
    gather_wo.forward()
    gather_cg.forward()
    for g in (gather_sets[0], gather_uk, gather_pc):
        g.start()
    gather_wo.wait()
    done(got_w1)
    done(got_w2)
    gather_xc.wait()
    gather_cg.wait()

    def class_forward(i):
        at = rows_at(i, plan.block)
        total = R.xc[at, :].astype(F32) + row(OUTB)
        joined = jnp.concatenate([R.cg[m, at, :].astype(F32) for m in range(mps)], 1)
        total += dot(joined.astype(BF16), R.wo[...])
        R.midc[at, :] = total
        mlp = norm_rows(total, row(G2), row(B2))[0].astype(BF16)
        put("mlp", i, mlp)
        pre = dot(mlp, R.w1[...]) + row(FC1B, plan.hidden)
        R.pre[at, :] = pre
        act = (pre * jax.nn.sigmoid(1.702 * pre)).astype(BF16)
        put("act", i, act)
        R.part1[at, :] = dot(act, R.w2[...]).astype(BF16)

    loop(plan.blocks, class_forward)
    sum1 = SumMp(R.part1, R.sums, 2, R.all1)
    sum1.start()

    size = plan.quarter

    def joined_context(index, i):
        side, joined = lax.div(index, 2), []
        for m in range(mps):
            tail = R.cx[m, i, 2 * size : 3 * size, :].astype(F32)
            tail = jnp.where(side == 0, tail[:, 0:64], tail[:, 64:128])
            joined += [R.cx[m, i, rows_at(side, size), :].astype(F32), tail]
        return jnp.concatenate(joined, 1).astype(BF16)

    def bulk(i):
        at = [rows_at(index, size) for index in (others[i], owned[i])]
        total = jnp.concatenate([R.x[a, :].astype(F32) for a in at], 0) + row(OUTB)
        joined = [joined_context(index, i) for index in (others[i], owned[i])]
        total += dot(jnp.concatenate(joined, 0), R.wo[...])
        R.midq[i] = total[size : 2 * size]
        mlp = norm_rows(total, row(G2), row(B2))[0].astype(BF16)
        pre = dot(mlp, R.w1[...]) + row(FC1B, plan.hidden)
        act = (pre * jax.nn.sigmoid(1.702 * pre)).astype(BF16)
        part = dot(act, R.w2[...]).astype(BF16)
        R.part[at[0], :] = part[0:size]
        R.part[at[1], :] = part[size : 2 * size]

    others = [2 * (1 - low_bit) + i for i in range(2)]
    owned = [2 * low_bit + i for i in range(2)]
    def cut_rows(*counts):
        starts = [sum(counts[:n]) for n in range(len(counts))]
        return [pl.ds(a, c) for a, c in zip(starts, counts)]

    pieces = [cut_rows(96, size - 96), cut_rows(64, 96, size - 160)]

    def near_move(i):
        rows_other = R.part.at[rows_at(others[i], size)]
        return send(rows_other, R.half.at[pl.ds(i * size, size)], dp, near, own(), sem())

    def far_move(i, p):
        return send(R.chip.at[i, p], R.got.at[i, p], dp, far, own(), sem())

    to_near = [near_move(i) for i in range(2)]
    to_far = [[far_move(i, p) for p in pieces[i]] for i in range(2)]

    def chip_sum(i):
        to_near[i].wait_recv()
        mine = R.part[rows_at(owned[i], size), :].astype(F32)
        R.chip[i] = (mine + R.half[i * size : (i + 1) * size, :].astype(F32)).astype(BF16)

    def block_rows(index, p):
        return pl.ds(pl.multiple_of(index * size + p.start, 16), p.size)

    def near_block(i, p):
        at = R.blk.at[block_rows(owned[i], p)]
        return send(at, at, dp, near, own(), sem())

    blk_near = [[near_block(i, p) for p in pieces[i]] for i in range(2)]

    def store_rows(index, p):
        at = block_rows(index, p)
        ends.append(load(R.blk.at[at], R.block_out.at[at]))

    def finish(i):
        for n, p in enumerate(pieces[i]):
            to_far[i][n].wait_recv()
            total = R.chip[i, p, :].astype(F32) + R.got[i, p, :].astype(F32)
            total += R.midq[i, p, :] + row(FC2B)
            R.blk[block_rows(owned[i], p), :] = total.astype(BF16)
            blk_near[i][n].start()
            store_rows(owned[i], p)

    def class_queries(i):
        normed = norm_rows(R.xc[rows_at(i, plan.block), :].astype(F32), row(G1), row(B1))[0]
        normed = normed.astype(BF16)
        put("ac", i, normed)
        queries = dot(normed, R.wt[0:local, :], 1, 1) + row(QB, local)
        put("qa", i, queries.astype(BF16))

    loop(plan.blocks, class_queries)
    sum1.middle()
    done(got_wp)
    R.wpb[...] = wp[...].astype(BF16)
    gather_sets[0].forward()
    gather_text.relay()
    gather_sets[0].wait()
    started = len(ends)
    gather_sets[1].start()
    gather_b = GatherDp(R.b_out, hg, R.brow)
    gather_b.start()
    ends.append(load(R.brow, R.b_out.at[rows_at(dp, hg)]))
    bulk(0)
    sum1.turn()
    to_near[0].start()
    gather_plan.wait()
    gather_text.wait()
    sum1.wait()
    settle(started)

    done(sum1.first)
    scale = jnp.exp(row(SCALE, 1))
    crow = R.crow
    crow[0:1, :] = jnp.full((1, plan.captions), LOW, F32)

    def class_out(at):
        return R.midc[at, :] + R.all1[at, :].astype(F32) + row(FC2B)

    def logits_at(at):
        if plan.blocks == 1:
            return R.lg[...]
        return scale * dot(R.low[at, :], R.text[...], 1, 1)

    def head(i):
        at = rows_at(i, plan.block)
        post = norm_rows(class_out(at), row(PG), row(PB))[0]
        put("post", i, post.astype(BF16))
        emb = dot(post.astype(BF16), R.wpb[...])
        factor = lax.rsqrt(jnp.sum(emb * emb, -1, keepdims=True) + 1e-06)
        R.stat[at, 0:1] = factor
        unit = emb * factor
        R.unit[at, :] = unit
        image_low = unit.astype(BF16)
        R.low[at, :] = image_low
        logits = scale * dot(image_low, R.text[...], 1, 1)
        R.lg[...] = logits
        crow[0:1, :] = jnp.maximum(crow[0:1, :], jnp.max(logits, 0, keepdims=True))

    loop(plan.blocks, head)
    chip_sum(0)
    to_far[0][0].start()

    def matches(at):
        ids = iota((plan.block, plan.captions), 1).astype(F32)
        found = R.plan[at, 0:1] == ids
        for place in range(1, plan.places):
            found |= R.plan[at, place : place + 1] == ids
        return jnp.where(found, 1.0, 0.0)

    def put_small(i, value):
        R.small[i : i + 1, 0 : value.shape[1]] += value

    half_i, half_c = 0.5 / plan.images, 0.5 / plan.captions

    def stats(i):
        at = rows_at(i, plan.block)
        logits = logits_at(at)
        matched = matches(at) * logits
        crow[1:2, :] += jnp.sum(jnp.exp(logits - crow[0:1, :]), 0, keepdims=True)
        crow[2:3, :] += jnp.sum(matched, 0, keepdims=True)
        top = jnp.max(logits, 1, keepdims=True)
        lse = top + jnp.log(jnp.sum(jnp.exp(logits - top), 1, keepdims=True))
        R.stat[at, 1:2] = lse
        counts = R.plan[at, plan.places : plan.places + 1]
        terms = lse - jnp.sum(matched, 1, keepdims=True) / counts
        put_small(LOSS, half_i * jnp.sum(terms, 0, keepdims=True))

    loop(plan.blocks, stats)
    crow[3:4, :] = crow[0:1, :] + jnp.log(crow[1:2, :])
    put_small(LOSS, half_c * jnp.sum(crow[3:4, :] - crow[2:3, :], 1, keepdims=True))

    shape = (plan.captions, plan.own)
    own_captions = iota(shape, 0) == iota(shape, 1) + dp * plan.own
    own_captions = jnp.where(own_captions, 1.0, 0.0).astype(BF16)

    def head_back(i):
        at = rows_at(i, plan.block)
        logits = logits_at(at)
        match = matches(at)
        counts = R.plan[at, plan.places : plan.places + 1]
        dlog = half_i * (jnp.exp(logits - R.stat[at, 1:2]) - match / counts)
        dlog += half_c * (jnp.exp(logits - crow[3:4, :]) - match)
        dlow = dlog.astype(BF16)
        both = jnp.sum(dlow.astype(F32) * logits, 1, keepdims=True)
        R.small[LOSS : LOSS + 1, 128:129] += jnp.sum(both, 0, keepdims=True)
        dimage = scale * dot(dlow, R.text[...])
        own = dot(dlow, own_captions).astype(BF16)
        R.dtext[...] += dot(own, R.low[at, :], 0, 0)
        unit = R.unit[at, :]
        demb = R.stat[at, 0:1] * (dimage - unit * jnp.sum(unit * dimage, -1, keepdims=True))
        put("demb", i, demb.astype(BF16))
        dpost = dot(demb.astype(BF16), R.wpb[...], 1, 1)
        _, hat, spread = norm_rows(class_out(at), row(PG), row(PB))
        dcls = norm_back(dpost, row(PG), hat, spread)
        put_small(DPG, jnp.sum(dpost * hat, 0, keepdims=True))
        put_small(DPB, jnp.sum(dpost, 0, keepdims=True))
        put_small(DFC2B, jnp.sum(dcls, 0, keepdims=True))
        R.dmid[at, :] = dcls
        dy = dcls.astype(BF16)
        put("dy", i, dy)
        pre = R.pre[at, :]
        sigma = jax.nn.sigmoid(1.702 * pre)
        slope = sigma + 1.702 * pre * sigma * (1.0 - sigma)
        dpre = (dot(dy, R.w2[...], 1, 1) * slope).astype(BF16)
        put("dpre", i, dpre)
        put_small(DFC1B, jnp.sum(dpre.astype(F32), 0, keepdims=True))
        R.part1[at, :] = dot(dpre, R.w1[...], 1, 1).astype(BF16)

    loop(plan.blocks, head_back)
    sum2 = SumMp(R.part1, R.sums, 3, R.all2)
    sum2.start()
    gather_sets[1].forward()
    ends.append(sum2.first)
    dtext = scale * R.dtext[...]
    text_unit = cap * cap_factor
    R.capg[...] = cap_factor * (
        dtext - text_unit * jnp.sum(text_unit * dtext, -1, keepdims=True)
    )
    store("capg", "cap_out")

    sum2.middle()
    gather_uk.forward()
    gather_pc.forward()
    gather_sets[1].wait()
    bulk(1)
    to_far[0][1].start()
    sum2.turn()
    to_near[1].start()
    sum2.wait()

    def class_back(i):
        at = rows_at(i, plan.block)
        dmlp = R.all2[at, :].astype(F32)
        _, hat, spread = norm_rows(R.midc[at, :], row(G2), row(B2))
        dmid = R.dmid[at, :] + norm_back(dmlp, row(G2), hat, spread)
        put_small(DG2, jnp.sum(dmlp * hat, 0, keepdims=True))
        put_small(DB2, jnp.sum(dmlp, 0, keepdims=True))
        put_small(DOUTB, jnp.sum(dmid, 0, keepdims=True))
        R.dmid[at, :] = dmid
        dlow = dmid.astype(BF16)
        put("dmidl", i, dlow)
        R.dctx[at, :] = dot(dlow, R.wo[rows_at(mp, local), :], 1, 1).astype(BF16)

    loop(plan.blocks, class_back)
    store("dctx")

    dx = spread_heads(R.dctx[mine, :])
    probs = R.probs[...]
    dprobs = dot(dx, R.v[...], 1, 1)
    dscores = probs * (dprobs - jnp.sum(probs * dprobs, -1, keepdims=True))
    dscores = (dscores * 0.125).astype(BF16)
    R.arow[...] = dot(dscores, R.attn[...]).astype(BF16)
    gather_a = GatherDpTwice(R.a_out, hg, R.arow)
    gather_a.start()
    ends.append(load(R.arow, R.a_out.at[rows_at(dp, hg)]))
    dq = join_heads(dot(dscores, R.k[...])).astype(BF16)
    R.u[late, :] = dot(dx, R.wt[2 * local : 3 * local, :]).astype(BF16)
    gather_uv = GatherMp(lambda i: R.u.at[rows_at(mps + i, hg)])
    gather_uv.start()
    R.coef[rows_at(mp, hg), :] = dot(dscores, fold).astype(BF16)
    R.uq[rows_at(mp, group), :] = dot(dq, R.wt[0:local, :]).astype(BF16)
    gather_dc = GatherMp(lambda i: R.coef.at[rows_at(i, hg)])
    gather_uq = GatherMp(lambda i: R.uq.at[rows_at(i, group)])
    gather_dc.start()
    gather_uq.start()
    put_small(DQB, jnp.sum(dq.astype(F32), 0, keepdims=True))
    prob_sum = jnp.sum(R.plow[...].astype(F32), -1, keepdims=True)
    put_small(DVB, jnp.sum(dx.astype(F32) * prob_sum, 0, keepdims=True))
    gather_pc.wait()
    shape = (mps * hg, rows)
    fits = lax.rem(iota(shape, 0), group) == lax.rem(iota(shape, 1), group)

    def by_rows(first):
        coef = R.coef[first : first + mps * hg, :]
        wide = jnp.where(fits, dot(coef, fold, 1, 1), 0.0).astype(BF16)
        return dot(wide, R.hat[...])

    by_probs = by_rows(mps * hg)
    chip_sum(1)
    for move in to_far[1]:
        move.start()
    gather_uv.forward()
    gather_dc.forward()
    gather_uq.forward()
    for g in (gather_uk, gather_uv, gather_dc, gather_uq):
        g.wait()
    gather_a.forward(1)

    query = R.uq[0:group, :].astype(F32)
    for m in range(1, mps):
        query += R.uq[m * group : (m + 1) * group, :].astype(F32)
    factors = R.u[...].astype(F32)
    weight = jnp.sum(R.coef[...].astype(F32), -1, keepdims=True)
    summed = jnp.concatenate([by_rows(0), by_probs], 0)
    scaled = jnp.sum(factors * summed, 0, keepdims=True)
    scaled += jnp.sum(query * R.hat[0:group, :].astype(F32), 0, keepdims=True)
    shift = jnp.sum(factors * weight, 0, keepdims=True) + jnp.sum(query, 0, keepdims=True)
    put_small(DG1, scaled)
    put_small(DB1, shift)
    spans = []
    for i, count in ((DG1, width), (DB1, width), (DQB, local), (DVB, local)):
        spans += [(i, c, min(128, count - c)) for c in range(0, count, 128)]
    tile = []
    for i, c, size_c in spans:
        piece = R.small[i : i + 1, c : c + size_c]
        tile.append(jnp.pad(piece, ((0, 0), (0, 128 - size_c))))
    R.tot[rows_at(dp, 16), :] = jnp.concatenate(tile, 0).astype(BF16)
    gather_tot = GatherDp(R.tot, 16)
    gather_tot.start()

    def spread_coef(i):
        at = rows_at(i, 2 * size)
        pick = jnp.where(
            iota((2 * size, 128), 0) // group + i * (2 * size // group)
            == iota((2 * size, 128), 1),
            1.0,
            0.0,
        ).astype(BF16)
        wide = dot(pick, R.coef[...], 1, 1)
        shape = wide.shape
        fits = lax.rem(iota(shape, 0), group) == lax.rem(iota(shape, 1), group)
        R.mid[at, :] = dot(jnp.where(fits, wide, 0.0).astype(BF16), R.u[...])

    gather_a.forward(2)
    loop(2, spread_coef)
    R.mid[0:group, :] += query
    gather_a.forward(3)
    def first_back(i):
        at = rows_at(i, step)
        hat = R.hat[at, :].astype(F32)
        R.attn[at, :] = norm_back(R.mid[at, :], row(G1), hat, R.spread[at, :]).astype(BF16)

    for i in range(mps):
        loop(size // step, lambda t, i=i: first_back(t + i * (size // step)))
        at = pl.ds(i * size, size)
        if i == 0:
            top = R.attn[0:group, :].astype(F32) + R.dmid[mine, :]
            R.attn[0:group, :] = top.astype(BF16)
        ends.append(load(R.attn.at[at], R.images_out.at[at]))

    finish(0)
    finish(1)
    gather_tot.wait()

    R.sums_left[...] = jnp.zeros((16, 128), F32)

    def add_up(i):
        R.sums_left[...] += R.tot[rows_at(i, 16), :].astype(F32)

    loop(dps, add_up)
    for n, (i, c, size_c) in enumerate(spans):
        R.small[i : i + 1, c : c + size_c] = R.sums_left[n : n + 1, 0:size_c]
    store("small")
    ends.append(load(cg, R.ctx_out))
    gather_b.wait()
    for i in range(2):
        for n, p in enumerate(pieces[i]):
            blk_near[i][n].wait_recv()
            store_rows(others[i], p)
    gather_a.wait()
    ends.extend([*to_near, *to_far[0], *to_far[1], *blk_near[0], *blk_near[1]])
    settle(len(ends))


def run_kernel(plan, *operands):
    anywhere = pl.BlockSpec(memory_space=pl.ANY)
    return pl.pallas_call(
        functools.partial(kernel, plan),
        out_shape=[jax.ShapeDtypeStruct(s, t) for s, t in plan.results().values()],
        in_specs=[anywhere] * len(plan.operands()),
        out_specs=[anywhere] * len(plan.results()),
        scratch_shapes=[pltpu.VMEM(s, t) for s, t in plan.scratch().values()]
        + [pltpu.SemaphoreType.DMA((plan.semaphores(),))],
        compiler_params=pltpu.CompilerParams(
            collective_id=0, has_side_effects=True, vmem_limit_bytes=62 << 20
        ),
    )(*operands)


def final_operands(plan):
    names = ("images", "block", "cap", "small", "post", "demb", "act", "dy", "mlp", "dpre")
    names += ("ctx", "dmid", "a", "b", "dctx", "ac", "qa")
    return {n: plan.results()[n + "_out"] for n in names}


def final_results(plan):
    d, loc, hid = plan.width, plan.local, plan.hidden
    return dict(
        loss=((1,), F32),
        block=((plan.rows, d), BF16),
        images=((plan.rows, d), F32),
        g1=((d,), F32),
        b1=((d,), F32),
        wt=((3 * loc, d), F32),
        qvb=((2, loc), F32),
        wo=((loc, d), F32),
        ob=((d,), F32),
        g2=((d,), F32),
        b2=((d,), F32),
        w1=((d, hid), F32),
        f1b=((hid,), F32),
        w2=((hid, d), F32),
        f2b=((d,), F32),
        pg=((d,), F32),
        pb=((d,), F32),
        wp=((d, plan.emb), F32),
        cap=((plan.own, plan.emb), F32),
        ls=((1,), F32),
    )


STRAIGHT = ("block", "cap")


def final_kernel(plan, *refs):
    taken, given = final_operands(plan), final_results(plan)
    given_scratch = [n for n in given if n not in STRAIGHT]
    sems = refs[-1]
    I = Named(zip((*taken, "wt"), refs))
    refs = refs[len(taken) + 1 :]
    O = Named(zip(given, refs))
    rest = refs[len(given) :]
    L = Named(zip((*taken, "wk", "dq"), rest))
    S = Named(zip(given_scratch, rest[len(taken) + 2 :]))
    used, ends, free = iter(range(40)), [], []

    def copy(src, dst):
        place = free.pop() if free else next(used)
        move = pltpu.make_async_copy(src, dst, sems.at[place])
        move.start()

        def wait():
            move.wait()
            free.append(place)

        return wait

    late = ("images", "block", "cap", "small")
    order = ("act", "dy", "mlp", "dpre", *(n for n in taken if n not in late), *late)
    local = plan.local
    loads = {n: copy(I[n], L[n]) for n in dict.fromkeys(order)}
    loads["wk"] = copy(I.wt.at[pl.ds(local, local)], L.wk)

    def product(name, left, right, at=0, fix=None):
        for n in (left, right):
            if n in loads:
                loads.pop(n)()
        size = L[left].shape[1]
        step = 128 if size % 128 == 0 else size
        for c in range(0, size, step):
            a, b = L[left][:, c : c + step], L[right][...]
            rows = pl.ds(at + c, step)
            S[name][rows, :] = dot(fix(a) if fix else a, b, 0, 0)
            ends.append(copy(S[name].at[rows], O[name].at[rows]))

    group, heads = plan.group, plan.heads

    def spread_heads(t):
        pieces = []
        lane = iota((group, local), 1) // HEAD_DIM
        t = t.astype(F32)
        for i in range(plan.dps):
            for h in range(heads):
                pieces.append(jnp.where(lane == h, t[i * group : (i + 1) * group], 0.0))
        return jnp.concatenate(pieces, 0).astype(BF16)

    product("w2", "act", "dy")
    product("w1", "mlp", "dpre")
    product("wp", "post", "demb")
    loads.pop("images")()
    for i in range(plan.mps):
        rows = pl.ds(i * plan.quarter, plan.quarter)
        S.images[rows, :] = L.images[rows, :].astype(F32)
        ends.append(copy(S.images.at[rows], O.images.at[rows]))
    product("wo", "ctx", "dmid")
    loads.pop("block")()
    ends.append(copy(L.block, O.block))
    product("wt", "dctx", "b", 2 * local, spread_heads)
    product("wt", "qa", "a", local, spread_heads)
    loads.pop("wk")()
    wide = dot(L.a[...], L.wk[...], 1, 1)
    lane = iota((group, local), 1) // HEAD_DIM
    for i in range(plan.dps):
        total = jnp.zeros((group, local), F32)
        for h in range(heads):
            first = (i * heads + h) * group
            total += jnp.where(lane == h, wide[first : first + group], 0.0)
        L.dq[i * group : (i + 1) * group, :] = total.astype(BF16)
    product("wt", "dq", "ac")
    loads.pop("cap")()
    ends.append(copy(L.cap, O.cap))
    loads.pop("small")()
    small = L.small
    S.loss[...] = small[LOSS, 0:1]
    S.ls[...] = small[LOSS, 128:129]
    S.qvb[...] = small[DQB : DVB + 1, 0:local]
    vectors = dict(g1=DG1, b1=DB1, ob=DOUTB, g2=DG2, b2=DB2, f1b=DFC1B, f2b=DFC2B, pg=DPG, pb=DPB)
    for n, i in vectors.items():
        S[n][...] = small[i, 0 : S[n].shape[0]]
    for n in ("loss", "ls", "qvb", *vectors):
        ends.append(copy(S[n], O[n]))
    for end in ends:
        end()


def run_final(plan, got, wt):
    taken, given = final_operands(plan), final_results(plan)
    anywhere = pl.BlockSpec(memory_space=pl.ANY)
    scratch = [*taken.values(), ((plan.local, plan.width), BF16), ((plan.images, plan.local), BF16)]
    scratch += [st for n, st in given.items() if n not in STRAIGHT]
    out = pl.pallas_call(
        functools.partial(final_kernel, plan),
        out_shape=[jax.ShapeDtypeStruct(s, t) for s, t in given.values()],
        in_specs=[anywhere] * (len(taken) + 1),
        out_specs=[anywhere] * len(given),
        scratch_shapes=[pltpu.VMEM(s, t) for s, t in scratch]
        + [pltpu.SemaphoreType.DMA((40,))],
        compiler_params=pltpu.CompilerParams(vmem_limit_bytes=60 << 20),
    )(*(got[n + "_out"] for n in taken), wt)
    return dict(zip(given, out))


def body(
    images,
    ln1_gain,
    ln1_bias,
    w_qkv,
    qv_bias,
    w_out,
    out_bias,
    ln2_gain,
    ln2_bias,
    w_fc1,
    fc1_bias,
    w_fc2,
    fc2_bias,
    post_gain,
    post_bias,
    w_proj,
    captions,
    logit_scale,
    caption_counts,
    positives,
):
    sizes = (lax.axis_size("dp"), lax.axis_size("mp"))
    plan = Plan(sizes, images, w_qkv, w_fc1, w_proj, captions, positives)

    x = jnp.transpose(images, (1, 0, 2)).reshape(plan.rows, plan.width)
    wt = jnp.transpose(w_qkv, (1, 2, 0)).reshape(3 * plan.local, plan.width)

    got = run_kernel(
        plan,
        *(x, wt, w_out, w_fc1, w_fc2, w_proj, captions),
        jnp.transpose(positives),
        caption_counts,
        *(ln1_gain, ln1_bias, ln2_gain, ln2_bias, out_bias, fc2_bias),
        *(post_gain, post_bias, fc1_bias, qv_bias, logit_scale),
    )
    out = run_final(plan, dict(zip(plan.results(), got)), wt)

    def as_images(t):
        return jnp.transpose(t.reshape(plan.seq, plan.group, plan.width), (1, 0, 2))

    out["block"], out["images"] = as_images(out["block"]), as_images(out["images"])
    out["wt"] = jnp.transpose(out["wt"].reshape(3, plan.local, plan.width), (2, 0, 1))
    return tuple(out.values())


def solution(mesh):
    full, per_dp = P(), P("dp")
    return jax.shard_map(
        body,
        mesh=mesh,
        in_specs=(
            P("dp", None, None),
            full,
            full,
            P(None, None, "mp"),
            P(None, "mp"),
            P("mp", None),
            full,
            full,
            full,
            P(None, "mp"),
            P("mp"),
            P("mp", None),
            full,
            full,
            full,
            full,
            P("dp", None),
            full,
            per_dp,
            P("dp", None),
        ),
        out_specs=(
            full,
            P("dp", None, None),
            P("dp", None, None),
            full,
            full,
            P(None, None, "mp"),
            P(None, "mp"),
            P("mp", None),
            full,
            full,
            full,
            P(None, "mp"),
            P("mp"),
            P("mp", None),
            full,
            full,
            full,
            full,
            P("dp", None),
            full,
        ),
        check_vma=False,
    )
```

```python
import functools

import jax
import jax.numpy as jnp
from jax import lax
from jax.experimental import pallas as pl
from jax.experimental.pallas import tpu as pltpu
from jax.sharding import PartitionSpec as P

HEAD_DIM = 64
HIGH = lax.Precision.HIGHEST
F32 = jnp.float32
BF16 = jnp.bfloat16
MESH = pl.DeviceIdType.MESH
LOW = -1e30

G1, B1, G2, B2, OUTB, FC2B, PG, PB, FC1B, QB, VB, SCALE = range(12)
(LOSS, DG1, DB1, DQB, DVB, DOUTB, DG2, DB2, DFC1B, DFC2B, DPG, DPB) = range(12)


def norm_rows(values, gain, shift):
    centre = values - jnp.mean(values, -1, keepdims=True)
    spread = lax.rsqrt(jnp.mean(centre * centre, -1, keepdims=True) + 1e-05)
    scaled = centre * spread
    return (scaled * gain + shift, scaled, spread)


def norm_back(upper, gain, scaled, spread):
    inner = upper * gain
    return spread * (
        inner
        - jnp.mean(inner, -1, keepdims=True)
        - scaled * jnp.mean(inner * scaled, -1, keepdims=True)
    )


def dot(a, b, ca=1, cb=0, precision=None):
    return lax.dot_general(
        a, b, (((ca,), (cb,)), ((), ())), precision=precision, preferred_element_type=F32
    )


def iota(shape, dim):
    return lax.broadcasted_iota(jnp.int32, shape, dim)


def loop(count, step):
    if count == 1:
        step(0)
    else:
        lax.fori_loop(0, count, lambda i, c: (step(i), c)[1], 0)


def rows_at(index, size):
    if isinstance(index, int):
        return pl.ds(index * size, size)
    return pl.ds(pl.multiple_of(index * size, size), size)


class Named(dict):
    __getattr__ = dict.__getitem__


SEMS = 110


class Plan:
    def __init__(self, mesh_sizes, images, w_qkv, w_fc1, w_proj, captions, positives):
        self.dps, self.mps = mesh_sizes
        self.group, self.seq, self.width = images.shape
        self.rows = self.group * self.seq
        self.local = w_qkv.shape[2]
        self.heads = self.local // HEAD_DIM
        self.hg = self.heads * self.group
        self.hidden = w_fc1.shape[1]
        self.emb = w_proj.shape[1]
        self.images = self.group * self.dps
        self.own = captions.shape[0]
        self.captions = self.own * self.dps
        self.places = positives.shape[1]
        self.block = min(128, self.images)
        self.blocks = self.images // self.block
        self.part = self.images // self.mps
        self.quarter = self.rows // self.mps

    def semaphores(self):
        return SEMS + self.dps // 2 + (0 if self.blocks == 1 else 4)

    def operands(self):
        r, d, loc, hid = self.rows, self.width, self.local, self.hidden
        return dict(
            x_in=((r, d), BF16),
            wt_in=((3 * loc, d), BF16),
            wo_in=((loc, d), BF16),
            w1_in=((d, hid), BF16),
            w2_in=((hid, d), BF16),
            wp_in=((d, self.emb), F32),
            cap_in=((self.own, self.emb), F32),
            pos_in=((self.places, self.group), jnp.int32),
            count_in=((self.group,), jnp.int32),
            **{name + "_in": (s, t) for name, (s, t) in self.vectors().items()},
        )

    def vectors(self):
        d = self.width
        low = {name: ((d,), BF16) for name in ("g1", "b1", "g2", "b2", "ob", "f2b")}
        return dict(
            **low,
            pg=((d,), F32),
            pb=((d,), F32),
            f1b=((self.hidden,), BF16),
            qvb=((2, self.local), BF16),
            ls=((1,), F32),
        )

    def results(self):
        n, d, loc, hid = self.images, self.width, self.local, self.hidden
        return dict(
            block_out=((self.rows, d), BF16),
            images_out=((self.rows, d), BF16),
            small_out=((16, d), F32),
            cap_out=((self.own, self.emb), F32),
            post_out=((n, d), BF16),
            demb_out=((n, self.emb), BF16),
            act_out=((n, hid), BF16),
            dy_out=((n, d), BF16),
            mlp_out=((n, d), BF16),
            dpre_out=((n, hid), BF16),
            ctx_out=((n, loc), BF16),
            dmid_out=((n, d), BF16),
            a_out=((self.dps * self.hg, d), BF16),
            b_out=((self.dps * self.hg, d), BF16),
            dctx_out=((n, loc), BF16),
            ac_out=((n, d), BF16),
            qa_out=((n, loc), BF16),
        )

    def scratch(self):
        r, d, loc, hid = self.rows, self.width, self.local, self.hidden
        n, m, hg, b = self.images, self.mps, self.hg, self.block
        return dict(
            x=((r, d), BF16),
            vec=((16, d), F32),
            pos=((self.places, self.group), jnp.int32),
            count=((self.group,), jnp.int32),
            **self.vectors(),
            wt=((3 * loc, d), BF16),
            w1=((d, hid), BF16),
            w2=((hid, d), BF16),
            wpb=((d, self.emb), BF16),
            cap=((self.own, self.emb), F32),
            wo=((m * loc, d), BF16),
            attn=((r, d), BF16),
            hat=((r, d), BF16),
            spread=((r, 1), F32),
            q=((r, loc), BF16),
            k=((r, loc), BF16),
            v=((r, loc), BF16),
            q0=((64 * self.group, 128), F32),
            q1=((64 * self.group, 128), F32),
            k0=((64 * self.group, 128), F32),
            k1=((64 * self.group, 128), F32),
            v0=((64 * self.group, 128), F32),
            v1=((64 * self.group, 128), F32),
            probs=((hg, r), F32),
            plow=((hg, r), BF16),
            cx=((m, 2, 3 * self.quarter, 128), BF16),
            mid=((r, d), F32),
            midq=((2, r // m, d), F32),
            part=((r, d), BF16),
            half=((r // 2, d), BF16),
            chip=((2, r // m, d), BF16),
            got=((2, r // m, d), BF16),
            blk=((r, d), BF16),
            xc=((n, d), BF16),
            plan=((n, 128), F32),
            text=((self.captions, self.emb), BF16),
            own=((self.own, self.emb), BF16),
            cg=((m, n, loc), BF16),
            midc=((n, d), F32),
            mlp=((b, d), BF16),
            pre=((n, hid), F32),
            act=((b, hid), BF16),
            part1=((n, d), BF16),
            sums=((4, n // 2, d), BF16),
            all1=((n, d), BF16),
            all2=((n, d), BF16),
            post=((b, d), BF16),
            unit=((n, self.emb), F32),
            stat=((n, 2), F32),
            low=((n, self.emb), BF16),
            lg=((b, self.captions), F32),
            dtext=((self.own, self.emb), F32),
            arow=((hg, d), BF16),
            brow=((hg, d), BF16),
            crow=((8, self.captions), F32),
            demb=((b, self.emb), BF16),
            dy=((b, d), BF16),
            dpre=((b, hid), BF16),
            dmid=((n, d), F32),
            dmidl=((b, d), BF16),
            dctx=((n, loc), BF16),
            capg=((self.own, self.emb), F32),
            small=((16, d), F32),
            ac=((b, d), BF16),
            qa=((b, loc), BF16),
            u=((m * 2 * hg, d), BF16),
            uq=((m * self.group, d), BF16),
            coef=((m * 2 * hg, 128), BF16),
            tot=((self.dps * 16, 128), BF16),
            sums_left=((16, 128), F32),
        )


def kernel(plan, *refs):
    names = [*plan.operands(), *plan.results(), *plan.scratch()]
    sems = refs[len(names)]
    used = iter(range(plan.semaphores()))

    places, free, ends = {}, [], []

    def sem():
        return sems.at[next(used)]

    def own():
        place = free.pop() if free else next(used)
        ref = sems.at[place]
        places[id(ref)] = (place, ref)
        return ref

    def done(copy):
        if copy.is_remote:
            copy.wait_send()
        else:
            copy.wait()
        free.append(places[id(copy.src_sem if copy.is_remote else copy.dst_sem)][0])

    def settle(count):
        for copy in ends[:count]:
            done(copy)
        del ends[:count]

    R = Named(zip(names, refs))
    rows, width, local, heads = plan.rows, plan.width, plan.local, plan.heads
    group, hg, dps, mps = plan.group, plan.hg, plan.dps, plan.mps
    dp, mp = lax.axis_index("dp"), lax.axis_index("mp")
    low_bit, high_bit = lax.rem(mp, 2), lax.div(mp, 2)
    near = mp + 1 - 2 * low_bit
    far = lax.rem(mp + 2, 4)
    put_sem = {n: own() for n in ("mlp", "act", "post", "demb", "dy", "dpre", "dmidl", "ac", "qa")}

    def dp_peer(i):
        return lax.rem(dp + dps + (i + 2) // 2 * (1 - 2 * (i % 2)), dps)

    def load(src, dst):
        copy = pltpu.make_async_copy(src, dst, own())
        copy.start()
        return copy

    def store(name, dst=None):
        ends.append(load(R[name], R[dst or name + "_out"]))

    def put(name, i, value):
        R[name][...] = value
        copy = pltpu.make_async_copy(
            R[name], R[name.removesuffix("l") + "_out"].at[rows_at(i, plan.block)], put_sem[name]
        )
        copy.start()
        if plan.blocks == 1:
            ends.append(copy)
        else:
            copy.wait()

    def send(src, dst, dp_to, mp_to, out, into):
        return pltpu.make_async_remote_copy(
            src_ref=src,
            dst_ref=dst,
            send_sem=out,
            recv_sem=into,
            device_id=(dp_to, mp_to),
            device_id_type=MESH,
        )

    class GatherDp:
        def __init__(self, buf, size, source=None):
            self.buf, self.size, self.source = buf, size, source
            self.out, self.into = own(), sem()

        def start(self):
            mine = self.buf.at[rows_at(dp, self.size)]
            source = mine if self.source is None else self.source

            def one(i):
                send(source, mine, dp_peer(i), mp, self.out, self.into).start()

            loop(dps - 1, one)
            rest = self.buf.at[pl.ds(0, (dps - 1) * self.size)]
            self.all = send(rest, rest, dp, near, self.out, self.into)
            ends.append(self.all)

        def wait(self):
            self.all.wait_recv()

    class GatherDpHalf:
        def __init__(self, buf, size, source):
            self.size, self.source = size, source
            self.out, self.into = own(), sem()
            half = buf.shape[1] // 2
            self.cols = pl.ds(pl.multiple_of(low_bit * half, 128), half)
            self.buf = buf.at[:, self.cols]
            self.near = send(self.buf, self.buf, dp, near, own(), sem())

        def start(self):
            source = self.source.at[:, self.cols]
            mine = self.buf.at[rows_at(dp, self.size)]
            self.own = load(source, mine)

            def one(i):
                send(source, mine, dp_peer(i), mp, self.out, self.into).start()

            loop(dps - 1, one)
            rest = self.buf.at[pl.ds(0, (dps - 1) * self.size)]
            self.all = send(rest, rest, dp, near, self.out, self.into)
            ends.append(self.all)

        def relay(self):
            done(self.own)
            self.all.wait_recv()
            self.near.start()
            ends.append(self.near)

        def wait(self):
            self.near.wait_recv()

    class GatherDpTwice:
        def __init__(self, buf, size, source):
            self.buf, self.size, self.source = buf, size, source
            self.out, self.into = own(), sem()
            self.beside = dp + 1 - 2 * lax.rem(dp, 2)
            self.arrive = [sem() for _ in range(dps // 2 - 1)]
            self.left = list(range(dps // 2 - 1))

        def at(self, i):
            return self.buf.at[rows_at(i, self.size)]

        def start(self):
            send(self.source, self.at(dp), self.beside, mp, self.out, self.into).start()
            for i, into in enumerate(self.arrive):
                send(self.source, self.at(dp), self.pair(i), mp, self.out, into).start()

        def pair(self, i):
            other, bit = lax.rem(dp, 2), 1
            while bit < dps // 2:
                other += 2 * bit * lax.rem(lax.div(dp, 2 * bit) + (i + 1) // bit, 2)
                bit *= 2
            return other

        def forward(self, part):
            count = len(self.arrive)
            for i in range(count * (part - 1) // 3, count * part // 3):
                block = self.at(self.pair(i))
                send(block, block, self.beside, mp, self.out, self.arrive[i]).wait_recv()
                send(block, block, self.beside, mp, self.out, self.into).start()

        def wait(self):
            half = self.buf.at[pl.ds(0, dps // 2 * self.size)]
            rest = self.buf.at[pl.ds(0, (dps - 1) * self.size)]
            send(half, half, self.beside, mp, self.out, self.into).wait_recv()
            ends.append(send(rest, rest, self.beside, mp, self.out, self.into))

    class GatherMp:
        def __init__(self, slot):
            self.slot = slot
            self.to_near = send(slot(mp), slot(mp), dp, near, own(), sem())
            self.to_far = send(slot(mp), slot(mp), dp, far, own(), sem())
            self.pass_on = send(slot(far), slot(far), dp, near, own(), sem())

        def start(self):
            self.to_far.start()
            self.to_near.start()
            ends.extend([self.to_near, self.to_far])

        def forward(self):
            self.to_far.wait_recv()
            self.pass_on.start()
            ends.append(self.pass_on)

        def wait(self):
            self.to_near.wait_recv()
            self.pass_on.wait_recv()

    class SumMp:
        def __init__(self, part, slots, got, total):
            self.part, self.slots, self.got, self.total = part, slots, got, total
            count = part.shape[0] // 2
            self.mine, other = rows_at(low_bit, count), rows_at(1 - low_bit, count)
            half = self.total.at[self.mine]
            self.first = send(part.at[other], slots.at[0], dp, near, own(), sem())
            self.second = send(slots.at[1], slots.at[got], dp, far, own(), sem())
            self.third = send(half, half, dp, near, own(), sem())

        def start(self):
            self.first.start()

        def middle(self):
            self.first.wait_recv()
            mine = self.part[self.mine, :].astype(F32)
            self.slots[1] = (mine + self.slots[0].astype(F32)).astype(BF16)
            self.second.start()

        def turn(self):
            self.second.wait_recv()
            done(self.second)
            total = self.slots[1].astype(F32) + self.slots[self.got].astype(F32)
            self.total[self.mine, :] = total.astype(BF16)
            self.third.start()
            ends.append(self.third)

        def wait(self):
            self.third.wait_recv()

    barrier = pltpu.get_barrier_semaphore()

    def greet(i):
        pl.semaphore_signal(
            barrier, inc=1, device_id=(lax.rem(dp + 1 + i, dps), mp), device_id_type=MESH
        )

    loop(dps - 1, greet)
    for i in range(1, mps):
        pl.semaphore_signal(
            barrier, inc=1, device_id=(dp, lax.rem(mp + i, mps)), device_id_type=MESH
        )
    vec = R.vec
    vectors = ("g1", "b1", "g2", "b2", "ob", "f2b", "pg", "pb", "f1b")
    got_first = [load(R[n + "_in"], R[n]) for n in ("x", "g1", "b1")]
    got_wo = load(R.wo_in, R.wo.at[rows_at(mp, local)])
    got_wt = load(R.wt_in, R.wt)
    got_small = [
        load(R[n + "_in"], R[n]) for n in (*vectors[2:], "qvb", "ls", "pos", "count", "cap")
    ]
    got_w1 = load(R.w1_in, R.w1)
    got_w2 = load(R.w2_in, R.w2)
    wp = R.mid.at[pl.ds(0, width), pl.ds(0, plan.emb)]
    got_wp = load(R.wp_in, wp)
    for name in ("small", "crow", "dtext", "q1"):
        R[name][...] = jnp.zeros_like(R[name])
    for name in ("v0", "v1"):
        R[name][rows : 64 * group, :] = jnp.zeros((64 * group - rows, 128), F32)

    def place(i):
        name = vectors[i]
        vec[i : i + 1, 0 : R[name].shape[0]] = R[name][...].astype(F32).reshape(1, -1)

    for got in got_first:
        done(got)
    place(0)
    place(1)

    def row(i, size=width):
        return vec[i : i + 1, 0:size]

    step = rows // 4

    def first_norm(i):
        at = rows_at(i, rows // 2)
        normed, hat, spread = norm_rows(R.x[at, :].astype(F32), row(G1), row(B1))
        R.spread[at, :] = spread
        R.attn[at, :] = normed.astype(BF16)
        R.hat[at, :] = hat.astype(BF16)

    loop(2, first_norm)
    for got in got_small:
        done(got)
    for i in range(2, len(vectors)):
        place(i)
    vec[QB : VB + 1, 0:local] = R.qvb[...].astype(F32)
    vec[SCALE : SCALE + 1, 0:1] = R.ls[...].reshape(1, 1)
    pl.semaphore_wait(barrier, dps - 1 + mps - 1)
    done(got_wo)
    gather_wo = GatherMp(lambda i: R.wo.at[rows_at(i, local)])
    gather_wo.start()
    done(got_wt)

    def project(i):
        at = rows_at(i, rows // 2)
        a = R.attn[at, :]
        for j, (name, shift) in enumerate((("q", QB), ("k", None), ("v", VB))):
            t = dot(a, R.wt[j * local : (j + 1) * local, :], 1, 1)
            if shift is not None:
                t = t + row(shift, local)
            t = t.astype(BF16)
            R[name][at, :] = t
            t = t.astype(F32)
            R[name + "0"][at, :] = t[:, 0:128]
            R[name + "1"][at, 0 : local - 128] = t[:, 128:local]

    loop(2, project)

    lane_head = iota((hg, local), 1) // HEAD_DIM
    own_head = lane_head == iota((hg, local), 0) // group

    def spread_heads(t):
        wide = jnp.concatenate([t.astype(F32)] * heads, 0)
        return jnp.where(own_head, wide, 0.0).astype(BF16)

    def join_heads(t):
        t = jnp.where(own_head, t, 0.0)
        total = t[0:group]
        for h in range(1, heads):
            total = total + t[h * group : (h + 1) * group]
        return total

    same = lax.rem(iota((hg, rows), 0), group) == lax.rem(iota((hg, rows), 1), group)
    qx = spread_heads(R.q[0:group, :])
    scores = jnp.where(same, dot(qx, R.k[...], 1, 1) * 0.125, LOW)
    weights = jnp.exp(scores - jnp.max(scores, -1, keepdims=True))
    probs = weights * (1.0 / jnp.sum(weights, -1, keepdims=True))
    R.probs[...] = probs
    R.plow[...] = probs.astype(BF16)
    mine = rows_at(dp, group)
    ctx = join_heads(dot(R.plow[...], R.v[...])).astype(BF16)
    cg = R.cg.at[mp]
    cg[mine, :] = ctx
    gather_ctx = GatherDp(cg, group)
    gather_ctx.start()
    gather_xc = GatherDpHalf(R.xc, group, R.x.at[pl.ds(0, group)])
    gather_xc.start()
    head_of = iota((128, 256), 1) // HEAD_DIM
    seen = iota((128, 128), 0) // 64 == iota((128, 128), 1) // 64
    seen &= lax.rem(iota((128, 128), 1), 64) < plan.seq

    def pair(t):
        both = [pl.ds(2 * t + j, 64, stride=group) for j in range(2)]

        def taken(name):
            parts = [R[name + i] for i in "01"]
            return jnp.concatenate(
                [jnp.concatenate([ref[at, :] for at in both], 0) for ref in parts], 1
            )

        qb = (taken("q") * 0.125).astype(BF16)
        kb, vb = taken("k"), taken("v")
        of_head = [head_of == h for h in range(heads)]
        k_wide = jnp.concatenate([jnp.where(m, kb, 0.0) for m in of_head], 0).astype(BF16)
        v_wide = jnp.concatenate([jnp.where(m, vb, 0.0) for m in of_head], 0).astype(BF16)
        scores = dot(qb, k_wide, 1, 1)
        scale = jnp.zeros((128, 256), F32)
        parts = []
        for h in range(heads):
            s = jnp.where(seen, scores[:, h * 128 : (h + 1) * 128], LOW)
            e = jnp.exp(s - jnp.max(s, -1, keepdims=True))
            scale = jnp.where(of_head[h], 1.0 / jnp.sum(e, -1, keepdims=True), scale)
            parts.append(e.astype(BF16))
        total = dot(jnp.concatenate(parts, 1), v_wide) * scale
        for j, at in enumerate(both):
            R.q0[at, :] = total[j * 64 : j * 64 + 64, 0:128]
            R.q1[at, :] = total[j * 64 : j * 64 + 64, 128:256]

    def attend(t):
        pair(2 * t)
        pair(2 * t + 1)

    first_part = 3 * group // 16
    loop(first_part, attend)
    table = [R.pos[...].astype(F32), R.count[...].astype(F32).reshape(1, group)]
    table = jnp.concatenate(table, 0)
    table = jnp.pad(table, ((0, 128 - table.shape[0]), (0, 128 - group)))
    R.plan[rows_at(dp, group), :] = table.T[0:group]
    gather_plan = GatherDp(R.plan, group)
    gather_plan.start()
    cap = R.cap[...]
    cap_factor = lax.rsqrt(jnp.sum(cap * cap, -1, keepdims=True) + 1e-06)
    R.own[...] = (cap * cap_factor).astype(BF16)
    gather_text = GatherDpHalf(R.text, plan.own, R.own)
    gather_text.start()
    gather_ctx.wait()
    gather_cg = GatherMp(lambda i: R.cg.at[i])
    gather_cg.start()
    loop(group // 4 - first_part, lambda t: attend(t + first_part))
    quarter = plan.quarter
    for i in range(2):
        both = [slice((i + 2 * n) * quarter, (i + 2 * n + 1) * quarter) for n in range(2)]
        for n, at in enumerate(both):
            R.cx[mp, i, n * quarter : (n + 1) * quarter, :] = R.q0[at, :].astype(BF16)
        last = jnp.concatenate([R.q1[at, 0:64] for at in both], 1)
        R.cx[mp, i, 2 * quarter : 3 * quarter, :] = last.astype(BF16)
    gather_sets = [GatherMp(lambda m, i=i: R.cx.at[m, i]) for i in range(2)]
    gather_uk = GatherMp(lambda i: R.u.at[rows_at(i, hg)])
    gather_pc = GatherMp(lambda i: R.coef.at[rows_at(mps + i, hg)])
    gather_xc.relay()
    R.brow[...] = dot(R.plow[...], R.attn[...]).astype(BF16)
    uk = dot(qx, R.wt[local : 2 * local, :])
    R.u[rows_at(mp, hg), :] = uk.astype(BF16)
    fold = jnp.where(
        iota((rows, 128), 0) // group == iota((rows, 128), 1), 1.0, 0.0
    ).astype(BF16)
    late = rows_at(mps + mp, hg)
    R.coef[late, :] = dot(R.plow[...], fold).astype(BF16)
    gather_wo.forward()
    gather_cg.forward()
    for g in (gather_sets[0], gather_uk, gather_pc):
        g.start()
    gather_wo.wait()
    done(got_w1)
    done(got_w2)
    gather_xc.wait()
    gather_cg.wait()

    def class_forward(i):
        at = rows_at(i, plan.block)
        total = R.xc[at, :].astype(F32) + row(OUTB)
        joined = jnp.concatenate([R.cg[m, at, :].astype(F32) for m in range(mps)], 1)
        total += dot(joined.astype(BF16), R.wo[...])
        R.midc[at, :] = total
        mlp = norm_rows(total, row(G2), row(B2))[0].astype(BF16)
        put("mlp", i, mlp)
        pre = dot(mlp, R.w1[...]) + row(FC1B, plan.hidden)
        R.pre[at, :] = pre
        act = (pre * jax.nn.sigmoid(1.702 * pre)).astype(BF16)
        put("act", i, act)
        R.part1[at, :] = dot(act, R.w2[...]).astype(BF16)

    loop(plan.blocks, class_forward)
    sum1 = SumMp(R.part1, R.sums, 2, R.all1)
    sum1.start()

    size = plan.quarter

    def joined_context(index, i):
        side, joined = lax.div(index, 2), []
        for m in range(mps):
            tail = R.cx[m, i, 2 * size : 3 * size, :].astype(F32)
            tail = jnp.where(side == 0, tail[:, 0:64], tail[:, 64:128])
            joined += [R.cx[m, i, rows_at(side, size), :].astype(F32), tail]
        return jnp.concatenate(joined, 1).astype(BF16)

    def bulk(i):
        at = [rows_at(index, size) for index in (others[i], owned[i])]
        total = jnp.concatenate([R.x[a, :].astype(F32) for a in at], 0) + row(OUTB)
        joined = [joined_context(index, i) for index in (others[i], owned[i])]
        total += dot(jnp.concatenate(joined, 0), R.wo[...])
        R.midq[i] = total[size : 2 * size]
        mlp = norm_rows(total, row(G2), row(B2))[0].astype(BF16)
        pre = dot(mlp, R.w1[...]) + row(FC1B, plan.hidden)
        act = (pre * jax.nn.sigmoid(1.702 * pre)).astype(BF16)
        part = dot(act, R.w2[...]).astype(BF16)
        R.part[at[0], :] = part[0:size]
        R.part[at[1], :] = part[size : 2 * size]

    others = [2 * (1 - low_bit) + i for i in range(2)]
    owned = [2 * low_bit + i for i in range(2)]
    def cut_rows(*counts):
        starts = [sum(counts[:n]) for n in range(len(counts))]
        return [pl.ds(a, c) for a, c in zip(starts, counts)]

    pieces = [cut_rows(96, size - 96), cut_rows(64, 96, size - 160)]

    def near_move(i):
        rows_other = R.part.at[rows_at(others[i], size)]
        return send(rows_other, R.half.at[pl.ds(i * size, size)], dp, near, own(), sem())

    def far_move(i, p):
        return send(R.chip.at[i, p], R.got.at[i, p], dp, far, own(), sem())

    to_near = [near_move(i) for i in range(2)]
    to_far = [[far_move(i, p) for p in pieces[i]] for i in range(2)]

    def chip_sum(i):
        to_near[i].wait_recv()
        mine = R.part[rows_at(owned[i], size), :].astype(F32)
        R.chip[i] = (mine + R.half[i * size : (i + 1) * size, :].astype(F32)).astype(BF16)

    def block_rows(index, p):
        return pl.ds(pl.multiple_of(index * size + p.start, 16), p.size)

    def near_block(i, p):
        at = R.blk.at[block_rows(owned[i], p)]
        return send(at, at, dp, near, own(), sem())

    blk_near = [[near_block(i, p) for p in pieces[i]] for i in range(2)]

    def store_rows(index, p):
        at = block_rows(index, p)
        ends.append(load(R.blk.at[at], R.block_out.at[at]))

    def finish(i):
        for n, p in enumerate(pieces[i]):
            to_far[i][n].wait_recv()
            total = R.chip[i, p, :].astype(F32) + R.got[i, p, :].astype(F32)
            total += R.midq[i, p, :] + row(FC2B)
            R.blk[block_rows(owned[i], p), :] = total.astype(BF16)
            blk_near[i][n].start()
            store_rows(owned[i], p)

    def class_queries(i):
        normed = norm_rows(R.xc[rows_at(i, plan.block), :].astype(F32), row(G1), row(B1))[0]
        normed = normed.astype(BF16)
        put("ac", i, normed)
        queries = dot(normed, R.wt[0:local, :], 1, 1) + row(QB, local)
        put("qa", i, queries.astype(BF16))

    loop(plan.blocks, class_queries)
    sum1.middle()
    done(got_wp)
    R.wpb[...] = wp[...].astype(BF16)
    gather_sets[0].forward()
    gather_text.relay()
    gather_sets[0].wait()
    started = len(ends)
    gather_sets[1].start()
    gather_b = GatherDp(R.b_out, hg, R.brow)
    gather_b.start()
    ends.append(load(R.brow, R.b_out.at[rows_at(dp, hg)]))
    bulk(0)
    sum1.turn()
    to_near[0].start()
    gather_plan.wait()
    gather_text.wait()
    sum1.wait()
    settle(started)

    done(sum1.first)
    scale = jnp.exp(row(SCALE, 1))
    crow = R.crow
    crow[0:1, :] = jnp.full((1, plan.captions), LOW, F32)

    def class_out(at):
        return R.midc[at, :] + R.all1[at, :].astype(F32) + row(FC2B)

    def logits_at(at):
        if plan.blocks == 1:
            return R.lg[...]
        return scale * dot(R.low[at, :], R.text[...], 1, 1)

    def head(i):
        at = rows_at(i, plan.block)
        post = norm_rows(class_out(at), row(PG), row(PB))[0]
        put("post", i, post.astype(BF16))
        emb = dot(post.astype(BF16), R.wpb[...])
        factor = lax.rsqrt(jnp.sum(emb * emb, -1, keepdims=True) + 1e-06)
        R.stat[at, 0:1] = factor
        unit = emb * factor
        R.unit[at, :] = unit
        image_low = unit.astype(BF16)
        R.low[at, :] = image_low
        logits = scale * dot(image_low, R.text[...], 1, 1)
        R.lg[...] = logits
        crow[0:1, :] = jnp.maximum(crow[0:1, :], jnp.max(logits, 0, keepdims=True))

    loop(plan.blocks, head)
    chip_sum(0)
    to_far[0][0].start()

    def matches(at):
        ids = iota((plan.block, plan.captions), 1).astype(F32)
        found = R.plan[at, 0:1] == ids
        for place in range(1, plan.places):
            found |= R.plan[at, place : place + 1] == ids
        return jnp.where(found, 1.0, 0.0)

    def put_small(i, value):
        R.small[i : i + 1, 0 : value.shape[1]] += value

    half_i, half_c = 0.5 / plan.images, 0.5 / plan.captions

    def stats(i):
        at = rows_at(i, plan.block)
        logits = logits_at(at)
        matched = matches(at) * logits
        crow[1:2, :] += jnp.sum(jnp.exp(logits - crow[0:1, :]), 0, keepdims=True)
        crow[2:3, :] += jnp.sum(matched, 0, keepdims=True)
        top = jnp.max(logits, 1, keepdims=True)
        lse = top + jnp.log(jnp.sum(jnp.exp(logits - top), 1, keepdims=True))
        R.stat[at, 1:2] = lse
        counts = R.plan[at, plan.places : plan.places + 1]
        terms = lse - jnp.sum(matched, 1, keepdims=True) / counts
        put_small(LOSS, half_i * jnp.sum(terms, 0, keepdims=True))

    loop(plan.blocks, stats)
    crow[3:4, :] = crow[0:1, :] + jnp.log(crow[1:2, :])
    put_small(LOSS, half_c * jnp.sum(crow[3:4, :] - crow[2:3, :], 1, keepdims=True))

    shape = (plan.captions, plan.own)
    own_captions = iota(shape, 0) == iota(shape, 1) + dp * plan.own
    own_captions = jnp.where(own_captions, 1.0, 0.0).astype(BF16)

    def head_back(i):
        at = rows_at(i, plan.block)
        logits = logits_at(at)
        match = matches(at)
        counts = R.plan[at, plan.places : plan.places + 1]
        dlog = half_i * (jnp.exp(logits - R.stat[at, 1:2]) - match / counts)
        dlog += half_c * (jnp.exp(logits - crow[3:4, :]) - match)
        dlow = dlog.astype(BF16)
        both = jnp.sum(dlow.astype(F32) * logits, 1, keepdims=True)
        R.small[LOSS : LOSS + 1, 128:129] += jnp.sum(both, 0, keepdims=True)
        dimage = scale * dot(dlow, R.text[...])
        own = dot(dlow, own_captions).astype(BF16)
        R.dtext[...] += dot(own, R.low[at, :], 0, 0)
        unit = R.unit[at, :]
        demb = R.stat[at, 0:1] * (dimage - unit * jnp.sum(unit * dimage, -1, keepdims=True))
        put("demb", i, demb.astype(BF16))
        dpost = dot(demb.astype(BF16), R.wpb[...], 1, 1)
        _, hat, spread = norm_rows(class_out(at), row(PG), row(PB))
        dcls = norm_back(dpost, row(PG), hat, spread)
        put_small(DPG, jnp.sum(dpost * hat, 0, keepdims=True))
        put_small(DPB, jnp.sum(dpost, 0, keepdims=True))
        put_small(DFC2B, jnp.sum(dcls, 0, keepdims=True))
        R.dmid[at, :] = dcls
        dy = dcls.astype(BF16)
        put("dy", i, dy)
        pre = R.pre[at, :]
        sigma = jax.nn.sigmoid(1.702 * pre)
        slope = sigma + 1.702 * pre * sigma * (1.0 - sigma)
        dpre = (dot(dy, R.w2[...], 1, 1) * slope).astype(BF16)
        put("dpre", i, dpre)
        put_small(DFC1B, jnp.sum(dpre.astype(F32), 0, keepdims=True))
        R.part1[at, :] = dot(dpre, R.w1[...], 1, 1).astype(BF16)

    loop(plan.blocks, head_back)
    sum2 = SumMp(R.part1, R.sums, 3, R.all2)
    sum2.start()
    gather_sets[1].forward()
    ends.append(sum2.first)
    dtext = scale * R.dtext[...]
    text_unit = cap * cap_factor
    R.capg[...] = cap_factor * (
        dtext - text_unit * jnp.sum(text_unit * dtext, -1, keepdims=True)
    )
    store("capg", "cap_out")

    sum2.middle()
    gather_uk.forward()
    gather_pc.forward()
    gather_sets[1].wait()
    bulk(1)
    to_far[0][1].start()
    sum2.turn()
    to_near[1].start()
    sum2.wait()

    def class_back(i):
        at = rows_at(i, plan.block)
        dmlp = R.all2[at, :].astype(F32)
        _, hat, spread = norm_rows(R.midc[at, :], row(G2), row(B2))
        dmid = R.dmid[at, :] + norm_back(dmlp, row(G2), hat, spread)
        put_small(DG2, jnp.sum(dmlp * hat, 0, keepdims=True))
        put_small(DB2, jnp.sum(dmlp, 0, keepdims=True))
        put_small(DOUTB, jnp.sum(dmid, 0, keepdims=True))
        R.dmid[at, :] = dmid
        dlow = dmid.astype(BF16)
        put("dmidl", i, dlow)
        R.dctx[at, :] = dot(dlow, R.wo[rows_at(mp, local), :], 1, 1).astype(BF16)

    loop(plan.blocks, class_back)
    store("dctx")

    dx = spread_heads(R.dctx[mine, :])
    probs = R.probs[...]
    dprobs = dot(dx, R.v[...], 1, 1)
    dscores = probs * (dprobs - jnp.sum(probs * dprobs, -1, keepdims=True))
    dscores = (dscores * 0.125).astype(BF16)
    R.arow[...] = dot(dscores, R.attn[...]).astype(BF16)
    gather_a = GatherDpTwice(R.a_out, hg, R.arow)
    gather_a.start()
    ends.append(load(R.arow, R.a_out.at[rows_at(dp, hg)]))
    dq = join_heads(dot(dscores, R.k[...])).astype(BF16)
    R.u[late, :] = dot(dx, R.wt[2 * local : 3 * local, :]).astype(BF16)
    gather_uv = GatherMp(lambda i: R.u.at[rows_at(mps + i, hg)])
    gather_uv.start()
    R.coef[rows_at(mp, hg), :] = dot(dscores, fold).astype(BF16)
    R.uq[rows_at(mp, group), :] = dot(dq, R.wt[0:local, :]).astype(BF16)
    gather_dc = GatherMp(lambda i: R.coef.at[rows_at(i, hg)])
    gather_uq = GatherMp(lambda i: R.uq.at[rows_at(i, group)])
    gather_dc.start()
    gather_uq.start()
    put_small(DQB, jnp.sum(dq.astype(F32), 0, keepdims=True))
    prob_sum = jnp.sum(R.plow[...].astype(F32), -1, keepdims=True)
    put_small(DVB, jnp.sum(dx.astype(F32) * prob_sum, 0, keepdims=True))
    gather_pc.wait()
    shape = (mps * hg, rows)
    fits = lax.rem(iota(shape, 0), group) == lax.rem(iota(shape, 1), group)

    def by_rows(first):
        coef = R.coef[first : first + mps * hg, :]
        wide = jnp.where(fits, dot(coef, fold, 1, 1), 0.0).astype(BF16)
        return dot(wide, R.hat[...])

    by_probs = by_rows(mps * hg)
    chip_sum(1)
    for move in to_far[1]:
        move.start()
    gather_uv.forward()
    gather_dc.forward()
    gather_uq.forward()
    for g in (gather_uk, gather_uv, gather_dc, gather_uq):
        g.wait()
    gather_a.forward(1)

    query = R.uq[0:group, :].astype(F32)
    for m in range(1, mps):
        query += R.uq[m * group : (m + 1) * group, :].astype(F32)
    factors = R.u[...].astype(F32)
    weight = jnp.sum(R.coef[...].astype(F32), -1, keepdims=True)
    summed = jnp.concatenate([by_rows(0), by_probs], 0)
    scaled = jnp.sum(factors * summed, 0, keepdims=True)
    scaled += jnp.sum(query * R.hat[0:group, :].astype(F32), 0, keepdims=True)
    shift = jnp.sum(factors * weight, 0, keepdims=True) + jnp.sum(query, 0, keepdims=True)
    put_small(DG1, scaled)
    put_small(DB1, shift)
    spans = []
    for i, count in ((DG1, width), (DB1, width), (DQB, local), (DVB, local)):
        spans += [(i, c, min(128, count - c)) for c in range(0, count, 128)]
    tile = []
    for i, c, size_c in spans:
        piece = R.small[i : i + 1, c : c + size_c]
        tile.append(jnp.pad(piece, ((0, 0), (0, 128 - size_c))))
    R.tot[rows_at(dp, 16), :] = jnp.concatenate(tile, 0).astype(BF16)
    gather_tot = GatherDp(R.tot, 16)
    gather_tot.start()

    def spread_coef(i):
        at = rows_at(i, 2 * size)
        pick = jnp.where(
            iota((2 * size, 128), 0) // group + i * (2 * size // group)
            == iota((2 * size, 128), 1),
            1.0,
            0.0,
        ).astype(BF16)
        wide = dot(pick, R.coef[...], 1, 1)
        shape = wide.shape
        fits = lax.rem(iota(shape, 0), group) == lax.rem(iota(shape, 1), group)
        R.mid[at, :] = dot(jnp.where(fits, wide, 0.0).astype(BF16), R.u[...])

    gather_a.forward(2)
    loop(2, spread_coef)
    R.mid[0:group, :] += query
    gather_a.forward(3)
    def first_back(i):
        at = rows_at(i, step)
        hat = R.hat[at, :].astype(F32)
        R.attn[at, :] = norm_back(R.mid[at, :], row(G1), hat, R.spread[at, :]).astype(BF16)

    for i in range(mps):
        loop(size // step, lambda t, i=i: first_back(t + i * (size // step)))
        at = pl.ds(i * size, size)
        if i == 0:
            top = R.attn[0:group, :].astype(F32) + R.dmid[mine, :]
            R.attn[0:group, :] = top.astype(BF16)
        ends.append(load(R.attn.at[at], R.images_out.at[at]))

    finish(0)
    finish(1)
    gather_tot.wait()

    R.sums_left[...] = jnp.zeros((16, 128), F32)

    def add_up(i):
        R.sums_left[...] += R.tot[rows_at(i, 16), :].astype(F32)

    loop(dps, add_up)
    for n, (i, c, size_c) in enumerate(spans):
        R.small[i : i + 1, c : c + size_c] = R.sums_left[n : n + 1, 0:size_c]
    store("small")
    ends.append(load(cg, R.ctx_out))
    gather_b.wait()
    for i in range(2):
        for n, p in enumerate(pieces[i]):
            blk_near[i][n].wait_recv()
            store_rows(others[i], p)
    gather_a.wait()
    ends.extend([*to_near, *to_far[0], *to_far[1], *blk_near[0], *blk_near[1]])
    settle(len(ends))


def run_kernel(plan, *operands):
    anywhere = pl.BlockSpec(memory_space=pl.ANY)
    return pl.pallas_call(
        functools.partial(kernel, plan),
        out_shape=[jax.ShapeDtypeStruct(s, t) for s, t in plan.results().values()],
        in_specs=[anywhere] * len(plan.operands()),
        out_specs=[anywhere] * len(plan.results()),
        scratch_shapes=[pltpu.VMEM(s, t) for s, t in plan.scratch().values()]
        + [pltpu.SemaphoreType.DMA((plan.semaphores(),))],
        compiler_params=pltpu.CompilerParams(
            collective_id=0, has_side_effects=True, vmem_limit_bytes=62 << 20
        ),
    )(*operands)


def final_operands(plan):
    names = ("images", "block", "cap", "small", "post", "demb", "act", "dy", "mlp", "dpre")
    names += ("ctx", "dmid", "a", "b", "dctx", "ac", "qa")
    return {n: plan.results()[n + "_out"] for n in names}


def final_results(plan):
    d, loc, hid = plan.width, plan.local, plan.hidden
    return dict(
        loss=((1,), F32),
        block=((plan.rows, d), BF16),
        images=((plan.rows, d), F32),
        g1=((d,), F32),
        b1=((d,), F32),
        wt=((3 * loc, d), F32),
        qvb=((2, loc), F32),
        wo=((loc, d), F32),
        ob=((d,), F32),
        g2=((d,), F32),
        b2=((d,), F32),
        w1=((d, hid), F32),
        f1b=((hid,), F32),
        w2=((hid, d), F32),
        f2b=((d,), F32),
        pg=((d,), F32),
        pb=((d,), F32),
        wp=((d, plan.emb), F32),
        cap=((plan.own, plan.emb), F32),
        ls=((1,), F32),
    )


STRAIGHT = ("block", "cap")


def final_kernel(plan, *refs):
    taken, given = final_operands(plan), final_results(plan)
    given_scratch = [n for n in given if n not in STRAIGHT]
    sems = refs[-1]
    I = Named(zip((*taken, "wt"), refs))
    refs = refs[len(taken) + 1 :]
    O = Named(zip(given, refs))
    rest = refs[len(given) :]
    L = Named(zip((*taken, "wk", "dq"), rest))
    S = Named(zip(given_scratch, rest[len(taken) + 2 :]))
    used, ends, free = iter(range(40)), [], []

    def copy(src, dst):
        place = free.pop() if free else next(used)
        move = pltpu.make_async_copy(src, dst, sems.at[place])
        move.start()

        def wait():
            move.wait()
            free.append(place)

        return wait

    late = ("images", "block", "cap", "small")
    order = ("act", "dy", "mlp", "dpre", *(n for n in taken if n not in late), *late)
    local = plan.local
    loads = {n: copy(I[n], L[n]) for n in dict.fromkeys(order)}
    loads["wk"] = copy(I.wt.at[pl.ds(local, local)], L.wk)

    def product(name, left, right, at=0, fix=None):
        for n in (left, right):
            if n in loads:
                loads.pop(n)()
        size = L[left].shape[1]
        step = 128 if size % 128 == 0 else size
        for c in range(0, size, step):
            a, b = L[left][:, c : c + step], L[right][...]
            rows = pl.ds(at + c, step)
            S[name][rows, :] = dot(fix(a) if fix else a, b, 0, 0)
            ends.append(copy(S[name].at[rows], O[name].at[rows]))

    group, heads = plan.group, plan.heads

    def spread_heads(t):
        pieces = []
        lane = iota((group, local), 1) // HEAD_DIM
        t = t.astype(F32)
        for i in range(plan.dps):
            for h in range(heads):
                pieces.append(jnp.where(lane == h, t[i * group : (i + 1) * group], 0.0))
        return jnp.concatenate(pieces, 0).astype(BF16)

    product("w2", "act", "dy")
    product("w1", "mlp", "dpre")
    product("wp", "post", "demb")
    loads.pop("images")()
    for i in range(plan.mps):
        rows = pl.ds(i * plan.quarter, plan.quarter)
        S.images[rows, :] = L.images[rows, :].astype(F32)
        ends.append(copy(S.images.at[rows], O.images.at[rows]))
    product("wo", "ctx", "dmid")
    product("wt", "dctx", "b", 2 * local, spread_heads)
    product("wt", "qa", "a", local, spread_heads)
    loads.pop("block")()
    ends.append(copy(L.block, O.block))
    loads.pop("wk")()
    wide = dot(L.a[...], L.wk[...], 1, 1)
    lane = iota((group, local), 1) // HEAD_DIM
    for i in range(plan.dps):
        total = jnp.zeros((group, local), F32)
        for h in range(heads):
            first = (i * heads + h) * group
            total += jnp.where(lane == h, wide[first : first + group], 0.0)
        L.dq[i * group : (i + 1) * group, :] = total.astype(BF16)
    product("wt", "dq", "ac")
    loads.pop("cap")()
    ends.append(copy(L.cap, O.cap))
    loads.pop("small")()
    small = L.small
    S.loss[...] = small[LOSS, 0:1]
    S.ls[...] = small[LOSS, 128:129]
    S.qvb[...] = small[DQB : DVB + 1, 0:local]
    vectors = dict(g1=DG1, b1=DB1, ob=DOUTB, g2=DG2, b2=DB2, f1b=DFC1B, f2b=DFC2B, pg=DPG, pb=DPB)
    for n, i in vectors.items():
        S[n][...] = small[i, 0 : S[n].shape[0]]
    for n in ("loss", "ls", "qvb", *vectors):
        ends.append(copy(S[n], O[n]))
    for end in ends:
        end()


def run_final(plan, got, wt):
    taken, given = final_operands(plan), final_results(plan)
    anywhere = pl.BlockSpec(memory_space=pl.ANY)
    scratch = [*taken.values(), ((plan.local, plan.width), BF16), ((plan.images, plan.local), BF16)]
    scratch += [st for n, st in given.items() if n not in STRAIGHT]
    out = pl.pallas_call(
        functools.partial(final_kernel, plan),
        out_shape=[jax.ShapeDtypeStruct(s, t) for s, t in given.values()],
        in_specs=[anywhere] * (len(taken) + 1),
        out_specs=[anywhere] * len(given),
        scratch_shapes=[pltpu.VMEM(s, t) for s, t in scratch]
        + [pltpu.SemaphoreType.DMA((40,))],
        compiler_params=pltpu.CompilerParams(vmem_limit_bytes=60 << 20),
    )(*(got[n + "_out"] for n in taken), wt)
    return dict(zip(given, out))


def body(
    images,
    ln1_gain,
    ln1_bias,
    w_qkv,
    qv_bias,
    w_out,
    out_bias,
    ln2_gain,
    ln2_bias,
    w_fc1,
    fc1_bias,
    w_fc2,
    fc2_bias,
    post_gain,
    post_bias,
    w_proj,
    captions,
    logit_scale,
    caption_counts,
    positives,
):
    sizes = (lax.axis_size("dp"), lax.axis_size("mp"))
    plan = Plan(sizes, images, w_qkv, w_fc1, w_proj, captions, positives)

    x = jnp.transpose(images, (1, 0, 2)).reshape(plan.rows, plan.width)
    wt = jnp.transpose(w_qkv, (1, 2, 0)).reshape(3 * plan.local, plan.width)

    got = run_kernel(
        plan,
        *(x, wt, w_out, w_fc1, w_fc2, w_proj, captions),
        jnp.transpose(positives),
        caption_counts,
        *(ln1_gain, ln1_bias, ln2_gain, ln2_bias, out_bias, fc2_bias),
        *(post_gain, post_bias, fc1_bias, qv_bias, logit_scale),
    )
    out = run_final(plan, dict(zip(plan.results(), got)), wt)

    def as_images(t):
        return jnp.transpose(t.reshape(plan.seq, plan.group, plan.width), (1, 0, 2))

    out["block"], out["images"] = as_images(out["block"]), as_images(out["images"])
    out["wt"] = jnp.transpose(out["wt"].reshape(3, plan.local, plan.width), (2, 0, 1))
    return tuple(out.values())


def solution(mesh):
    full, per_dp = P(), P("dp")
    return jax.shard_map(
        body,
        mesh=mesh,
        in_specs=(
            P("dp", None, None),
            full,
            full,
            P(None, None, "mp"),
            P(None, "mp"),
            P("mp", None),
            full,
            full,
            full,
            P(None, "mp"),
            P("mp"),
            P("mp", None),
            full,
            full,
            full,
            full,
            P("dp", None),
            full,
            per_dp,
            P("dp", None),
        ),
        out_specs=(
            full,
            P("dp", None, None),
            P("dp", None, None),
            full,
            full,
            P(None, None, "mp"),
            P(None, "mp"),
            P("mp", None),
            full,
            full,
            full,
            P(None, "mp"),
            P("mp"),
            P("mp", None),
            full,
            full,
            full,
            full,
            P("dp", None),
            full,
        ),
        check_vma=False,
    )
```
